512 devices in a mesh: seq: 32 (over z, core), table: 16 (over x, y).
Axes of the slice: x: 4, y: 4, z: 16, core: 2. Of those that a mesh axis runs over, the one named last changes fastest.
Arguments:
- columns: bfloat16 [16, 8192, 512], P(None, 'seq', 'table'), may hold values from -6 to 6
- gaps: float32 [16, 8192], P('table', 'seq'), may hold values from 0.2 to 9830.4
- norm_in: float32 [512], replicated, may hold values from 0.1 to 1.9
- w_gate: bfloat16 [512, 1024], replicated, may hold values from -0.25 to 0.25
- w_xbc: bfloat16 [512, 1280], replicated, may hold values from -0.25 to 0.25
- w_step: bfloat16 [512, 16], replicated, may hold values from -0.25 to 0.25
- step_bias: float32 [16], replicated, may hold values from -1 to 1
- conv_weight: float32 [4, 1280], replicated, may hold values from -1 to 1
- conv_bias: float32 [1280], replicated, may hold values from -1.5 to 1.5
- rates: float32 [16], replicated, may hold values from 6.1035156e-06 to 0.04
- norm_out: float32 [1024], replicated, may hold values from 0.1 to 1.9
- w_out: bfloat16 [1024, 512], replicated, may hold values from -0.1875 to 0.1875
Outputs:
- mixed: bfloat16 [16, 8192, 512], P('table', 'seq')
The draws below stay inside these ranges and needn't reach their ends.
All inputs are finite; a program needn't handle non-finite values.
Results may differ from the reference program's by a relative error of at most 0.02.
Values may be sent and summed in bfloat16 or wider, within the bound.
No kernel may reach another device: no remote copies, remote signals or barrier semaphores. Data moves between devices by JAX's collectives and lax.ppermute only.
A program may use at most 64 MiB of HBM per device.

```python
import math
import jax
import jax.numpy as jnp
from jax import lax

D = 512
HEADS = 16
HEAD_DIM = 64
STATE = 128
BLOCK = 256
CONV = 4
INNER = 1024
SEQ_DEV = 256
HISTS = 16
LEN = 8192


def draw_gaps(key, part):
    first = jax.random.fold_in(key, 11)
    second = jax.random.fold_in(key, 12)
    third = jax.random.fold_in(key, 13)
    span = SEQ_DEV // 2
    count = LEN // span
    levels = jnp.exp(jax.random.uniform(first, (HISTS, count), jnp.float32, math.log(0.4), math.log(3.2)))
    jitter = jnp.exp(jax.random.uniform(second, (HISTS, LEN), jnp.float32, math.log(0.5), math.log(2.0)))
    spread = jnp.repeat(levels, span, axis=1) * jitter
    places = jax.random.randint(third, (HISTS, 3, 1), 0, LEN)
    marks = jnp.any(places == jnp.arange(LEN)[None, None, :], axis=1)
    return jnp.where(marks, 1.2 * LEN, spread).astype(jnp.float32)


def draw_rates(key, part):
    first = jax.random.fold_in(key, 21)
    second = jax.random.fold_in(key, 22)
    third = jax.random.fold_in(key, 23)
    order = jax.random.permutation(first, HEADS)
    edge = math.log(2.0 / LEN)
    top = math.log(0.039)
    half = HEADS // 2
    quick_heads = order < half
    place = (order.astype(jnp.float32) + jax.random.uniform(second, (HEADS,), jnp.float32, 0.0, 1.0)) / half
    quick = jnp.exp(edge + jnp.minimum(place, 1.0) * (top - edge))
    slow = jnp.exp(jax.random.uniform(third, (HEADS,), jnp.float32, math.log(0.06 / LEN), edge))
    return jnp.where(quick_heads, quick, slow).astype(jnp.float32)


def draw_conv_weight(key, part):
    raw = jax.random.normal(jax.random.fold_in(key, 31), (CONV, INNER + 2 * STATE), jnp.float32)
    length = jnp.sqrt(jnp.sum(raw * raw, axis=0, keepdims=True))
    return (raw / jnp.maximum(length, 0.5)).astype(jnp.float32)


def draw_conv_bias(key, part):
    width = INNER + 2 * STATE
    centred = jax.random.uniform(jax.random.fold_in(key, 41), (width,), jnp.float32, -0.15, 0.15) - 0.55
    spread = jax.random.uniform(jax.random.fold_in(key, 42), (width,), jnp.float32, -1.5, 1.5)
    channel = jnp.arange(width)
    return jnp.where(channel < INNER + STATE, centred, spread).astype(jnp.float32)


def shard_levels(own_key, extent, shards, least, high):
    factor_of = 1.0
    for position, parts in shards:
        steps = jax.random.uniform(jax.random.fold_in(jax.random.fold_in(own_key, 6), position), (parts,), jnp.float32, least / len(shards), high / len(shards))
        factor_of = factor_of * jnp.repeat(jnp.exp(steps), extent[position] // parts).reshape((-1,) + (1,) * (len(extent) - 1 - position))
    return factor_of


def normal_values(stream_key, shape, deviation, most, cuts=(), dtype=jnp.bfloat16):
    array = deviation * jax.random.normal(stream_key, shape, jnp.float32)
    if cuts:
        array = array * shard_levels(stream_key, shape, cuts, -0.22, 0.18)
    return jnp.clip(array, -most, most).astype(dtype)


def setup_inputs(seed: int = 0) -> dict:
    streams_of = jax.random.split(jax.random.key(seed), 13)
    return {
        "columns": normal_values(streams_of[0], (HISTS, LEN, D), 1.0, 6.0, ((1, 32), (2, 16))),
        "gaps": draw_gaps(jax.random.fold_in(streams_of[12], 71), 0),
        "norm_in": jnp.clip(1.0 + 0.18 * jax.random.normal(streams_of[2], (D,), jnp.float32), 0.1, 1.9),
        "w_gate": normal_values(streams_of[3], (D, INNER), D ** -0.5, 0.25),
        "w_xbc": normal_values(streams_of[4], (D, INNER + 2 * STATE), D ** -0.5, 0.25),
        "w_step": normal_values(streams_of[5], (D, HEADS), D ** -0.5, 0.25),
        "step_bias": jnp.clip(jax.random.uniform(streams_of[6], (HEADS,), jnp.float32, -1.0, 1.0), -1.0, 1.0),
        "conv_weight": draw_conv_weight(jax.random.fold_in(streams_of[12], 71), 0),
        "conv_bias": draw_conv_bias(jax.random.fold_in(streams_of[12], 71), 0),
        "rates": draw_rates(jax.random.fold_in(streams_of[12], 71), 0),
        "norm_out": jnp.clip(1.0 + 0.18 * jax.random.normal(streams_of[10], (INNER,), jnp.float32), 0.1, 1.9),
        "w_out": normal_values(streams_of[11], (INNER, D), INNER ** -0.5, 0.1875),
    }


epsilon = 1e-05

def rms_rows(values, gain):
    return values * lax.rsqrt(lax.optimization_barrier(jnp.mean(values * values, axis=-1, keepdims=True)) + epsilon) * gain

def history(columns_one, gaps_one, norm_in, w_gate, w_xbc, w_step, step_bias, conv_weight, conv_bias, rates, norm_out, w_out):
    inner = HEADS * HEAD_DIM
    normed = rms_rows(columns_one.astype(jnp.float32), norm_in).astype(jnp.bfloat16)
    gate = jnp.dot(normed, w_gate, preferred_element_type=jnp.float32).astype(jnp.bfloat16)
    xbc = jnp.dot(normed, w_xbc, preferred_element_type=jnp.float32).astype(jnp.bfloat16)
    step_raw = jnp.dot(normed, w_step, preferred_element_type=jnp.float32)
    width = xbc.shape[1]
    padded = jnp.concatenate([jnp.zeros((CONV - 1, width), jnp.float32), xbc.astype(jnp.float32)], axis=0)
    conv = conv_bias + conv_weight[0] * padded[0:LEN]
    for offset in range(1, CONV):
        conv = conv + conv_weight[offset] * padded[offset:offset + LEN]
    act = jax.nn.silu(conv).astype(jnp.bfloat16)
    count = LEN // BLOCK
    xs = act[:, :inner].reshape(count, BLOCK, HEADS, HEAD_DIM)
    bm = act[:, inner:inner + STATE].reshape(count, BLOCK, STATE)
    cm = act[:, inner + STATE:].reshape(count, BLOCK, STATE)
    steps_dt = jax.nn.softplus(step_raw + step_bias)
    decay = -rates * steps_dt * gaps_one[:, None]
    steps_dt = steps_dt.reshape(count, BLOCK, HEADS)
    decay = decay.reshape(count, BLOCK, HEADS)
    rows = lax.broadcasted_iota(jnp.int32, (BLOCK, BLOCK), 0)
    cols = lax.broadcasted_iota(jnp.int32, (BLOCK, BLOCK), 1)

    def advance(state, block):
        cx, cb, cc, cdt, cda = block
        cs = jnp.cumsum(cda, axis=0)
        scores = jnp.dot(cc, cb.T, preferred_element_type=jnp.float32)
        trail = cs.T
        diff = trail[:, :, None] - trail[:, None, :]
        factor = jnp.exp(jnp.where((rows >= cols)[None], diff, -jnp.inf))
        mix = (scores[None] * factor * cdt.T[:, None, :]).astype(jnp.bfloat16)
        y_in = jnp.einsum('hts,shp->thp', mix.astype(jnp.float32), cx.astype(jnp.float32))
        rounded_state = lax.optimization_barrier(state.astype(jnp.bfloat16)).astype(jnp.float32)
        picked = jnp.einsum('tn,hpn->thp', cc.astype(jnp.float32), rounded_state)
        y_state = jnp.exp(cs)[:, :, None] * picked
        weighted = ((jnp.exp(cs[-1][None, :] - cs) * cdt)[:, :, None] * cx.astype(jnp.float32)).astype(jnp.bfloat16)
        block_state = jnp.einsum('shp,sn->hpn', weighted.astype(jnp.float32), cb.astype(jnp.float32))
        state = jnp.exp(cs[-1])[:, None, None] * state + block_state
        return (state, y_in + y_state)
    start_state = jnp.zeros((HEADS, HEAD_DIM, STATE), jnp.float32)
    final_state, outputs = lax.scan(advance, start_state, (xs, bm, cm, steps_dt, decay))
    y = outputs.reshape(LEN, inner)
    gated = y * jax.nn.silu(gate.astype(jnp.float32))
    out_normed = rms_rows(gated, norm_out).astype(jnp.bfloat16)
    return jnp.dot(out_normed, w_out, preferred_element_type=jnp.float32).astype(jnp.bfloat16)

def reference(columns, gaps, norm_in, w_gate, w_xbc, w_step, step_bias, conv_weight, conv_bias, rates, norm_out, w_out):

    def one_history(paired):
        return history(paired[0], paired[1], norm_in, w_gate, w_xbc, w_step, step_bias, conv_weight, conv_bias, rates, norm_out, w_out)
    return lax.map(one_history, (columns, gaps))
```

```python
import jax
import jax.numpy as jnp
from jax import lax
from jax.sharding import PartitionSpec as P

BLOCK = 256


epsilon = 1e-05


def passed_along(block, axis, distance):
    devices = range(lax.axis_size(axis))
    route = [(i - distance, i) for i in devices if i - distance in devices]
    return lax.ppermute(block, axis, route)


def rms_rows(values, gain):
    return values * lax.rsqrt(jnp.mean(values * values, axis=-1, keepdims=True) + epsilon) * gain


def block_terms(cx, cb, cc, cdt, cda):
    length = cx.shape[0]
    cs = jnp.cumsum(cda, axis=0)
    scores = jnp.dot(cc, cb.T, preferred_element_type=jnp.float32)
    trail = cs.T
    diff = trail[:, :, None] - trail[:, None, :]
    rows = lax.broadcasted_iota(jnp.int32, (length, length), 0)
    cols = lax.broadcasted_iota(jnp.int32, (length, length), 1)
    factor = jnp.exp(jnp.where((rows >= cols)[None], diff, -jnp.inf))
    mix = (scores[None] * factor * cdt.T[:, None, :]).astype(jnp.bfloat16)
    y_in = jnp.einsum("hts,shp->thp", mix, cx, preferred_element_type=jnp.float32)
    weighted = ((jnp.exp(cs[-1][None, :] - cs) * cdt)[:, :, None] * cx.astype(jnp.float32)).astype(
        jnp.bfloat16
    )
    block_state = jnp.einsum("shp,sn->hpn", weighted, cb, preferred_element_type=jnp.float32)
    return (y_in, block_state, cs)


def local_pass(xs, bm, cm, steps_dt, decay):
    length, heads, head_dim = xs.shape
    state_width = bm.shape[1]
    count = length // BLOCK
    blocks = (
        xs.reshape(count, BLOCK, heads, head_dim),
        bm.reshape(count, BLOCK, state_width),
        cm.reshape(count, BLOCK, state_width),
        steps_dt.reshape(count, BLOCK, heads),
        decay.reshape(count, BLOCK, heads),
    )

    def one_block(block):
        return block_terms(block[0], block[1], block[2], block[3], block[4])

    y_in, states, cs = lax.map(one_block, blocks)
    ends = cs[:, -1, :]

    def walk(state, paired):
        return (jnp.exp(paired[0])[:, None, None] * state + paired[1], state)

    final, entries = lax.scan(walk, jnp.zeros(states.shape[1:], jnp.float32), (ends, states))
    starts = jnp.cumsum(ends, axis=0) - ends
    total = jnp.sum(ends, axis=0)
    return (y_in, cs, entries, starts, final, total)


def carried_output(cm, cs, entries, starts, incoming):
    count, length = (cs.shape[0], cs.shape[1])
    queries = cm.reshape(count, length, cm.shape[1])
    enter = (entries + jnp.exp(starts)[:, :, None, None] * incoming[None]).astype(jnp.bfloat16)
    picked = jnp.einsum("ktn,khpn->kthp", queries, enter, preferred_element_type=jnp.float32)
    return jnp.exp(cs)[..., None] * picked


GROUP = 8


def parts_of(values):
    high = values.astype(jnp.bfloat16)
    rest = values - high.astype(jnp.float32)
    middle = rest.astype(jnp.bfloat16)
    low = (rest - middle.astype(jnp.float32)).astype(jnp.bfloat16)
    return jnp.stack([high, middle, low])


def within_groups(blocks):
    count = lax.axis_size("seq") // GROUP
    groups = [[g * GROUP + i for i in range(GROUP)] for g in range(count)]
    return lax.all_to_all(
        blocks, "seq", split_axis=0, concat_axis=0, tiled=True, axis_index_groups=groups
    )


def with_decay(state, logs):
    lead = state.shape[:-3]
    heads, head_dim, width = state.shape[-3:]
    rows = jnp.moveaxis(parts_of(logs), 0, -1).reshape(lead + (heads * 3, 1))
    rows = jnp.broadcast_to(rows, lead + (heads * 3, width))
    pad = [(0, 0)] * len(lead) + [(0, -(heads * 3) % 8), (0, 0)]
    flat = state.astype(jnp.bfloat16).reshape(lead + (heads * head_dim, width))
    return jnp.concatenate([flat, jnp.pad(rows, pad)], axis=-2)


def without_decay(block, heads):
    width = block.shape[-1]
    lead = block.shape[:-2]
    block = block.astype(jnp.float32)
    size = block.shape[-2] - heads * 3 - (-(heads * 3) % 8)
    state = block[..., :size, :].reshape(lead + (heads, size // heads, width))
    logs = block[..., size : size + heads * 3, 0].reshape(lead + (heads, 3)).sum(-1)
    return (state, logs)


def carry_in(total, final):
    heads, head_dim, width = final.shape
    own = heads // GROUP
    grouped = with_decay(
        final.reshape(GROUP, own, head_dim, width), total.reshape(GROUP, own)
    )
    states, logs = without_decay(within_groups(grouped), own)
    prefix = [jnp.zeros_like(states[0])]
    before = [jnp.zeros_like(logs[0])]
    for member in range(GROUP):
        prefix.append(jnp.exp(logs[member])[:, None, None] * prefix[-1] + states[member])
        before.append(before[-1] + logs[member])
    block = with_decay(prefix[-1], before[-1])
    count = lax.axis_size("seq") // GROUP
    arrived = [
        without_decay(passed_along(block, "seq", GROUP * step), own) for step in range(1, count)
    ]
    enter = arrived[-1][0]
    for state, log in arrived[-2::-1]:
        enter = state + jnp.exp(log)[:, None, None] * enter
    back = jnp.stack(
        [
            prefix[member] + jnp.exp(before[member])[:, None, None] * enter
            for member in range(GROUP)
        ]
    ).astype(jnp.bfloat16)
    return within_groups(back.reshape(GROUP, own * head_dim, width)).reshape(
        heads, head_dim, width
    )


def local(
    columns,
    gaps,
    norm_in,
    w_gate,
    w_xbc,
    w_step,
    step_bias,
    conv_weight,
    conv_bias,
    rates,
    norm_out,
    w_out,
):
    inner = w_gate.shape[1]
    heads = w_step.shape[1]
    head_dim = inner // heads
    state_width = (w_xbc.shape[1] - inner) // 2
    reach = conv_weight.shape[0] - 1
    normed = rms_rows(
        lax.all_to_all(columns, "table", split_axis=0, concat_axis=2, tiled=True).astype(
            jnp.float32
        ),
        norm_in,
    ).astype(jnp.bfloat16)
    gate = jnp.einsum("brd,de->bre", normed, w_gate, preferred_element_type=jnp.float32).astype(
        jnp.bfloat16
    )
    xbc = jnp.einsum("brd,de->bre", normed, w_xbc, preferred_element_type=jnp.float32).astype(
        jnp.bfloat16
    )
    step_raw = jnp.einsum("brd,de->bre", normed, w_step, preferred_element_type=jnp.float32)
    gate, xbc, step_raw, normed = (gate, xbc, step_raw, normed)
    hists, length = (xbc.shape[0], xbc.shape[1])
    rim = passed_along(xbc[:, length - reach :, :], "seq", 1)
    padded = jnp.concatenate([rim, xbc], axis=1).astype(jnp.float32)
    conv = conv_bias + conv_weight[0] * padded[:, 0:length]
    for offset in range(1, reach + 1):
        conv = conv + conv_weight[offset] * padded[:, offset : offset + length]
    act = jax.nn.silu(conv).astype(jnp.bfloat16)
    xs = act[:, :, :inner].reshape(hists, length, heads, head_dim)
    bm = act[:, :, inner : inner + state_width]
    cm = act[:, :, inner + state_width :]
    steps_dt = jax.nn.softplus(step_raw + step_bias)
    decay = -rates * steps_dt * gaps[:, :, None]
    y_in, cs, entries, starts, final, total = jax.vmap(local_pass)(xs, bm, cm, steps_dt, decay)
    incoming = carry_in(total[0], final[0])[None].astype(jnp.float32)
    state_terms = jax.vmap(carried_output)(cm, cs, entries, starts, incoming)
    y = (y_in + state_terms).reshape(hists, length, inner)
    gated = y * jax.nn.silu(gate.astype(jnp.float32))
    out_normed = rms_rows(gated, norm_out).astype(jnp.bfloat16)
    return jnp.einsum("bri,id->brd", out_normed, w_out, preferred_element_type=jnp.float32).astype(
        jnp.bfloat16
    )


def solution(mesh):
    in_specs = (
        P(None, "seq", "table"),
        P("table", "seq"),
        P(),
        P(),
        P(),
        P(),
        P(),
        P(),
        P(),
        P(),
        P(),
        P(),
    )
    out_specs = P("table", "seq", None)
    return jax.shard_map(local, mesh=mesh, in_specs=in_specs, out_specs=out_specs, check_vma=False)
```

```python
import functools

import jax
import jax.numpy as jnp
from jax import lax
from jax.experimental import pallas as pl
from jax.experimental.pallas import tpu as pltpu
from jax.sharding import PartitionSpec as P

GROUP = 8
EDGE = 128
EXTRA = 8
BIAS, GAIN_IN, GAIN_OUT = 4, 5, 6
epsilon = 1e-05
f32 = jnp.float32
bf16 = jnp.bfloat16


def passed_along(block, axis, distance):
    devices = range(lax.axis_size(axis))
    route = [(i - distance, i) for i in devices if i - distance in devices]
    return lax.ppermute(block, axis, route)


def within_groups(blocks):
    count = lax.axis_size("seq") // GROUP
    groups = [[g * GROUP + i for i in range(GROUP)] for g in range(count)]
    return lax.all_to_all(
        blocks, "seq", split_axis=0, concat_axis=0, tiled=True, axis_index_groups=groups
    )


def contract(a, b, dims):
    return lax.dot_general(a, b, (dims, ((), ())), preferred_element_type=f32)


def columns_of(vec_ref, at):
    return vec_ref[:, at : at + EDGE].T


def normed_columns(x_ref, vec_ref, out_ref):
    depth, length = x_ref.shape
    total = jnp.zeros((1, length), f32)
    for at in range(0, depth, 64):
        x = x_ref[at : at + 64, :].astype(f32)
        total = total + jnp.sum(x * x, axis=0, keepdims=True)
    scale = lax.rsqrt(total / depth + epsilon)
    for at in range(0, depth, EDGE):
        gain = columns_of(vec_ref, at)[:, GAIN_IN : GAIN_IN + 1]
        x = x_ref[at : at + EDGE, :].astype(f32)
        out_ref[at : at + EDGE, :] = (x * scale * gain).astype(bf16)


def running_sum(values):
    length = values.shape[1]
    lane = lax.broadcasted_iota(jnp.int32, values.shape, 1)
    reach = 1
    while reach < length:
        values = values + jnp.where(lane >= reach, pltpu.roll(values, reach, axis=1), 0.0)
        reach *= 2
    return values


def main_kernel(x_ref, vec_ref, w_xbc_ref, w_step_ref, head_ref, gaps_ref,
                normed_ref, act_ref, dt_ref, cs_ref, state_ref, logs_ref, first_ref, coef_first_ref,
                coef_ref, rows_ref):
    width = act_ref.shape[0]
    length = x_ref.shape[1]
    heads = dt_ref.shape[0]
    inner, state_width = state_ref.shape
    head_dim = inner // heads
    normed_columns(x_ref, vec_ref, normed_ref)
    first_ref[...] = x_ref[:, 0:EDGE].astype(f32).T[0:EXTRA, :]
    normed = normed_ref[...]
    raw = jnp.dot(w_step_ref[...], normed, preferred_element_type=f32)
    raw = raw + head_ref[:, 0:1]
    dt = jnp.maximum(raw, 0.0) + jnp.log1p(jnp.exp(-jnp.abs(raw)))
    dt_ref[...] = dt
    cs = running_sum(-head_ref[:, 1:2] * dt * gaps_ref[...])
    cs_ref[...] = cs
    coef = jnp.exp(cs[:, length - 1 : length] - cs) * dt
    coef_first = coef[:, 0:EDGE].T[0:EXTRA, :]
    for head in range(heads):
        coef_first_ref[:, head * head_dim : (head + 1) * head_dim] = jnp.broadcast_to(
            coef_first[:, head : head + 1], (EXTRA, head_dim)
        )
    lane = lax.broadcasted_iota(jnp.int32, coef.shape, 1)
    coef_ref[...] = jnp.where(lane >= EXTRA, coef, 0.0)
    total = jnp.broadcast_to(cs[:, length - 1 : length], (heads, state_width))
    pack_logs(total, rows_ref)
    logs_ref[...] = rows_ref[...].astype(bf16)

    def act_of(at, step):
        whole = (
            jnp.dot(w_xbc_ref[at : at + step, :], normed, preferred_element_type=f32)
            .astype(bf16)
            .astype(f32)
        )
        weights = columns_of(vec_ref, at)
        conv = weights[:, BIAS : BIAS + 1]
        for tap in range(BIAS):
            back = BIAS - 1 - tap
            moved = pltpu.roll(whole, back, axis=1) if back else whole
            conv = conv + weights[:, tap : tap + 1] * moved
        act = (conv * jax.nn.sigmoid(conv)).astype(bf16)
        act_ref[at : at + step, :] = act
        return act

    b = act_of(inner, state_width)
    act_of(inner + state_width, state_width)
    step = 2 * head_dim
    for at in range(0, inner, step):
        act = act_of(at, step).astype(f32)
        head = at // head_dim
        coef = jnp.concatenate(
            [jnp.broadcast_to(coef_ref[h : h + 1, :], (head_dim, length)) for h in (head, head + 1)],
            axis=0,
        )
        state_ref[at : at + step, :] = contract((act * coef).astype(bf16), b, ((1,), (1,)))


def edge_kernel(edge_ref, first_ref, vec_ref, w_xbc_ref, coef_ref, state_ref, logs_ref,
                send_ref, act_ref, rows_ref):
    inner, state_width = state_ref.shape
    depth = first_ref.shape[1]
    before = edge_ref[...].astype(f32).T[EDGE - EXTRA :, :]
    x = jnp.concatenate([before, first_ref[...]], axis=0)
    scale = lax.rsqrt(jnp.mean(x * x, axis=1, keepdims=True) + epsilon)
    normed = (x * scale * vec_ref[GAIN_IN : GAIN_IN + 1, :depth]).astype(bf16)
    rows_ref[...] = contract(normed, w_xbc_ref[...], ((1,), (1,))).astype(bf16).astype(f32)
    conv = vec_ref[BIAS : BIAS + 1, :]
    for tap in range(BIAS):
        at = EXTRA - (BIAS - 1 - tap)
        conv = conv + vec_ref[tap : tap + 1, :] * rows_ref[at : at + EXTRA, :]
    act = (conv * jax.nn.sigmoid(conv)).astype(bf16).astype(f32)
    act_ref[...] = act
    weighted = (act[:, :inner] * coef_ref[...]).astype(bf16).astype(f32)
    none = jnp.zeros_like(weighted)
    weighted = jnp.concatenate([weighted, none], axis=0).astype(bf16)
    b = act[:, inner : inner + state_width]
    b = jnp.concatenate([b, jnp.zeros_like(b)], axis=0).astype(bf16)
    size = inner // GROUP
    for part in range(GROUP):
        rows = slice(part * size, (part + 1) * size)
        late = contract(weighted[:, rows], b, ((0,), (0,)))
        send_ref[part, 0:size, :] = (state_ref[rows, :] + late).astype(bf16)
        send_ref[part, size : size + EXTRA, :] = logs_ref[part * EXTRA : (part + 1) * EXTRA, :]


def pack_logs(total, rows_ref):
    heads = total.shape[0]
    own = rows_ref.shape[0] // EXTRA
    own = heads // own
    rows_ref[...] = jnp.zeros_like(rows_ref)
    rest = total
    for piece in range(3):
        part = rest.astype(bf16).astype(f32)
        rest = rest - part
        for head in range(heads):
            at = head // own * EXTRA + head % own * 3 + piece
            rows_ref[at : at + 1, :] = part[head : head + 1, :]


def read_logs(rows, own):
    rows = rows.astype(f32)
    return [
        rows[3 * h : 3 * h + 1, :] + rows[3 * h + 1 : 3 * h + 2, :] + rows[3 * h + 2 : 3 * h + 3, :]
        for h in range(own)
    ]


def prefix_kernel(own, states_ref, send_ref, rows_ref):
    size = send_ref.shape[0] - EXTRA
    head_dim = size // own
    width = send_ref.shape[1]
    logs = [read_logs(states_ref[m, size : size + EXTRA, :], own) for m in range(GROUP)]
    for h in range(own):
        rows = slice(h * head_dim, (h + 1) * head_dim)
        state = jnp.zeros((head_dim, width), f32)
        for m in range(GROUP):
            state = jnp.exp(logs[m][h]) * state + states_ref[m, rows, :].astype(f32)
        send_ref[rows, :] = state.astype(bf16)
    total = [sum(logs[m][h] for m in range(GROUP)) for h in range(own)]
    pack_logs(jnp.concatenate(total, axis=0), rows_ref)
    send_ref[size : size + EXTRA, :] = rows_ref[...].astype(bf16)


def combine_kernel(own, states_ref, *refs):
    arrived, back_ref = refs[:-1], refs[-1]
    size = back_ref.shape[1]
    head_dim = size // own
    width = back_ref.shape[2]
    logs = [read_logs(states_ref[m, size : size + EXTRA, :], own) for m in range(GROUP)]
    jumps = [read_logs(ref[size : size + EXTRA, :], own) for ref in arrived]
    for h in range(own):
        rows = slice(h * head_dim, (h + 1) * head_dim)
        state = jnp.zeros((head_dim, width), f32)
        for ref, jump in zip(arrived[::-1], jumps[::-1]):
            state = jnp.exp(jump[h]) * state + ref[rows, :].astype(f32)
        for m in range(GROUP):
            back_ref[m, rows, :] = state.astype(bf16)
            state = jnp.exp(logs[m][h]) * state + states_ref[m, rows, :].astype(f32)


def inside_kernel(normed_ref, w_gate_ref, main_ref, first_ref, dt_ref, cs_ref,
                  gate_ref, y_ref, query_ref, act_ref, scores_ref, mix_ref, weight_ref, sem):
    fetch = pltpu.make_async_copy(w_gate_ref, weight_ref, sem)
    fetch.start()
    heads, length = dt_ref.shape
    inner = gate_ref.shape[0]
    lane = lax.broadcasted_iota(jnp.int32, (EDGE, EDGE), 1)
    rest = jnp.zeros((EDGE - EXTRA, EDGE), f32)
    for at in range(0, act_ref.shape[0], EDGE):
        rows = slice(at, at + EDGE)
        first = jnp.concatenate([first_ref[:, rows], rest], axis=0).T
        kept = main_ref[rows, 0:EDGE].astype(f32)
        act_ref[rows, 0:EDGE] = jnp.where(lane < EXTRA, first, kept).astype(bf16)
        act_ref[rows, EDGE:] = main_ref[rows, EDGE:]
    head_dim = inner // heads
    state_width = (act_ref.shape[0] - inner) // 2
    query_ref[...] = act_ref[inner + state_width :, :]
    scores_ref[...] = contract(
        act_ref[inner : inner + state_width, :], act_ref[inner + state_width :, :], ((0,), (0,))
    )
    cs_col = cs_ref[...].T
    dt_col = dt_ref[...].T
    half = length // 2
    mix_ref[...] = jnp.zeros_like(mix_ref)
    later = lax.broadcasted_iota(jnp.int32, (half, half), 1)
    early = lax.broadcasted_iota(jnp.int32, (half, half), 0)
    keep = later >= early
    for h in range(heads):
        for s in (0, half):
            cs_s = jnp.broadcast_to(cs_col[s : s + half, h : h + 1], (half, half))
            dt_s = jnp.broadcast_to(dt_col[s : s + half, h : h + 1], (half, half))
            for t in range(s, length, half):
                diff = cs_ref[h : h + 1, t : t + half] - cs_s
                if s == t:
                    diff = jnp.where(keep, diff, -jnp.inf)
                mix_ref[s : s + half, t : t + half] = (
                    scores_ref[s : s + half, t : t + half] * jnp.exp(diff) * dt_s
                ).astype(bf16)
        rows = slice(h * head_dim, (h + 1) * head_dim)
        y_ref[rows, :] = jnp.dot(act_ref[rows, :], mix_ref[...], preferred_element_type=f32)
    fetch.wait()
    normed = normed_ref[...]
    for at in range(0, inner, 256):
        gate = contract(weight_ref[:, at : at + 256], normed, ((0,), (0,)))
        gate = gate.astype(bf16).astype(f32)
        gate_ref[at : at + 256, :] = gate * jax.nn.sigmoid(gate)


def output_kernel(carried_ref, query_ref, cs_ref, y_ref, gate_ref, vec_ref, w_out_ref,
                  out_ref, gated_ref, normed_ref, weight_ref, sem):
    fetch = pltpu.make_async_copy(w_out_ref, weight_ref, sem)
    fetch.start()
    heads, length = cs_ref.shape
    inner = y_ref.shape[0]
    head_dim = inner // heads
    queries = query_ref[...]
    grown = jnp.exp(cs_ref[...])
    total = jnp.zeros((1, length), f32)
    step = 2 * head_dim
    for at in range(0, inner, step):
        picked = jnp.dot(carried_ref[at : at + step, :], queries, preferred_element_type=f32)
        for h in range(at // head_dim, (at + step) // head_dim):
            rows = slice(h * head_dim, (h + 1) * head_dim)
            own = picked[h * head_dim - at : (h + 1) * head_dim - at, :]
            y = y_ref[rows, :] + grown[h : h + 1, :] * own
            gated = y * gate_ref[rows, :]
            gated_ref[rows, :] = gated
            total = total + jnp.sum(gated * gated, axis=0, keepdims=True)
    scale = lax.rsqrt(total / inner + epsilon)
    for at in range(0, inner, EDGE):
        gain = columns_of(vec_ref, at)[:, GAIN_OUT : GAIN_OUT + 1]
        normed_ref[at : at + EDGE, :] = (gated_ref[at : at + EDGE, :] * scale * gain).astype(bf16)
    fetch.wait()
    out_ref[...] = contract(normed_ref[...], weight_ref[...], ((0,), (0,))).astype(bf16)


def call(kernel, outs, scratch, *args, fetched=()):
    vmem = pl.BlockSpec(memory_space=pltpu.VMEM)
    left = pl.BlockSpec(memory_space=pl.ANY)
    single = not isinstance(outs, list)
    return pl.pallas_call(
        kernel,
        out_shape=outs,
        in_specs=[left if at in fetched else vmem for at in range(len(args))],
        out_specs=vmem if single else [vmem] * len(outs),
        scratch_shapes=scratch,
        compiler_params=pltpu.CompilerParams(vmem_limit_bytes=12 << 20),
    )(*args)


def local(
    columns,
    gaps,
    norm_in,
    w_gate,
    w_xbc,
    w_step,
    step_bias,
    conv_weight,
    conv_bias,
    rates,
    norm_out,
    w_out,
):
    length = columns.shape[1]
    depth, inner = w_gate.shape
    heads = w_step.shape[1]
    width = w_xbc.shape[1]
    state_width = (width - inner) // 2
    own = heads // GROUP
    size = inner // GROUP
    shape = jax.ShapeDtypeStruct

    rows = [conv_weight, conv_bias[None], norm_in[None], norm_out[None]]
    vec = jnp.concatenate([jnp.pad(r, ((0, 0), (0, width - r.shape[1]))) for r in rows])
    vec = jnp.pad(vec, ((0, 8 - vec.shape[0]), (0, 0)))
    head = jnp.stack([step_bias, rates], axis=1)

    whole = lax.all_to_all(columns, "table", split_axis=0, concat_axis=2, tiled=True)
    whole, w_xbc_t, vec, head = lax.optimization_barrier((whole, w_xbc.T, vec, head))
    x = whole.reshape(length, depth).T
    edge = passed_along(x[:, length - EDGE :], "seq", 1)
    normed, act, dt, cs, state, logs, first, coef_first = call(
        main_kernel,
        [
            shape((depth, length), bf16),
            shape((width, length), bf16),
            shape((heads, length), f32),
            shape((heads, length), f32),
            shape((inner, state_width), f32),
            shape((GROUP * EXTRA, state_width), bf16),
            shape((EXTRA, depth), f32),
            shape((EXTRA, inner), f32),
        ],
        [pltpu.VMEM((heads, length), f32), pltpu.VMEM((GROUP * EXTRA, state_width), f32)],
        x, vec, w_xbc_t, w_step.T, head, gaps,
    )
    send, act_first = call(
        edge_kernel,
        [shape((GROUP, size + EXTRA, state_width), bf16), shape((EXTRA, width), f32)],
        [pltpu.VMEM((2 * EXTRA, width), f32)],
        edge, first, vec, w_xbc_t, coef_first, state, logs,
    )
    states = within_groups(send)
    total = call(
        functools.partial(prefix_kernel, own),
        shape((size + EXTRA, state_width), bf16),
        [pltpu.VMEM((EXTRA, state_width), f32)],
        states,
    )
    count = lax.axis_size("seq") // GROUP
    arrived = [passed_along(total, "seq", GROUP * step) for step in range(1, count)]
    gate, y, query = call(
        inside_kernel,
        [
            shape((inner, length), f32),
            shape((inner, length), f32),
            shape((state_width, length), bf16),
        ],
        [
            pltpu.VMEM((width, length), bf16),
            pltpu.VMEM((length, length), f32),
            pltpu.VMEM((length, length), bf16),
            pltpu.VMEM((depth, inner), bf16),
            pltpu.SemaphoreType.DMA,
        ],
        normed, w_gate, act, act_first, dt, cs,
        fetched=(1,),
    )
    gate, y, *arrived = lax.optimization_barrier((gate, y, *arrived))
    back = call(
        functools.partial(combine_kernel, own),
        shape((GROUP, size, state_width), bf16),
        [],
        states, *arrived,
    )
    carried = within_groups(back).reshape(inner, state_width)
    out = call(
        output_kernel,
        shape((length, w_out.shape[1]), bf16),
        [
            pltpu.VMEM((inner, length), f32),
            pltpu.VMEM((inner, length), bf16),
            pltpu.VMEM(w_out.shape, bf16),
            pltpu.SemaphoreType.DMA,
        ],
        carried, query, cs, y, gate, vec, w_out,
        fetched=(6,),
    )
    return out[None]


def solution(mesh):
    in_specs = (
        P(None, "seq", "table"),
        P("table", "seq"),
        P(),
        P(),
        P(),
        P(),
        P(),
        P(),
        P(),
        P(),
        P(),
        P(),
    )
    out_specs = P("table", "seq", None)
    return jax.shard_map(local, mesh=mesh, in_specs=in_specs, out_specs=out_specs, check_vma=False)
```

```python
import functools

import jax
import jax.numpy as jnp
from jax import lax
from jax.experimental import pallas as pl
from jax.experimental.pallas import tpu as pltpu
from jax.sharding import PartitionSpec as P

GROUP = 8
EDGE = 128
EXTRA = 8
BIAS, GAIN_IN, GAIN_OUT = 4, 5, 6
epsilon = 1e-05
f32 = jnp.float32
bf16 = jnp.bfloat16


def passed_along(block, axis, distance):
    devices = range(lax.axis_size(axis))
    route = [(i - distance, i) for i in devices if i - distance in devices]
    return lax.ppermute(block, axis, route)


def within_groups(blocks):
    count = lax.axis_size("seq") // GROUP
    groups = [[g * GROUP + i for i in range(GROUP)] for g in range(count)]
    return lax.all_to_all(
        blocks, "seq", split_axis=0, concat_axis=0, tiled=True, axis_index_groups=groups
    )


def contract(a, b, dims):
    return lax.dot_general(a, b, (dims, ((), ())), preferred_element_type=f32)


def columns_of(vec_ref, at):
    return vec_ref[:, at : at + EDGE].T


def normed_columns(x_ref, vec_ref, out_ref):
    depth, length = x_ref.shape
    total = jnp.zeros((1, length), f32)
    for at in range(0, depth, 64):
        x = x_ref[at : at + 64, :].astype(f32)
        total = total + jnp.sum(x * x, axis=0, keepdims=True)
    scale = lax.rsqrt(total / depth + epsilon)
    for at in range(0, depth, EDGE):
        gain = columns_of(vec_ref, at)[:, GAIN_IN : GAIN_IN + 1]
        x = x_ref[at : at + EDGE, :].astype(f32)
        out_ref[at : at + EDGE, :] = (x * scale * gain).astype(bf16)


def running_sum(values):
    length = values.shape[1]
    lane = lax.broadcasted_iota(jnp.int32, values.shape, 1)
    reach = 1
    while reach < length:
        values = values + jnp.where(lane >= reach, pltpu.roll(values, reach, axis=1), 0.0)
        reach *= 2
    return values


def main_kernel(x_ref, vec_ref, w_xbc_ref, w_step_ref, head_ref, gaps_ref,
                normed_ref, act_ref, dt_ref, cs_ref, state_ref, logs_ref, first_ref, coef_first_ref,
                coef_ref, rows_ref, upright_ref, shift_ref):
    depth, length = x_ref.shape
    heads = dt_ref.shape[0]
    inner, state_width = state_ref.shape
    head_dim = inner // heads
    normed_columns(x_ref, vec_ref, normed_ref)
    first_ref[...] = x_ref[:, 0:EDGE].astype(f32).T[0:EXTRA, :]
    normed = normed_ref[...]
    raw = jnp.dot(w_step_ref[...], normed, preferred_element_type=f32)
    raw = raw + head_ref[:, 0:1]
    dt = jnp.maximum(raw, 0.0) + jnp.log1p(jnp.exp(-jnp.abs(raw)))
    dt_ref[...] = dt
    cs = running_sum(-head_ref[:, 1:2] * dt * gaps_ref[...])
    cs_ref[...] = cs
    coef = jnp.exp(cs[:, length - 1 : length] - cs) * dt
    coef_first = coef[:, 0:EDGE].T[0:EXTRA, :]
    for head in range(heads):
        coef_first_ref[:, head * head_dim : (head + 1) * head_dim] = jnp.broadcast_to(
            coef_first[:, head : head + 1], (EXTRA, head_dim)
        )
    lane = lax.broadcasted_iota(jnp.int32, coef.shape, 1)
    coef_ref[...] = jnp.where(lane >= EXTRA, coef, 0.0)
    total = jnp.broadcast_to(cs[:, length - 1 : length], (heads, state_width))
    pack_logs(total, rows_ref)
    logs_ref[...] = rows_ref[...].astype(bf16)

    for at in range(0, depth, EDGE):
        upright_ref[:, at : at + EDGE] = normed_ref[at : at + EDGE, :].astype(f32).T.astype(bf16)
    shift_ref[0:EXTRA, :] = jnp.zeros((EXTRA, shift_ref.shape[1]), f32)
    upright = upright_ref[...]

    def act_of(at, step):
        cols = slice(at, at + step)
        whole = jnp.dot(upright, w_xbc_ref[:, cols], preferred_element_type=f32)
        shift_ref[EXTRA:, cols] = whole.astype(bf16).astype(f32)
        conv = vec_ref[BIAS : BIAS + 1, cols]
        for tap in range(BIAS):
            first = EXTRA - (BIAS - 1 - tap)
            conv = conv + vec_ref[tap : tap + 1, cols] * shift_ref[first : first + length, cols]
        act = (conv * jax.nn.sigmoid(conv)).T.astype(bf16)
        act_ref[at : at + step, :] = act
        return act

    b = act_of(inner, state_width)
    act_of(inner + state_width, state_width)
    step = 2 * head_dim
    for at in range(0, inner, step):
        act = act_of(at, step).astype(f32)
        head = at // head_dim
        coef = jnp.concatenate(
            [jnp.broadcast_to(coef_ref[h : h + 1, :], (head_dim, length)) for h in (head, head + 1)],
            axis=0,
        )
        state_ref[at : at + step, :] = contract((act * coef).astype(bf16), b, ((1,), (1,)))


def edge_kernel(edge_ref, first_ref, vec_ref, w_xbc_ref, coef_ref, state_ref, logs_ref,
                send_ref, act_ref, rows_ref):
    inner, state_width = state_ref.shape
    depth = first_ref.shape[1]
    before = edge_ref[...].astype(f32).T[EDGE - EXTRA :, :]
    x = jnp.concatenate([before, first_ref[...]], axis=0)
    scale = lax.rsqrt(jnp.mean(x * x, axis=1, keepdims=True) + epsilon)
    normed = (x * scale * vec_ref[GAIN_IN : GAIN_IN + 1, :depth]).astype(bf16)
    whole = jnp.dot(normed, w_xbc_ref[...], preferred_element_type=f32)
    rows_ref[...] = whole.astype(bf16).astype(f32)
    conv = vec_ref[BIAS : BIAS + 1, :]
    for tap in range(BIAS):
        at = EXTRA - (BIAS - 1 - tap)
        conv = conv + vec_ref[tap : tap + 1, :] * rows_ref[at : at + EXTRA, :]
    act = (conv * jax.nn.sigmoid(conv)).astype(bf16).astype(f32)
    act_ref[...] = act
    weighted = (act[:, :inner] * coef_ref[...]).astype(bf16).astype(f32)
    none = jnp.zeros_like(weighted)
    weighted = jnp.concatenate([weighted, none], axis=0).astype(bf16)
    b = act[:, inner : inner + state_width]
    b = jnp.concatenate([b, jnp.zeros_like(b)], axis=0).astype(bf16)
    size = inner // GROUP
    for part in range(GROUP):
        rows = slice(part * size, (part + 1) * size)
        late = contract(weighted[:, rows], b, ((0,), (0,)))
        send_ref[part, 0:size, :] = (state_ref[rows, :] + late).astype(bf16)
        send_ref[part, size : size + EXTRA, :] = logs_ref[part * EXTRA : (part + 1) * EXTRA, :]


def pack_logs(total, rows_ref):
    heads = total.shape[0]
    own = rows_ref.shape[0] // EXTRA
    own = heads // own
    rows_ref[...] = jnp.zeros_like(rows_ref)
    rest = total
    for piece in range(3):
        part = rest.astype(bf16).astype(f32)
        rest = rest - part
        for head in range(heads):
            at = head // own * EXTRA + head % own * 3 + piece
            rows_ref[at : at + 1, :] = part[head : head + 1, :]


def read_logs(rows, own):
    rows = rows.astype(f32)
    return [
        rows[3 * h : 3 * h + 1, :] + rows[3 * h + 1 : 3 * h + 2, :] + rows[3 * h + 2 : 3 * h + 3, :]
        for h in range(own)
    ]


def prefix_kernel(own, states_ref, send_ref, rows_ref):
    size = send_ref.shape[0] - EXTRA
    head_dim = size // own
    width = send_ref.shape[1]
    logs = [read_logs(states_ref[m, size : size + EXTRA, :], own) for m in range(GROUP)]
    for h in range(own):
        rows = slice(h * head_dim, (h + 1) * head_dim)
        state = jnp.zeros((head_dim, width), f32)
        for m in range(GROUP):
            state = jnp.exp(logs[m][h]) * state + states_ref[m, rows, :].astype(f32)
        send_ref[rows, :] = state.astype(bf16)
    total = [sum(logs[m][h] for m in range(GROUP)) for h in range(own)]
    pack_logs(jnp.concatenate(total, axis=0), rows_ref)
    send_ref[size : size + EXTRA, :] = rows_ref[...].astype(bf16)


def combine_kernel(own, states_ref, *refs):
    arrived, back_ref = refs[:-1], refs[-1]
    size = back_ref.shape[1]
    head_dim = size // own
    width = back_ref.shape[2]
    logs = [read_logs(states_ref[m, size : size + EXTRA, :], own) for m in range(GROUP)]
    jumps = [read_logs(ref[size : size + EXTRA, :], own) for ref in arrived]
    for h in range(own):
        rows = slice(h * head_dim, (h + 1) * head_dim)
        state = jnp.zeros((head_dim, width), f32)
        for ref, jump in zip(arrived, jumps):
            state = jnp.exp(jump[h]) * state + ref[rows, :].astype(f32)
        for m in range(GROUP):
            back_ref[m, rows, :] = state.astype(bf16)
            state = jnp.exp(logs[m][h]) * state + states_ref[m, rows, :].astype(f32)


def inside_kernel(normed_ref, w_gate_ref, main_ref, first_ref, dt_ref, cs_ref,
                  gate_ref, y_ref, query_ref, act_ref, scores_ref, mix_ref, weight_ref, sem):
    fetch = pltpu.make_async_copy(w_gate_ref, weight_ref, sem)
    fetch.start()
    heads, length = dt_ref.shape
    inner = gate_ref.shape[0]
    lane = lax.broadcasted_iota(jnp.int32, (EDGE, EDGE), 1)
    rest = jnp.zeros((EDGE - EXTRA, EDGE), f32)
    for at in range(0, act_ref.shape[0], EDGE):
        rows = slice(at, at + EDGE)
        first = jnp.concatenate([first_ref[:, rows], rest], axis=0).T
        kept = main_ref[rows, 0:EDGE].astype(f32)
        act_ref[rows, 0:EDGE] = jnp.where(lane < EXTRA, first, kept).astype(bf16)
        act_ref[rows, EDGE:] = main_ref[rows, EDGE:]
    head_dim = inner // heads
    state_width = (act_ref.shape[0] - inner) // 2
    query_ref[...] = act_ref[inner + state_width :, :]
    scores_ref[...] = contract(
        act_ref[inner : inner + state_width, :], act_ref[inner + state_width :, :], ((0,), (0,))
    )
    cs_col = cs_ref[...].T
    dt_col = dt_ref[...].T
    half = length // 2
    mix_ref[...] = jnp.zeros_like(mix_ref)
    later = lax.broadcasted_iota(jnp.int32, (half, half), 1)
    early = lax.broadcasted_iota(jnp.int32, (half, half), 0)
    keep = later >= early
    for h in range(heads):
        for s in (0, half):
            cs_s = jnp.broadcast_to(cs_col[s : s + half, h : h + 1], (half, half))
            dt_s = jnp.broadcast_to(dt_col[s : s + half, h : h + 1], (half, half))
            for t in range(s, length, half):
                diff = cs_ref[h : h + 1, t : t + half] - cs_s
                if s == t:
                    diff = jnp.where(keep, diff, -jnp.inf)
                mix_ref[s : s + half, t : t + half] = (
                    scores_ref[s : s + half, t : t + half] * jnp.exp(diff) * dt_s
                ).astype(bf16)
        rows = slice(h * head_dim, (h + 1) * head_dim)
        y_ref[rows, :] = jnp.dot(act_ref[rows, :], mix_ref[...], preferred_element_type=f32)
    fetch.wait()
    normed = normed_ref[...]
    for at in range(0, inner, 256):
        gate = contract(weight_ref[:, at : at + 256], normed, ((0,), (0,)))
        gate = gate.astype(bf16).astype(f32)
        gate_ref[at : at + 256, :] = gate * jax.nn.sigmoid(gate)


def output_kernel(carried_ref, query_ref, cs_ref, y_ref, gate_ref, vec_ref, w_out_ref,
                  out_ref, gated_ref, normed_ref, weight_ref, sem):
    fetch = pltpu.make_async_copy(w_out_ref, weight_ref, sem)
    fetch.start()
    heads, length = cs_ref.shape
    inner = y_ref.shape[0]
    head_dim = inner // heads
    queries = query_ref[...]
    grown = jnp.exp(cs_ref[...])
    total = jnp.zeros((1, length), f32)
    step = 2 * head_dim
    for at in range(0, inner, step):
        picked = jnp.dot(carried_ref[at : at + step, :], queries, preferred_element_type=f32)
        for h in range(at // head_dim, (at + step) // head_dim):
            rows = slice(h * head_dim, (h + 1) * head_dim)
            own = picked[h * head_dim - at : (h + 1) * head_dim - at, :]
            y = y_ref[rows, :] + grown[h : h + 1, :] * own
            gated = y * gate_ref[rows, :]
            gated_ref[rows, :] = gated
            total = total + jnp.sum(gated * gated, axis=0, keepdims=True)
    scale = lax.rsqrt(total / inner + epsilon)
    for at in range(0, inner, EDGE):
        gain = columns_of(vec_ref, at)[:, GAIN_OUT : GAIN_OUT + 1]
        normed_ref[at : at + EDGE, :] = (gated_ref[at : at + EDGE, :] * scale * gain).astype(bf16)
    fetch.wait()
    out_ref[...] = contract(normed_ref[...], weight_ref[...], ((0,), (0,))).astype(bf16)


def call(kernel, outs, scratch, *args, fetched=()):
    vmem = pl.BlockSpec(memory_space=pltpu.VMEM)
    left = pl.BlockSpec(memory_space=pl.ANY)
    single = not isinstance(outs, list)
    return pl.pallas_call(
        kernel,
        out_shape=outs,
        in_specs=[left if at in fetched else vmem for at in range(len(args))],
        out_specs=vmem if single else [vmem] * len(outs),
        scratch_shapes=scratch,
        compiler_params=pltpu.CompilerParams(vmem_limit_bytes=12 << 20),
    )(*args)


def local(
    columns,
    gaps,
    norm_in,
    w_gate,
    w_xbc,
    w_step,
    step_bias,
    conv_weight,
    conv_bias,
    rates,
    norm_out,
    w_out,
):
    length = columns.shape[1]
    depth, inner = w_gate.shape
    heads = w_step.shape[1]
    width = w_xbc.shape[1]
    state_width = (width - inner) // 2
    own = heads // GROUP
    size = inner // GROUP
    shape = jax.ShapeDtypeStruct

    rows = [conv_weight, conv_bias[None], norm_in[None], norm_out[None]]
    vec = jnp.concatenate([jnp.pad(r, ((0, 0), (0, width - r.shape[1]))) for r in rows])
    vec = jnp.pad(vec, ((0, 8 - vec.shape[0]), (0, 0)))
    head = jnp.stack([step_bias, rates], axis=1)

    whole = lax.all_to_all(columns, "table", split_axis=0, concat_axis=2, tiled=True)
    whole, w_xbc, vec, head = lax.optimization_barrier((whole, w_xbc, vec, head))
    x = whole.reshape(length, depth).T
    edge = passed_along(x[:, length - EDGE :], "seq", 1)
    normed, act, dt, cs, state, logs, first, coef_first = call(
        main_kernel,
        [
            shape((depth, length), bf16),
            shape((width, length), bf16),
            shape((heads, length), f32),
            shape((heads, length), f32),
            shape((inner, state_width), f32),
            shape((GROUP * EXTRA, state_width), bf16),
            shape((EXTRA, depth), f32),
            shape((EXTRA, inner), f32),
        ],
        [
            pltpu.VMEM((heads, length), f32),
            pltpu.VMEM((GROUP * EXTRA, state_width), f32),
            pltpu.VMEM((length, depth), bf16),
            pltpu.VMEM((EXTRA + length, width), f32),
        ],
        x, vec, w_xbc, w_step.T, head, gaps,
    )
    send, act_first = call(
        edge_kernel,
        [shape((GROUP, size + EXTRA, state_width), bf16), shape((EXTRA, width), f32)],
        [pltpu.VMEM((2 * EXTRA, width), f32)],
        edge, first, vec, w_xbc, coef_first, state, logs,
    )
    states = within_groups(send)
    total = call(
        functools.partial(prefix_kernel, own),
        shape((size + EXTRA, state_width), bf16),
        [pltpu.VMEM((EXTRA, state_width), f32)],
        states,
    )
    count = lax.axis_size("seq") // GROUP
    arrived = [passed_along(total, "seq", GROUP * step) for step in range(count - 1, 0, -1)]
    gate, y, query = call(
        inside_kernel,
        [
            shape((inner, length), f32),
            shape((inner, length), f32),
            shape((state_width, length), bf16),
        ],
        [
            pltpu.VMEM((width, length), bf16),
            pltpu.VMEM((length, length), f32),
            pltpu.VMEM((length, length), bf16),
            pltpu.VMEM((depth, inner), bf16),
            pltpu.SemaphoreType.DMA,
        ],
        normed, w_gate, act, act_first, dt, cs,
        fetched=(1,),
    )
    gate, y, *arrived = lax.optimization_barrier((gate, y, *arrived))
    back = call(
        functools.partial(combine_kernel, own),
        shape((GROUP, size, state_width), bf16),
        [],
        states, *arrived,
    )
    carried = within_groups(back).reshape(inner, state_width)
    out = call(
        output_kernel,
        shape((length, w_out.shape[1]), bf16),
        [
            pltpu.VMEM((inner, length), f32),
            pltpu.VMEM((inner, length), bf16),
            pltpu.VMEM(w_out.shape, bf16),
            pltpu.SemaphoreType.DMA,
        ],
        carried, query, cs, y, gate, vec, w_out,
        fetched=(6,),
    )
    return out[None]


def solution(mesh):
    in_specs = (
        P(None, "seq", "table"),
        P("table", "seq"),
        P(),
        P(),
        P(),
        P(),
        P(),
        P(),
        P(),
        P(),
        P(),
        P(),
    )
    out_specs = P("table", "seq", None)
    return jax.shard_map(local, mesh=mesh, in_specs=in_specs, out_specs=out_specs, check_vma=False)
```

```python
import functools

import jax
import jax.numpy as jnp
from jax import lax
from jax.experimental import pallas as pl
from jax.experimental.pallas import tpu as pltpu
from jax.sharding import PartitionSpec as P

GROUP = 8
EDGE = 128
EXTRA = 8
BIAS, GAIN_IN, GAIN_OUT = 4, 5, 6
epsilon = 1e-05
f32 = jnp.float32
bf16 = jnp.bfloat16


def passed_along(block, axis, distance, senders=None):
    devices = range(lax.axis_size(axis))
    route = [(i, i + distance) for i in senders or devices if i + distance in devices]
    return lax.ppermute(block, axis, route)


def members(*groups):
    return [g * GROUP + i for g in groups for i in range(GROUP)]


def within_groups(blocks):
    count = lax.axis_size("seq") // GROUP
    groups = [[g * GROUP + i for i in range(GROUP)] for g in range(count)]
    return lax.all_to_all(
        blocks, "seq", split_axis=0, concat_axis=0, tiled=True, axis_index_groups=groups
    )


def contract(a, b, dims):
    return lax.dot_general(a, b, (dims, ((), ())), preferred_element_type=f32)


def columns_of(vec_ref, at):
    return vec_ref[:, at : at + EDGE].T


def normed_columns(x_ref, vec_ref, out_ref):
    depth, length = x_ref.shape
    total = jnp.zeros((1, length), f32)
    for at in range(0, depth, 64):
        x = x_ref[at : at + 64, :].astype(f32)
        total = total + jnp.sum(x * x, axis=0, keepdims=True)
    scale = lax.rsqrt(total / depth + epsilon)
    for at in range(0, depth, EDGE):
        gain = columns_of(vec_ref, at)[:, GAIN_IN : GAIN_IN + 1]
        x = x_ref[at : at + EDGE, :].astype(f32)
        out_ref[at : at + EDGE, :] = (x * scale * gain).astype(bf16)


def running_sum(values):
    length = values.shape[1]
    lane = lax.broadcasted_iota(jnp.int32, values.shape, 1)
    reach = 1
    while reach < length:
        values = values + jnp.where(lane >= reach, pltpu.roll(values, reach, axis=1), 0.0)
        reach *= 2
    return values


def stage_kernel(*refs):
    count = len(refs) // 2
    sems = refs[-1]
    copies = [
        pltpu.make_async_copy(refs[at], refs[count + at], sems.at[at]) for at in range(count)
    ]
    for copy in copies:
        copy.start()
    for copy in copies:
        copy.wait()


def main_kernel(x_ref, vec_ref, w_xbc_ref, w_step_ref, head_ref, gaps_ref,
                normed_ref, act_ref, dt_ref, cs_ref, state_ref, logs_ref, first_ref, coef_first_ref,
                coef_ref, rows_ref, upright_ref, shift_ref):
    depth, length = x_ref.shape
    heads = dt_ref.shape[0]
    inner, state_width = state_ref.shape
    head_dim = inner // heads
    normed_columns(x_ref, vec_ref, normed_ref)
    first_ref[...] = x_ref[:, 0:EDGE].astype(f32).T[0:EXTRA, :]
    normed = normed_ref[...]
    raw = jnp.dot(w_step_ref[...], normed, preferred_element_type=f32)
    raw = raw + head_ref[:, 0:1]
    dt = jnp.maximum(raw, 0.0) + jnp.log1p(jnp.exp(-jnp.abs(raw)))
    dt_ref[...] = dt
    cs = running_sum(-head_ref[:, 1:2] * dt * gaps_ref[...])
    cs_ref[...] = cs
    coef = jnp.exp(cs[:, length - 1 : length] - cs) * dt
    coef_first = coef[:, 0:EDGE].T[0:EXTRA, :]
    for head in range(heads):
        coef_first_ref[:, head * head_dim : (head + 1) * head_dim] = jnp.broadcast_to(
            coef_first[:, head : head + 1], (EXTRA, head_dim)
        )
    lane = lax.broadcasted_iota(jnp.int32, coef.shape, 1)
    coef_ref[...] = jnp.where(lane >= EXTRA, coef, 0.0)
    total = jnp.broadcast_to(cs[:, length - 1 : length], (heads, state_width))
    pack_logs(total, rows_ref)
    logs_ref[...] = rows_ref[...].astype(bf16)

    for at in range(0, depth, EDGE):
        upright_ref[:, at : at + EDGE] = normed_ref[at : at + EDGE, :].astype(f32).T.astype(bf16)
    shift_ref[0:EXTRA, :] = jnp.zeros((EXTRA, shift_ref.shape[1]), f32)
    upright = upright_ref[...]

    def act_of(at, step):
        cols = slice(at, at + step)
        whole = jnp.dot(upright, w_xbc_ref[:, cols], preferred_element_type=f32)
        shift_ref[EXTRA:, cols] = whole.astype(bf16).astype(f32)
        conv = vec_ref[BIAS : BIAS + 1, cols]
        for tap in range(BIAS):
            first = EXTRA - (BIAS - 1 - tap)
            conv = conv + vec_ref[tap : tap + 1, cols] * shift_ref[first : first + length, cols]
        act = (conv * jax.nn.sigmoid(conv)).T.astype(bf16)
        act_ref[at : at + step, :] = act
        return act

    b = act_of(inner, state_width)
    act_of(inner + state_width, state_width)
    step = 2 * head_dim
    for at in range(0, inner, step):
        act = act_of(at, step).astype(f32)
        head = at // head_dim
        coef = jnp.concatenate(
            [jnp.broadcast_to(coef_ref[h : h + 1, :], (head_dim, length)) for h in (head, head + 1)],
            axis=0,
        )
        state_ref[at : at + step, :] = contract((act * coef).astype(bf16), b, ((1,), (1,)))


def edge_kernel(edge_ref, first_ref, vec_ref, w_xbc_ref, coef_ref, state_ref, logs_ref,
                send_ref, act_ref, rows_ref):
    inner, state_width = state_ref.shape
    depth = first_ref.shape[1]
    before = edge_ref[...].astype(f32).T[EDGE - EXTRA :, :]
    x = jnp.concatenate([before, first_ref[...]], axis=0)
    scale = lax.rsqrt(jnp.mean(x * x, axis=1, keepdims=True) + epsilon)
    normed = (x * scale * vec_ref[GAIN_IN : GAIN_IN + 1, :depth]).astype(bf16)
    whole = jnp.dot(normed, w_xbc_ref[...], preferred_element_type=f32)
    rows_ref[...] = whole.astype(bf16).astype(f32)
    conv = vec_ref[BIAS : BIAS + 1, :]
    for tap in range(BIAS):
        at = EXTRA - (BIAS - 1 - tap)
        conv = conv + vec_ref[tap : tap + 1, :] * rows_ref[at : at + EXTRA, :]
    act = (conv * jax.nn.sigmoid(conv)).astype(bf16).astype(f32)
    act_ref[...] = act
    weighted = (act[:, :inner] * coef_ref[...]).astype(bf16).astype(f32)
    none = jnp.zeros_like(weighted)
    weighted = jnp.concatenate([weighted, none], axis=0).astype(bf16)
    b = act[:, inner : inner + state_width]
    b = jnp.concatenate([b, jnp.zeros_like(b)], axis=0).astype(bf16)
    size = inner // GROUP
    for part in range(GROUP):
        rows = slice(part * size, (part + 1) * size)
        late = contract(weighted[:, rows], b, ((0,), (0,)))
        send_ref[part, 0:size, :] = (state_ref[rows, :] + late).astype(bf16)
        send_ref[part, size : size + EXTRA, :] = logs_ref[part * EXTRA : (part + 1) * EXTRA, :]


def pack_logs(total, rows_ref):
    heads = total.shape[0]
    own = rows_ref.shape[0] // EXTRA
    own = heads // own
    rows_ref[...] = jnp.zeros_like(rows_ref)
    rest = total
    for piece in range(3):
        part = rest.astype(bf16).astype(f32)
        rest = rest - part
        for head in range(heads):
            at = head // own * EXTRA + head % own * 3 + piece
            rows_ref[at : at + 1, :] = part[head : head + 1, :]


def read_logs(rows, own):
    rows = rows.astype(f32)
    return [
        rows[3 * h : 3 * h + 1, :] + rows[3 * h + 1 : 3 * h + 2, :] + rows[3 * h + 2 : 3 * h + 3, :]
        for h in range(own)
    ]


def prefix_kernel(own, states_ref, send_ref, rows_ref):
    size = send_ref.shape[0] - EXTRA
    head_dim = size // own
    width = send_ref.shape[1]
    logs = [read_logs(states_ref[m, size : size + EXTRA, :], own) for m in range(GROUP)]
    for h in range(own):
        rows = slice(h * head_dim, (h + 1) * head_dim)
        state = jnp.zeros((head_dim, width), f32)
        for m in range(GROUP):
            state = jnp.exp(logs[m][h]) * state + states_ref[m, rows, :].astype(f32)
        send_ref[rows, :] = state.astype(bf16)
    total = [sum(logs[m][h] for m in range(GROUP)) for h in range(own)]
    pack_logs(jnp.concatenate(total, axis=0), rows_ref)
    send_ref[size : size + EXTRA, :] = rows_ref[...].astype(bf16)


def join_kernel(own, total_ref, earlier_ref, send_ref):
    size = send_ref.shape[0]
    head_dim = size // own
    jumps = read_logs(total_ref[size : size + EXTRA, :], own)
    for h in range(own):
        rows = slice(h * head_dim, (h + 1) * head_dim)
        state = jnp.exp(jumps[h]) * earlier_ref[rows, :].astype(f32)
        send_ref[rows, :] = (total_ref[rows, :].astype(f32) + state).astype(bf16)


def combine_kernel(own, states_ref, near_ref, far_a_ref, far_b_ref, back_ref):
    size = back_ref.shape[1]
    head_dim = size // own
    logs = [read_logs(states_ref[m, size : size + EXTRA, :], own) for m in range(GROUP)]
    jumps = read_logs(near_ref[size : size + EXTRA, :], own)
    for h in range(own):
        rows = slice(h * head_dim, (h + 1) * head_dim)
        far = far_a_ref[rows, :].astype(f32) + far_b_ref[rows, :].astype(f32)
        state = near_ref[rows, :].astype(f32) + jnp.exp(jumps[h]) * far
        for m in range(GROUP):
            back_ref[m, rows, :] = state.astype(bf16)
            state = jnp.exp(logs[m][h]) * state + states_ref[m, rows, :].astype(f32)


def inside_kernel(normed_ref, w_gate_ref, main_ref, first_ref, dt_ref, cs_ref,
                  gate_ref, y_ref, query_ref, act_ref, scores_ref, mix_ref, weight_ref, sem):
    fetch = pltpu.make_async_copy(w_gate_ref, weight_ref, sem)
    fetch.start()
    heads, length = dt_ref.shape
    inner = gate_ref.shape[0]
    lane = lax.broadcasted_iota(jnp.int32, (EDGE, EDGE), 1)
    rest = jnp.zeros((EDGE - EXTRA, EDGE), f32)
    for at in range(0, act_ref.shape[0], EDGE):
        rows = slice(at, at + EDGE)
        first = jnp.concatenate([first_ref[:, rows], rest], axis=0).T
        kept = main_ref[rows, 0:EDGE].astype(f32)
        act_ref[rows, 0:EDGE] = jnp.where(lane < EXTRA, first, kept).astype(bf16)
        act_ref[rows, EDGE:] = main_ref[rows, EDGE:]
    head_dim = inner // heads
    state_width = (act_ref.shape[0] - inner) // 2
    query_ref[...] = act_ref[inner + state_width :, :]
    scores_ref[...] = contract(
        act_ref[inner : inner + state_width, :], act_ref[inner + state_width :, :], ((0,), (0,))
    )
    cs_col = cs_ref[...].T
    dt_col = dt_ref[...].T
    half = length // 2
    mix_ref[...] = jnp.zeros_like(mix_ref)
    later = lax.broadcasted_iota(jnp.int32, (half, half), 1)
    early = lax.broadcasted_iota(jnp.int32, (half, half), 0)
    keep = later >= early
    for h in range(heads):
        for s in (0, half):
            cs_s = jnp.broadcast_to(cs_col[s : s + half, h : h + 1], (half, half))
            dt_s = jnp.broadcast_to(dt_col[s : s + half, h : h + 1], (half, half))
            for t in range(s, length, half):
                diff = cs_ref[h : h + 1, t : t + half] - cs_s
                if s == t:
                    diff = jnp.where(keep, diff, -jnp.inf)
                mix_ref[s : s + half, t : t + half] = (
                    scores_ref[s : s + half, t : t + half] * jnp.exp(diff) * dt_s
                ).astype(bf16)
        rows = slice(h * head_dim, (h + 1) * head_dim)
        y_ref[rows, :] = jnp.dot(act_ref[rows, :], mix_ref[...], preferred_element_type=f32)
    fetch.wait()
    normed = normed_ref[...]
    for at in range(0, inner, 256):
        gate = contract(weight_ref[:, at : at + 256], normed, ((0,), (0,)))
        gate = gate.astype(bf16).astype(f32)
        gate_ref[at : at + 256, :] = gate * jax.nn.sigmoid(gate)


def output_kernel(carried_ref, query_ref, cs_ref, y_ref, gate_ref, vec_ref, w_out_ref,
                  out_ref, gated_ref, normed_ref, weight_ref, sem):
    fetch = pltpu.make_async_copy(w_out_ref, weight_ref, sem)
    fetch.start()
    heads, length = cs_ref.shape
    inner = y_ref.shape[0]
    head_dim = inner // heads
    queries = query_ref[...]
    grown = jnp.exp(cs_ref[...])
    total = jnp.zeros((1, length), f32)
    step = 2 * head_dim
    for at in range(0, inner, step):
        picked = jnp.dot(carried_ref[at : at + step, :], queries, preferred_element_type=f32)
        for h in range(at // head_dim, (at + step) // head_dim):
            rows = slice(h * head_dim, (h + 1) * head_dim)
            own = picked[h * head_dim - at : (h + 1) * head_dim - at, :]
            y = y_ref[rows, :] + grown[h : h + 1, :] * own
            gated = y * gate_ref[rows, :]
            gated_ref[rows, :] = gated
            total = total + jnp.sum(gated * gated, axis=0, keepdims=True)
    scale = lax.rsqrt(total / inner + epsilon)
    for at in range(0, inner, EDGE):
        gain = columns_of(vec_ref, at)[:, GAIN_OUT : GAIN_OUT + 1]
        normed_ref[at : at + EDGE, :] = (gated_ref[at : at + EDGE, :] * scale * gain).astype(bf16)
    fetch.wait()
    out_ref[...] = contract(normed_ref[...], weight_ref[...], ((0,), (0,))).astype(bf16)


def call(kernel, outs, scratch, *args, fetched=()):
    vmem = pl.BlockSpec(memory_space=pltpu.VMEM)
    left = pl.BlockSpec(memory_space=pltpu.HBM)
    single = not isinstance(outs, list)
    return pl.pallas_call(
        kernel,
        out_shape=outs,
        in_specs=[left if at in fetched else vmem for at in range(len(args))],
        out_specs=vmem if single else [vmem] * len(outs),
        scratch_shapes=scratch,
        compiler_params=pltpu.CompilerParams(vmem_limit_bytes=12 << 20),
    )(*args)


def local(
    columns,
    gaps,
    norm_in,
    w_gate,
    w_xbc,
    w_step,
    step_bias,
    conv_weight,
    conv_bias,
    rates,
    norm_out,
    w_out,
):
    length = columns.shape[1]
    depth, inner = w_gate.shape
    heads = w_step.shape[1]
    width = w_xbc.shape[1]
    state_width = (width - inner) // 2
    own = heads // GROUP
    size = inner // GROUP
    shape = jax.ShapeDtypeStruct

    rows = [conv_weight, conv_bias[None], norm_in[None], norm_out[None]]
    vec = jnp.concatenate([jnp.pad(r, ((0, 0), (0, width - r.shape[1]))) for r in rows])
    vec = jnp.pad(vec, ((0, 8 - vec.shape[0]), (0, 0)))
    head = jnp.stack([step_bias, rates], axis=1)

    whole = lax.all_to_all(columns, "table", split_axis=0, concat_axis=2, tiled=True)
    staged = [w_xbc, w_step.T, gaps]
    staged = call(
        stage_kernel,
        [shape(a.shape, a.dtype) for a in staged],
        [pltpu.SemaphoreType.DMA((len(staged),))],
        *staged,
        fetched=range(len(staged)),
    )
    whole, vec, head, *staged = lax.optimization_barrier((whole, vec, head, *staged))
    w_xbc, w_step_t, gaps = staged
    x = whole.reshape(length, depth).T
    edge = passed_along(x[:, length - EDGE :], "seq", 1)
    normed, act, dt, cs, state, logs, first, coef_first = call(
        main_kernel,
        [
            shape((depth, length), bf16),
            shape((width, length), bf16),
            shape((heads, length), f32),
            shape((heads, length), f32),
            shape((inner, state_width), f32),
            shape((GROUP * EXTRA, state_width), bf16),
            shape((EXTRA, depth), f32),
            shape((EXTRA, inner), f32),
        ],
        [
            pltpu.VMEM((heads, length), f32),
            pltpu.VMEM((GROUP * EXTRA, state_width), f32),
            pltpu.VMEM((length, depth), bf16),
            pltpu.VMEM((EXTRA + length, width), f32),
        ],
        x, vec, w_xbc, w_step_t, head, gaps,
    )
    send, act_first = call(
        edge_kernel,
        [shape((GROUP, size + EXTRA, state_width), bf16), shape((EXTRA, width), f32)],
        [pltpu.VMEM((2 * EXTRA, width), f32)],
        edge, first, vec, w_xbc, coef_first, state, logs,
    )
    states = within_groups(send)
    total = call(
        functools.partial(prefix_kernel, own),
        shape((size + EXTRA, state_width), bf16),
        [pltpu.VMEM((EXTRA, state_width), f32)],
        states,
    )
    assert lax.axis_size("seq") == 4 * GROUP
    near = passed_along(total, "seq", GROUP, members(0, 2))
    joined = call(
        functools.partial(join_kernel, own),
        shape((size, state_width), bf16),
        [],
        total, near,
    )
    far_b = passed_along(joined, "seq", 2 * GROUP, members(1))
    far_a = passed_along(joined, "seq", GROUP, members(1))
    gate, y, query = call(
        inside_kernel,
        [
            shape((inner, length), f32),
            shape((inner, length), f32),
            shape((state_width, length), bf16),
        ],
        [
            pltpu.VMEM((width, length), bf16),
            pltpu.VMEM((length, length), f32),
            pltpu.VMEM((length, length), bf16),
            pltpu.VMEM((depth, inner), bf16),
            pltpu.SemaphoreType.DMA,
        ],
        normed, w_gate, act, act_first, dt, cs,
        fetched=(1,),
    )
    gate, y, far_b, far_a = lax.optimization_barrier((gate, y, far_b, far_a))
    back = call(
        functools.partial(combine_kernel, own),
        shape((GROUP, size, state_width), bf16),
        [],
        states, near, far_a, far_b,
    )
    carried = within_groups(back).reshape(inner, state_width)
    out = call(
        output_kernel,
        shape((length, w_out.shape[1]), bf16),
        [
            pltpu.VMEM((inner, length), f32),
            pltpu.VMEM((inner, length), bf16),
            pltpu.VMEM(w_out.shape, bf16),
            pltpu.SemaphoreType.DMA,
        ],
        carried, query, cs, y, gate, vec, w_out,
        fetched=(6,),
    )
    return out[None]


def solution(mesh):
    in_specs = (
        P(None, "seq", "table"),
        P("table", "seq"),
        P(),
        P(),
        P(),
        P(),
        P(),
        P(),
        P(),
        P(),
        P(),
        P(),
    )
    out_specs = P("table", "seq", None)
    return jax.shard_map(local, mesh=mesh, in_specs=in_specs, out_specs=out_specs, check_vma=False)
```

```python
import functools

import jax
import jax.numpy as jnp
from jax import lax
from jax.experimental import pallas as pl
from jax.experimental.pallas import tpu as pltpu
from jax.sharding import PartitionSpec as P

GROUP = 8
EDGE = 128
EXTRA = 8
BIAS, GAIN_IN, GAIN_OUT = 4, 5, 6
epsilon = 1e-05
f32 = jnp.float32
bf16 = jnp.bfloat16


def passed_along(block, axis, distance, senders=None):
    devices = range(lax.axis_size(axis))
    route = [(i, i + distance) for i in senders or devices if i + distance in devices]
    return lax.ppermute(block, axis, route)


def members(*groups):
    return [g * GROUP + i for g in groups for i in range(GROUP)]


def within_groups(blocks):
    count = lax.axis_size("seq") // GROUP
    groups = [[g * GROUP + i for i in range(GROUP)] for g in range(count)]
    return lax.all_to_all(
        blocks, "seq", split_axis=0, concat_axis=0, tiled=True, axis_index_groups=groups
    )


def contract(a, b, dims):
    return lax.dot_general(a, b, (dims, ((), ())), preferred_element_type=f32)


def columns_of(vec_ref, at):
    return vec_ref[:, at : at + EDGE].T


def normed_columns(x_ref, vec_ref, out_ref):
    depth, length = x_ref.shape
    total = jnp.zeros((1, length), f32)
    for at in range(0, depth, 64):
        x = x_ref[at : at + 64, :].astype(f32)
        total = total + jnp.sum(x * x, axis=0, keepdims=True)
    scale = lax.rsqrt(total / depth + epsilon)
    for at in range(0, depth, EDGE):
        gain = columns_of(vec_ref, at)[:, GAIN_IN : GAIN_IN + 1]
        x = x_ref[at : at + EDGE, :].astype(f32)
        out_ref[at : at + EDGE, :] = (x * scale * gain).astype(bf16)


def running_sum(values):
    length = values.shape[1]
    lane = lax.broadcasted_iota(jnp.int32, values.shape, 1)
    reach = 1
    while reach < length:
        values = values + jnp.where(lane >= reach, pltpu.roll(values, reach, axis=1), 0.0)
        reach *= 2
    return values


def stage_kernel(*refs):
    count = len(refs) // 2
    sems = refs[-1]
    copies = [
        pltpu.make_async_copy(refs[at], refs[count + at], sems.at[at]) for at in range(count)
    ]
    for copy in copies:
        copy.start()
    for copy in copies:
        copy.wait()


def main_kernel(x_ref, vec_ref, w_xbc_ref, w_step_ref, head_ref, gaps_ref,
                normed_ref, act_ref, dt_ref, cs_ref, state_ref, logs_ref, first_ref, coef_first_ref,
                coef_ref, rows_ref, upright_ref, shift_ref):
    depth, length = x_ref.shape
    heads = dt_ref.shape[0]
    inner, state_width = state_ref.shape
    head_dim = inner // heads
    normed_columns(x_ref, vec_ref, normed_ref)
    first_ref[...] = x_ref[:, 0:EDGE].astype(f32).T[0:EXTRA, :]
    normed = normed_ref[...]
    raw = jnp.dot(w_step_ref[...], normed, preferred_element_type=f32)
    raw = raw + head_ref[:, 0:1]
    dt = jnp.maximum(raw, 0.0) + jnp.log1p(jnp.exp(-jnp.abs(raw)))
    dt_ref[...] = dt
    cs = running_sum(-head_ref[:, 1:2] * dt * gaps_ref[...])
    cs_ref[...] = cs
    coef = jnp.exp(cs[:, length - 1 : length] - cs) * dt
    coef_first = coef[:, 0:EDGE].T[0:EXTRA, :]
    for head in range(heads):
        coef_first_ref[:, head * head_dim : (head + 1) * head_dim] = jnp.broadcast_to(
            coef_first[:, head : head + 1], (EXTRA, head_dim)
        )
    lane = lax.broadcasted_iota(jnp.int32, coef.shape, 1)
    coef_ref[...] = jnp.where(lane >= EXTRA, coef, 0.0)
    total = jnp.broadcast_to(cs[:, length - 1 : length], (heads, state_width))
    pack_logs(total, rows_ref)
    logs_ref[...] = rows_ref[...].astype(bf16)

    for at in range(0, depth, EDGE):
        upright_ref[:, at : at + EDGE] = normed_ref[at : at + EDGE, :].astype(f32).T.astype(bf16)
    shift_ref[0:EXTRA, :] = jnp.zeros((EXTRA, shift_ref.shape[1]), f32)
    upright = upright_ref[...]

    def act_of(at, step):
        cols = slice(at, at + step)
        whole = jnp.dot(upright, w_xbc_ref[:, cols], preferred_element_type=f32)
        shift_ref[EXTRA:, cols] = whole.astype(bf16).astype(f32)
        conv = vec_ref[BIAS : BIAS + 1, cols]
        for tap in range(BIAS):
            first = EXTRA - (BIAS - 1 - tap)
            conv = conv + vec_ref[tap : tap + 1, cols] * shift_ref[first : first + length, cols]
        act = (conv * jax.nn.sigmoid(conv)).T.astype(bf16)
        act_ref[at : at + step, :] = act
        return act

    b = act_of(inner, state_width)
    act_of(inner + state_width, state_width)
    step = 2 * head_dim
    for at in range(0, inner, step):
        act = act_of(at, step).astype(f32)
        head = at // head_dim
        coef = jnp.concatenate(
            [jnp.broadcast_to(coef_ref[h : h + 1, :], (head_dim, length)) for h in (head, head + 1)],
            axis=0,
        )
        state_ref[at : at + step, :] = contract((act * coef).astype(bf16), b, ((1,), (1,)))


def edge_kernel(edge_ref, first_ref, vec_ref, w_xbc_ref, coef_ref, state_ref, logs_ref,
                send_ref, act_ref, rows_ref):
    inner, state_width = state_ref.shape
    depth = first_ref.shape[1]
    before = edge_ref[...].astype(f32).T[EDGE - EXTRA :, :]
    x = jnp.concatenate([before, first_ref[...]], axis=0)
    scale = lax.rsqrt(jnp.mean(x * x, axis=1, keepdims=True) + epsilon)
    normed = (x * scale * vec_ref[GAIN_IN : GAIN_IN + 1, :depth]).astype(bf16)
    whole = jnp.dot(normed, w_xbc_ref[...], preferred_element_type=f32)
    rows_ref[...] = whole.astype(bf16).astype(f32)
    conv = vec_ref[BIAS : BIAS + 1, :]
    for tap in range(BIAS):
        at = EXTRA - (BIAS - 1 - tap)
        conv = conv + vec_ref[tap : tap + 1, :] * rows_ref[at : at + EXTRA, :]
    act = (conv * jax.nn.sigmoid(conv)).astype(bf16).astype(f32)
    act_ref[...] = act
    weighted = (act[:, :inner] * coef_ref[...]).astype(bf16).astype(f32)
    none = jnp.zeros_like(weighted)
    weighted = jnp.concatenate([weighted, none], axis=0).astype(bf16)
    b = act[:, inner : inner + state_width]
    b = jnp.concatenate([b, jnp.zeros_like(b)], axis=0).astype(bf16)
    size = inner // GROUP
    for part in range(GROUP):
        rows = slice(part * size, (part + 1) * size)
        late = contract(weighted[:, rows], b, ((0,), (0,)))
        send_ref[part, 0:size, :] = (state_ref[rows, :] + late).astype(bf16)
        send_ref[part, size : size + EXTRA, :] = logs_ref[part * EXTRA : (part + 1) * EXTRA, :]


def pack_logs(total, rows_ref):
    heads = total.shape[0]
    own = rows_ref.shape[0] // EXTRA
    own = heads // own
    rows_ref[...] = jnp.zeros_like(rows_ref)
    rest = total
    for piece in range(3):
        part = rest.astype(bf16).astype(f32)
        rest = rest - part
        for head in range(heads):
            at = head // own * EXTRA + head % own * 3 + piece
            rows_ref[at : at + 1, :] = part[head : head + 1, :]


def read_logs(rows, own):
    rows = rows.astype(f32)
    return [
        rows[3 * h : 3 * h + 1, :] + rows[3 * h + 1 : 3 * h + 2, :] + rows[3 * h + 2 : 3 * h + 3, :]
        for h in range(own)
    ]


def prefix_kernel(own, states_ref, send_ref, rows_ref):
    size = send_ref.shape[0] - EXTRA
    head_dim = size // own
    width = send_ref.shape[1]
    logs = [read_logs(states_ref[m, size : size + EXTRA, :], own) for m in range(GROUP)]
    for h in range(own):
        rows = slice(h * head_dim, (h + 1) * head_dim)
        state = jnp.zeros((head_dim, width), f32)
        for m in range(GROUP):
            state = jnp.exp(logs[m][h]) * state + states_ref[m, rows, :].astype(f32)
        send_ref[rows, :] = state.astype(bf16)
    total = [sum(logs[m][h] for m in range(GROUP)) for h in range(own)]
    pack_logs(jnp.concatenate(total, axis=0), rows_ref)
    send_ref[size : size + EXTRA, :] = rows_ref[...].astype(bf16)


def join_kernel(own, total_ref, earlier_ref, send_ref):
    size = send_ref.shape[0]
    head_dim = size // own
    jumps = read_logs(total_ref[size : size + EXTRA, :], own)
    for h in range(own):
        rows = slice(h * head_dim, (h + 1) * head_dim)
        state = jnp.exp(jumps[h]) * earlier_ref[rows, :].astype(f32)
        send_ref[rows, :] = (total_ref[rows, :].astype(f32) + state).astype(bf16)


def combine_kernel(own, states_ref, *refs):
    arrived, back_ref = refs[:-1], refs[-1]
    size = back_ref.shape[1]
    head_dim = size // own
    logs = [read_logs(states_ref[m, size : size + EXTRA, :], own) for m in range(GROUP)]
    for h in range(own):
        rows = slice(h * head_dim, (h + 1) * head_dim)
        state = sum(ref[rows, :].astype(f32) for ref in arrived)
        for m in range(GROUP):
            back_ref[m, rows, :] = state.astype(bf16)
            state = jnp.exp(logs[m][h]) * state + states_ref[m, rows, :].astype(f32)


def inside_kernel(normed_ref, w_gate_ref, main_ref, first_ref, dt_ref, cs_ref,
                  gate_ref, y_ref, query_ref, act_ref, scores_ref, mix_ref, weight_ref, sem):
    fetch = pltpu.make_async_copy(w_gate_ref, weight_ref, sem)
    fetch.start()
    heads, length = dt_ref.shape
    inner = gate_ref.shape[0]
    lane = lax.broadcasted_iota(jnp.int32, (EDGE, EDGE), 1)
    rest = jnp.zeros((EDGE - EXTRA, EDGE), f32)
    for at in range(0, act_ref.shape[0], EDGE):
        rows = slice(at, at + EDGE)
        first = jnp.concatenate([first_ref[:, rows], rest], axis=0).T
        kept = main_ref[rows, 0:EDGE].astype(f32)
        act_ref[rows, 0:EDGE] = jnp.where(lane < EXTRA, first, kept).astype(bf16)
        act_ref[rows, EDGE:] = main_ref[rows, EDGE:]
    head_dim = inner // heads
    state_width = (act_ref.shape[0] - inner) // 2
    query_ref[...] = act_ref[inner + state_width :, :]
    scores_ref[...] = contract(
        act_ref[inner : inner + state_width, :], act_ref[inner + state_width :, :], ((0,), (0,))
    )
    cs_col = cs_ref[...].T
    dt_col = dt_ref[...].T
    half = length // 2
    mix_ref[...] = jnp.zeros_like(mix_ref)
    later = lax.broadcasted_iota(jnp.int32, (half, half), 1)
    early = lax.broadcasted_iota(jnp.int32, (half, half), 0)
    keep = later >= early
    for h in range(heads):
        for s in (0, half):
            cs_s = jnp.broadcast_to(cs_col[s : s + half, h : h + 1], (half, half))
            dt_s = jnp.broadcast_to(dt_col[s : s + half, h : h + 1], (half, half))
            for t in range(s, length, half):
                diff = cs_ref[h : h + 1, t : t + half] - cs_s
                if s == t:
                    diff = jnp.where(keep, diff, -jnp.inf)
                mix_ref[s : s + half, t : t + half] = (
                    scores_ref[s : s + half, t : t + half] * jnp.exp(diff) * dt_s
                ).astype(bf16)
        rows = slice(h * head_dim, (h + 1) * head_dim)
        y_ref[rows, :] = jnp.dot(act_ref[rows, :], mix_ref[...], preferred_element_type=f32)
    fetch.wait()
    normed = normed_ref[...]
    for at in range(0, inner, 256):
        gate = contract(weight_ref[:, at : at + 256], normed, ((0,), (0,)))
        gate_ref[at : at + 256, :] = gate.astype(bf16)


def output_kernel(carried_ref, query_ref, cs_ref, y_ref, gate_ref, vec_ref, w_out_ref,
                  out_ref, gated_ref, normed_ref, weight_ref, sem):
    fetch = pltpu.make_async_copy(w_out_ref, weight_ref, sem)
    fetch.start()
    heads, length = cs_ref.shape
    inner = y_ref.shape[0]
    head_dim = inner // heads
    queries = query_ref[...]
    grown = jnp.exp(cs_ref[...])
    total = jnp.zeros((1, length), f32)
    step = 2 * head_dim
    for at in range(0, inner, step):
        picked = jnp.dot(carried_ref[at : at + step, :], queries, preferred_element_type=f32)
        for h in range(at // head_dim, (at + step) // head_dim):
            rows = slice(h * head_dim, (h + 1) * head_dim)
            own = picked[h * head_dim - at : (h + 1) * head_dim - at, :]
            y = y_ref[rows, :] + grown[h : h + 1, :] * own
            gate = gate_ref[rows, :].astype(f32)
            gated = y * (gate * jax.nn.sigmoid(gate))
            gated_ref[rows, :] = gated
            total = total + jnp.sum(gated * gated, axis=0, keepdims=True)
    scale = lax.rsqrt(total / inner + epsilon)
    for at in range(0, inner, EDGE):
        gain = columns_of(vec_ref, at)[:, GAIN_OUT : GAIN_OUT + 1]
        normed_ref[at : at + EDGE, :] = (gated_ref[at : at + EDGE, :] * scale * gain).astype(bf16)
    fetch.wait()
    out_ref[...] = contract(normed_ref[...], weight_ref[...], ((0,), (0,))).astype(bf16)


def call(kernel, outs, scratch, *args, fetched=()):
    vmem = pl.BlockSpec(memory_space=pltpu.VMEM)
    left = pl.BlockSpec(memory_space=pltpu.HBM)
    single = not isinstance(outs, list)
    return pl.pallas_call(
        kernel,
        out_shape=outs,
        in_specs=[left if at in fetched else vmem for at in range(len(args))],
        out_specs=vmem if single else [vmem] * len(outs),
        scratch_shapes=scratch,
        compiler_params=pltpu.CompilerParams(vmem_limit_bytes=12 << 20),
    )(*args)


def local(
    columns,
    gaps,
    norm_in,
    w_gate,
    w_xbc,
    w_step,
    step_bias,
    conv_weight,
    conv_bias,
    rates,
    norm_out,
    w_out,
):
    length = columns.shape[1]
    depth, inner = w_gate.shape
    heads = w_step.shape[1]
    width = w_xbc.shape[1]
    state_width = (width - inner) // 2
    own = heads // GROUP
    size = inner // GROUP
    shape = jax.ShapeDtypeStruct

    rows = [conv_weight, conv_bias[None], norm_in[None], norm_out[None]]
    vec = jnp.concatenate([jnp.pad(r, ((0, 0), (0, width - r.shape[1]))) for r in rows])
    vec = jnp.pad(vec, ((0, 8 - vec.shape[0]), (0, 0)))
    head = jnp.stack([step_bias, rates], axis=1)

    whole = lax.all_to_all(columns, "table", split_axis=0, concat_axis=2, tiled=True)
    staged = [w_xbc, w_step.T, gaps]
    staged = call(
        stage_kernel,
        [shape(a.shape, a.dtype) for a in staged],
        [pltpu.SemaphoreType.DMA((len(staged),))],
        *staged,
        fetched=range(len(staged)),
    )
    whole, vec, head, *staged = lax.optimization_barrier((whole, vec, head, *staged))
    w_xbc, w_step_t, gaps = staged
    x = whole.reshape(length, depth).T
    edge = passed_along(x[:, length - EDGE :], "seq", 1)
    normed, act, dt, cs, state, logs, first, coef_first = call(
        main_kernel,
        [
            shape((depth, length), bf16),
            shape((width, length), bf16),
            shape((heads, length), f32),
            shape((heads, length), f32),
            shape((inner, state_width), f32),
            shape((GROUP * EXTRA, state_width), bf16),
            shape((EXTRA, depth), f32),
            shape((EXTRA, inner), f32),
        ],
        [
            pltpu.VMEM((heads, length), f32),
            pltpu.VMEM((GROUP * EXTRA, state_width), f32),
            pltpu.VMEM((length, depth), bf16),
            pltpu.VMEM((EXTRA + length, width), f32),
        ],
        x, vec, w_xbc, w_step_t, head, gaps,
    )
    send, act_first = call(
        edge_kernel,
        [shape((GROUP, size + EXTRA, state_width), bf16), shape((EXTRA, width), f32)],
        [pltpu.VMEM((2 * EXTRA, width), f32)],
        edge, first, vec, w_xbc, coef_first, state, logs,
    )
    states = within_groups(send)
    gate, y, query = call(
        inside_kernel,
        [
            shape((inner, length), bf16),
            shape((inner, length), f32),
            shape((state_width, length), bf16),
        ],
        [
            pltpu.VMEM((width, length), bf16),
            pltpu.VMEM((length, length), f32),
            pltpu.VMEM((length, length), bf16),
            pltpu.VMEM((depth, inner), bf16),
            pltpu.SemaphoreType.DMA,
        ],
        normed, w_gate, act, act_first, dt, cs,
        fetched=(1,),
    )
    total = call(
        functools.partial(prefix_kernel, own),
        shape((size + EXTRA, state_width), bf16),
        [pltpu.VMEM((EXTRA, state_width), f32)],
        states,
    )
    send = total[:size]
    arrived = []
    for group in range(lax.axis_size("seq") // GROUP - 1):
        if group:
            send = call(
                functools.partial(join_kernel, own),
                shape((size, state_width), bf16),
                [],
                total, arrived[-1],
            )
        arrived.append(passed_along(send, "seq", GROUP, members(group)))
        if not group:
            arrived[0], gate, y, query = lax.optimization_barrier((arrived[0], gate, y, query))
    back = call(
        functools.partial(combine_kernel, own),
        shape((GROUP, size, state_width), bf16),
        [],
        states, *arrived,
    )
    carried = within_groups(back).reshape(inner, state_width)
    out = call(
        output_kernel,
        shape((length, w_out.shape[1]), bf16),
        [
            pltpu.VMEM((inner, length), f32),
            pltpu.VMEM((inner, length), bf16),
            pltpu.VMEM(w_out.shape, bf16),
            pltpu.SemaphoreType.DMA,
        ],
        carried, query, cs, y, gate, vec, w_out,
        fetched=(6,),
    )
    return out[None]


def solution(mesh):
    in_specs = (
        P(None, "seq", "table"),
        P("table", "seq"),
        P(),
        P(),
        P(),
        P(),
        P(),
        P(),
        P(),
        P(),
        P(),
        P(),
    )
    out_specs = P("table", "seq", None)
    return jax.shard_map(local, mesh=mesh, in_specs=in_specs, out_specs=out_specs, check_vma=False)
```

```python
import functools

import jax
import jax.numpy as jnp
from jax import lax
from jax.experimental import pallas as pl
from jax.experimental.pallas import tpu as pltpu
from jax.sharding import PartitionSpec as P

GROUP = 8
EDGE = 128
EXTRA = 8
BIAS, GAIN_IN, GAIN_OUT = 4, 5, 6
epsilon = 1e-05
f32 = jnp.float32
bf16 = jnp.bfloat16


def passed_along(block, axis, distance, senders=None):
    devices = range(lax.axis_size(axis))
    route = [(i, i + distance) for i in senders or devices if i + distance in devices]
    return lax.ppermute(block, axis, route)


def members(*groups):
    return [g * GROUP + i for g in groups for i in range(GROUP)]


def within_groups(blocks):
    count = lax.axis_size("seq") // GROUP
    groups = [[g * GROUP + i for i in range(GROUP)] for g in range(count)]
    return lax.all_to_all(
        blocks, "seq", split_axis=0, concat_axis=0, tiled=True, axis_index_groups=groups
    )


def contract(a, b, dims):
    return lax.dot_general(a, b, (dims, ((), ())), preferred_element_type=f32)


def columns_of(vec_ref, at):
    return vec_ref[:, at : at + EDGE].T


def normed_columns(x_ref, vec_ref, out_ref):
    depth, length = x_ref.shape
    total = jnp.zeros((1, length), f32)
    for at in range(0, depth, 64):
        x = x_ref[at : at + 64, :].astype(f32)
        total = total + jnp.sum(x * x, axis=0, keepdims=True)
    scale = lax.rsqrt(total / depth + epsilon)
    for at in range(0, depth, EDGE):
        gain = columns_of(vec_ref, at)[:, GAIN_IN : GAIN_IN + 1]
        x = x_ref[at : at + EDGE, :].astype(f32)
        out_ref[at : at + EDGE, :] = (x * scale * gain).astype(bf16)


def running_sum(values):
    length = values.shape[1]
    lane = lax.broadcasted_iota(jnp.int32, values.shape, 1)
    reach = 1
    while reach < length:
        values = values + jnp.where(lane >= reach, pltpu.roll(values, reach, axis=1), 0.0)
        reach *= 2
    return values


def stage_kernel(*refs):
    count = len(refs) // 2
    sems = refs[-1]
    copies = [
        pltpu.make_async_copy(refs[at], refs[count + at], sems.at[at]) for at in range(count)
    ]
    for copy in copies:
        copy.start()
    for copy in copies:
        copy.wait()


def main_kernel(x_ref, vec_ref, w_xbc_ref, w_step_ref, head_ref, gaps_ref,
                normed_ref, act_ref, dt_ref, cs_ref, state_ref, logs_ref, first_ref, coef_first_ref,
                coef_ref, rows_ref, upright_ref, shift_ref):
    depth, length = x_ref.shape
    heads = dt_ref.shape[0]
    inner, state_width = state_ref.shape
    head_dim = inner // heads
    normed_columns(x_ref, vec_ref, normed_ref)
    first_ref[...] = x_ref[:, 0:EDGE].astype(f32).T[0:EXTRA, :]
    normed = normed_ref[...]
    raw = jnp.dot(w_step_ref[...], normed, preferred_element_type=f32)
    raw = raw + head_ref[:, 0:1]
    dt = jnp.maximum(raw, 0.0) + jnp.log1p(jnp.exp(-jnp.abs(raw)))
    dt_ref[...] = dt
    cs = running_sum(-head_ref[:, 1:2] * dt * gaps_ref[...])
    cs_ref[...] = cs
    coef = jnp.exp(cs[:, length - 1 : length] - cs) * dt
    coef_first = coef[:, 0:EDGE].T[0:EXTRA, :]
    for head in range(heads):
        coef_first_ref[:, head * head_dim : (head + 1) * head_dim] = jnp.broadcast_to(
            coef_first[:, head : head + 1], (EXTRA, head_dim)
        )
    lane = lax.broadcasted_iota(jnp.int32, coef.shape, 1)
    coef_ref[...] = jnp.where(lane >= EXTRA, coef, 0.0)
    total = jnp.broadcast_to(cs[:, length - 1 : length], (heads, state_width))
    pack_logs(total, rows_ref)
    logs_ref[...] = rows_ref[...].astype(bf16)

    for at in range(0, depth, EDGE):
        upright_ref[:, at : at + EDGE] = normed_ref[at : at + EDGE, :].astype(f32).T.astype(bf16)
    shift_ref[0:EXTRA, :] = jnp.zeros((EXTRA, shift_ref.shape[1]), f32)
    upright = upright_ref[...]

    def act_of(at, step):
        cols = slice(at, at + step)
        whole = jnp.dot(upright, w_xbc_ref[:, cols], preferred_element_type=f32)
        shift_ref[EXTRA:, cols] = whole.astype(bf16).astype(f32)
        conv = vec_ref[BIAS : BIAS + 1, cols]
        for tap in range(BIAS):
            first = EXTRA - (BIAS - 1 - tap)
            conv = conv + vec_ref[tap : tap + 1, cols] * shift_ref[first : first + length, cols]
        act = (conv * jax.nn.sigmoid(conv)).T.astype(bf16)
        act_ref[at : at + step, :] = act
        return act

    b = act_of(inner, state_width)
    act_of(inner + state_width, state_width)
    step = 2 * head_dim
    for at in range(0, inner, step):
        act = act_of(at, step).astype(f32)
        head = at // head_dim
        coef = jnp.concatenate(
            [jnp.broadcast_to(coef_ref[h : h + 1, :], (head_dim, length)) for h in (head, head + 1)],
            axis=0,
        )
        state_ref[at : at + step, :] = contract((act * coef).astype(bf16), b, ((1,), (1,)))


def edge_kernel(edge_ref, first_ref, vec_ref, w_xbc_ref, coef_ref, state_ref, logs_ref,
                send_ref, act_ref, rows_ref):
    inner, state_width = state_ref.shape
    depth = first_ref.shape[1]
    before = edge_ref[...].astype(f32).T[EDGE - EXTRA :, :]
    x = jnp.concatenate([before, first_ref[...]], axis=0)
    scale = lax.rsqrt(jnp.mean(x * x, axis=1, keepdims=True) + epsilon)
    normed = (x * scale * vec_ref[GAIN_IN : GAIN_IN + 1, :depth]).astype(bf16)
    whole = jnp.dot(normed, w_xbc_ref[...], preferred_element_type=f32)
    rows_ref[...] = whole.astype(bf16).astype(f32)
    conv = vec_ref[BIAS : BIAS + 1, :]
    for tap in range(BIAS):
        at = EXTRA - (BIAS - 1 - tap)
        conv = conv + vec_ref[tap : tap + 1, :] * rows_ref[at : at + EXTRA, :]
    act = (conv * jax.nn.sigmoid(conv)).astype(bf16).astype(f32)
    act_ref[...] = act
    weighted = (act[:, :inner] * coef_ref[...]).astype(bf16).astype(f32)
    none = jnp.zeros_like(weighted)
    weighted = jnp.concatenate([weighted, none], axis=0).astype(bf16)
    b = act[:, inner : inner + state_width]
    b = jnp.concatenate([b, jnp.zeros_like(b)], axis=0).astype(bf16)
    size = inner // GROUP
    for part in range(GROUP):
        rows = slice(part * size, (part + 1) * size)
        late = contract(weighted[:, rows], b, ((0,), (0,)))
        send_ref[part, 0:size, :] = (state_ref[rows, :] + late).astype(bf16)
        send_ref[part, size : size + EXTRA, :] = logs_ref[part * EXTRA : (part + 1) * EXTRA, :]


def pack_logs(total, rows_ref):
    heads = total.shape[0]
    own = rows_ref.shape[0] // EXTRA
    own = heads // own
    rows_ref[...] = jnp.zeros_like(rows_ref)
    rest = total
    for piece in range(3):
        part = rest.astype(bf16).astype(f32)
        rest = rest - part
        for head in range(heads):
            at = head // own * EXTRA + head % own * 3 + piece
            rows_ref[at : at + 1, :] = part[head : head + 1, :]


def read_logs(rows, own):
    rows = rows.astype(f32)
    return [
        rows[3 * h : 3 * h + 1, :] + rows[3 * h + 1 : 3 * h + 2, :] + rows[3 * h + 2 : 3 * h + 3, :]
        for h in range(own)
    ]


def prefix_kernel(own, states_ref, send_ref, rows_ref):
    size = send_ref.shape[0] - EXTRA
    head_dim = size // own
    width = send_ref.shape[1]
    logs = [read_logs(states_ref[m, size : size + EXTRA, :], own) for m in range(GROUP)]
    for h in range(own):
        rows = slice(h * head_dim, (h + 1) * head_dim)
        state = jnp.zeros((head_dim, width), f32)
        for m in range(GROUP):
            state = jnp.exp(logs[m][h]) * state + states_ref[m, rows, :].astype(f32)
        send_ref[rows, :] = state.astype(bf16)
    total = [sum(logs[m][h] for m in range(GROUP)) for h in range(own)]
    pack_logs(jnp.concatenate(total, axis=0), rows_ref)
    send_ref[size : size + EXTRA, :] = rows_ref[...].astype(bf16)


def join_kernel(own, total_ref, earlier_ref, send_ref):
    size = send_ref.shape[0] - EXTRA
    head_dim = size // own
    send_ref[size:, :] = jnp.zeros((EXTRA, send_ref.shape[1]), bf16)
    jumps = read_logs(total_ref[size : size + EXTRA, :], own)
    for h in range(own):
        rows = slice(h * head_dim, (h + 1) * head_dim)
        state = jnp.exp(jumps[h]) * earlier_ref[rows, :].astype(f32)
        send_ref[rows, :] = (total_ref[rows, :].astype(f32) + state).astype(bf16)


def combine_kernel(own, states_ref, near_ref, far_b_ref, far_a_ref, first_ref, back_ref):
    size = back_ref.shape[1]
    head_dim = size // own
    logs = [read_logs(states_ref[m, size : size + EXTRA, :], own) for m in range(GROUP)]
    jumps = read_logs(near_ref[size : size + EXTRA, :], own)
    for h in range(own):
        rows = slice(h * head_dim, (h + 1) * head_dim)
        far = far_a_ref[rows, :].astype(f32) + far_b_ref[rows, :].astype(f32)
        close = first_ref[rows, :].astype(f32) + near_ref[rows, :].astype(f32)
        state = close + jnp.exp(jumps[h]) * far
        for m in range(GROUP):
            back_ref[m, rows, :] = state.astype(bf16)
            state = jnp.exp(logs[m][h]) * state + states_ref[m, rows, :].astype(f32)


def inside_kernel(normed_ref, w_gate_ref, main_ref, first_ref, dt_ref, cs_ref,
                  gate_ref, y_ref, query_ref, act_ref, scores_ref, mix_ref, weight_ref, sem):
    fetch = pltpu.make_async_copy(w_gate_ref, weight_ref, sem)
    fetch.start()
    heads, length = dt_ref.shape
    inner = gate_ref.shape[0]
    lane = lax.broadcasted_iota(jnp.int32, (EDGE, EDGE), 1)
    rest = jnp.zeros((EDGE - EXTRA, EDGE), f32)
    for at in range(0, act_ref.shape[0], EDGE):
        rows = slice(at, at + EDGE)
        first = jnp.concatenate([first_ref[:, rows], rest], axis=0).T
        kept = main_ref[rows, 0:EDGE].astype(f32)
        act_ref[rows, 0:EDGE] = jnp.where(lane < EXTRA, first, kept).astype(bf16)
        act_ref[rows, EDGE:] = main_ref[rows, EDGE:]
    head_dim = inner // heads
    state_width = (act_ref.shape[0] - inner) // 2
    query_ref[...] = act_ref[inner + state_width :, :]
    scores_ref[...] = contract(
        act_ref[inner : inner + state_width, :], act_ref[inner + state_width :, :], ((0,), (0,))
    )
    cs_col = cs_ref[...].T
    dt_col = dt_ref[...].T
    half = length // 2
    mix_ref[...] = jnp.zeros_like(mix_ref)
    later = lax.broadcasted_iota(jnp.int32, (half, half), 1)
    early = lax.broadcasted_iota(jnp.int32, (half, half), 0)
    keep = later >= early
    for h in range(heads):
        for s in (0, half):
            cs_s = jnp.broadcast_to(cs_col[s : s + half, h : h + 1], (half, half))
            dt_s = jnp.broadcast_to(dt_col[s : s + half, h : h + 1], (half, half))
            for t in range(s, length, half):
                diff = cs_ref[h : h + 1, t : t + half] - cs_s
                if s == t:
                    diff = jnp.where(keep, diff, -jnp.inf)
                mix_ref[s : s + half, t : t + half] = (
                    scores_ref[s : s + half, t : t + half] * jnp.exp(diff) * dt_s
                ).astype(bf16)
        rows = slice(h * head_dim, (h + 1) * head_dim)
        y_ref[rows, :] = jnp.dot(act_ref[rows, :], mix_ref[...], preferred_element_type=f32)
    fetch.wait()
    normed = normed_ref[...]
    for at in range(0, inner, 256):
        gate = contract(weight_ref[:, at : at + 256], normed, ((0,), (0,)))
        gate_ref[at : at + 256, :] = gate.astype(bf16)


def output_kernel(carried_ref, query_ref, cs_ref, y_ref, gate_ref, vec_ref, w_out_ref,
                  out_ref, gated_ref, normed_ref, weight_ref, sem):
    fetch = pltpu.make_async_copy(w_out_ref, weight_ref, sem)
    fetch.start()
    heads, length = cs_ref.shape
    inner = y_ref.shape[0]
    head_dim = inner // heads
    queries = query_ref[...]
    grown = jnp.exp(cs_ref[...])
    total = jnp.zeros((1, length), f32)
    step = 2 * head_dim
    for at in range(0, inner, step):
        picked = jnp.dot(carried_ref[at : at + step, :], queries, preferred_element_type=f32)
        for h in range(at // head_dim, (at + step) // head_dim):
            rows = slice(h * head_dim, (h + 1) * head_dim)
            own = picked[h * head_dim - at : (h + 1) * head_dim - at, :]
            y = y_ref[rows, :] + grown[h : h + 1, :] * own
            gate = gate_ref[rows, :].astype(f32)
            gated = y * (gate * jax.nn.sigmoid(gate))
            gated_ref[rows, :] = gated
            total = total + jnp.sum(gated * gated, axis=0, keepdims=True)
    scale = lax.rsqrt(total / inner + epsilon)
    for at in range(0, inner, EDGE):
        gain = columns_of(vec_ref, at)[:, GAIN_OUT : GAIN_OUT + 1]
        normed_ref[at : at + EDGE, :] = (gated_ref[at : at + EDGE, :] * scale * gain).astype(bf16)
    fetch.wait()
    out_ref[...] = contract(normed_ref[...], weight_ref[...], ((0,), (0,))).astype(bf16)


def call(kernel, outs, scratch, *args, fetched=()):
    vmem = pl.BlockSpec(memory_space=pltpu.VMEM)
    left = pl.BlockSpec(memory_space=pltpu.HBM)
    single = not isinstance(outs, list)
    return pl.pallas_call(
        kernel,
        out_shape=outs,
        in_specs=[left if at in fetched else vmem for at in range(len(args))],
        out_specs=vmem if single else [vmem] * len(outs),
        scratch_shapes=scratch,
        compiler_params=pltpu.CompilerParams(vmem_limit_bytes=12 << 20),
    )(*args)


def local(
    columns,
    gaps,
    norm_in,
    w_gate,
    w_xbc,
    w_step,
    step_bias,
    conv_weight,
    conv_bias,
    rates,
    norm_out,
    w_out,
):
    length = columns.shape[1]
    depth, inner = w_gate.shape
    heads = w_step.shape[1]
    width = w_xbc.shape[1]
    state_width = (width - inner) // 2
    own = heads // GROUP
    size = inner // GROUP
    shape = jax.ShapeDtypeStruct

    rows = [conv_weight, conv_bias[None], norm_in[None], norm_out[None]]
    vec = jnp.concatenate([jnp.pad(r, ((0, 0), (0, width - r.shape[1]))) for r in rows])
    vec = jnp.pad(vec, ((0, 8 - vec.shape[0]), (0, 0)))
    head = jnp.stack([step_bias, rates], axis=1)

    whole = lax.all_to_all(columns, "table", split_axis=0, concat_axis=2, tiled=True)
    staged = [w_xbc, w_step.T, gaps]
    staged = call(
        stage_kernel,
        [shape(a.shape, a.dtype) for a in staged],
        [pltpu.SemaphoreType.DMA((len(staged),))],
        *staged,
        fetched=range(len(staged)),
    )
    whole, vec, head, *staged = lax.optimization_barrier((whole, vec, head, *staged))
    w_xbc, w_step_t, gaps = staged
    x = whole.reshape(length, depth).T
    edge = passed_along(x[:, length - EDGE :], "seq", 1)
    normed, act, dt, cs, state, logs, first, coef_first = call(
        main_kernel,
        [
            shape((depth, length), bf16),
            shape((width, length), bf16),
            shape((heads, length), f32),
            shape((heads, length), f32),
            shape((inner, state_width), f32),
            shape((GROUP * EXTRA, state_width), bf16),
            shape((EXTRA, depth), f32),
            shape((EXTRA, inner), f32),
        ],
        [
            pltpu.VMEM((heads, length), f32),
            pltpu.VMEM((GROUP * EXTRA, state_width), f32),
            pltpu.VMEM((length, depth), bf16),
            pltpu.VMEM((EXTRA + length, width), f32),
        ],
        x, vec, w_xbc, w_step_t, head, gaps,
    )
    send, act_first = call(
        edge_kernel,
        [shape((GROUP, size + EXTRA, state_width), bf16), shape((EXTRA, width), f32)],
        [pltpu.VMEM((2 * EXTRA, width), f32)],
        edge, first, vec, w_xbc, coef_first, state, logs,
    )
    states = within_groups(send)
    total = call(
        functools.partial(prefix_kernel, own),
        shape((size + EXTRA, state_width), bf16),
        [pltpu.VMEM((EXTRA, state_width), f32)],
        states,
    )
    assert lax.axis_size("seq") == 4 * GROUP
    first = passed_along(total, "seq", GROUP, members(0))
    joined = call(
        functools.partial(join_kernel, own),
        shape((size + EXTRA, state_width), bf16),
        [],
        total, first,
    )
    joined, act = lax.optimization_barrier((joined, act))
    far_a = passed_along(joined, "seq", GROUP, members(1))
    far_b = passed_along(joined, "seq", 2 * GROUP, members(1))
    gate, y, query = call(
        inside_kernel,
        [
            shape((inner, length), bf16),
            shape((inner, length), f32),
            shape((state_width, length), bf16),
        ],
        [
            pltpu.VMEM((width, length), bf16),
            pltpu.VMEM((length, length), f32),
            pltpu.VMEM((length, length), bf16),
            pltpu.VMEM((depth, inner), bf16),
            pltpu.SemaphoreType.DMA,
        ],
        normed, w_gate, act, act_first, dt, cs,
        fetched=(1,),
    )
    total, gate, y = lax.optimization_barrier((total, gate, y))
    near = passed_along(total, "seq", GROUP, members(2))
    back = call(
        functools.partial(combine_kernel, own),
        shape((GROUP, size, state_width), bf16),
        [],
        states, near, far_b, far_a, first,
    )
    carried = within_groups(back).reshape(inner, state_width)
    out = call(
        output_kernel,
        shape((length, w_out.shape[1]), bf16),
        [
            pltpu.VMEM((inner, length), f32),
            pltpu.VMEM((inner, length), bf16),
            pltpu.VMEM(w_out.shape, bf16),
            pltpu.SemaphoreType.DMA,
        ],
        carried, query, cs, y, gate, vec, w_out,
        fetched=(6,),
    )
    return out[None]


def solution(mesh):
    in_specs = (
        P(None, "seq", "table"),
        P("table", "seq"),
        P(),
        P(),
        P(),
        P(),
        P(),
        P(),
        P(),
        P(),
        P(),
        P(),
    )
    out_specs = P("table", "seq", None)
    return jax.shard_map(local, mesh=mesh, in_specs=in_specs, out_specs=out_specs, check_vma=False)
```

```python
import functools

import jax
import jax.numpy as jnp
from jax import lax
from jax.experimental import pallas as pl
from jax.experimental.pallas import tpu as pltpu
from jax.sharding import PartitionSpec as P

GROUP = 8
EDGE = 128
EXTRA = 8
BIAS, GAIN_IN, GAIN_OUT = 4, 5, 6
epsilon = 1e-05
f32 = jnp.float32
bf16 = jnp.bfloat16


def passed_along(block, axis, distance, senders=None):
    devices = range(lax.axis_size(axis))
    route = [(i, i + distance) for i in senders or devices if i + distance in devices]
    return lax.ppermute(block, axis, route)


def members(*groups):
    return [g * GROUP + i for g in groups for i in range(GROUP)]


def within_groups(blocks):
    count = lax.axis_size("seq") // GROUP
    groups = [[g * GROUP + i for i in range(GROUP)] for g in range(count)]
    return lax.all_to_all(
        blocks, "seq", split_axis=0, concat_axis=0, tiled=True, axis_index_groups=groups
    )


def contract(a, b, dims):
    return lax.dot_general(a, b, (dims, ((), ())), preferred_element_type=f32)


def columns_of(vec_ref, at):
    return vec_ref[:, at : at + EDGE].T


def normed_columns(x_ref, vec_ref, out_ref):
    depth, length = x_ref.shape
    total = jnp.zeros((1, length), f32)
    for at in range(0, depth, 64):
        x = x_ref[at : at + 64, :].astype(f32)
        total = total + jnp.sum(x * x, axis=0, keepdims=True)
    scale = lax.rsqrt(total / depth + epsilon)
    for at in range(0, depth, EDGE):
        gain = columns_of(vec_ref, at)[:, GAIN_IN : GAIN_IN + 1]
        x = x_ref[at : at + EDGE, :].astype(f32)
        out_ref[at : at + EDGE, :] = (x * scale * gain).astype(bf16)


def running_sum(values):
    length = values.shape[1]
    lane = lax.broadcasted_iota(jnp.int32, values.shape, 1)
    reach = 1
    while reach < length:
        values = values + jnp.where(lane >= reach, pltpu.roll(values, reach, axis=1), 0.0)
        reach *= 2
    return values


def stage_kernel(*refs):
    count = len(refs) // 2
    sems = refs[-1]
    copies = [
        pltpu.make_async_copy(refs[at], refs[count + at], sems.at[at]) for at in range(count)
    ]
    for copy in copies:
        copy.start()
    for copy in copies:
        copy.wait()


def main_kernel(x_ref, vec_ref, w_xbc_ref, w_step_ref, head_ref, gaps_ref,
                normed_ref, act_ref, dt_ref, cs_ref, state_ref, logs_ref, first_ref, coef_first_ref,
                coef_ref, rows_ref, upright_ref, shift_ref):
    depth, length = x_ref.shape
    heads = dt_ref.shape[0]
    inner, state_width = state_ref.shape
    head_dim = inner // heads
    normed_columns(x_ref, vec_ref, normed_ref)
    first_ref[...] = x_ref[:, 0:EDGE].astype(f32).T[0:EXTRA, :]
    normed = normed_ref[...]
    raw = jnp.dot(w_step_ref[...], normed, preferred_element_type=f32)
    raw = raw + head_ref[:, 0:1]
    dt = jnp.maximum(raw, 0.0) + jnp.log1p(jnp.exp(-jnp.abs(raw)))
    dt_ref[...] = dt
    cs = running_sum(-head_ref[:, 1:2] * dt * gaps_ref[...])
    cs_ref[...] = cs
    coef = jnp.exp(cs[:, length - 1 : length] - cs) * dt
    coef_first = coef[:, 0:EDGE].T[0:EXTRA, :]
    for head in range(heads):
        coef_first_ref[:, head * head_dim : (head + 1) * head_dim] = jnp.broadcast_to(
            coef_first[:, head : head + 1], (EXTRA, head_dim)
        )
    lane = lax.broadcasted_iota(jnp.int32, coef.shape, 1)
    coef_ref[...] = jnp.where(lane >= EXTRA, coef, 0.0)
    total = jnp.broadcast_to(cs[:, length - 1 : length], (heads, state_width))
    pack_logs(total, rows_ref)
    logs_ref[...] = rows_ref[...].astype(bf16)

    for at in range(0, depth, EDGE):
        upright_ref[:, at : at + EDGE] = normed_ref[at : at + EDGE, :].astype(f32).T.astype(bf16)
    shift_ref[0:EXTRA, :] = jnp.zeros((EXTRA, shift_ref.shape[1]), f32)
    upright = upright_ref[...]

    def act_of(at, step):
        cols = slice(at, at + step)
        whole = jnp.dot(upright, w_xbc_ref[:, cols], preferred_element_type=f32)
        shift_ref[EXTRA:, cols] = whole.astype(bf16).astype(f32)
        conv = vec_ref[BIAS : BIAS + 1, cols]
        for tap in range(BIAS):
            first = EXTRA - (BIAS - 1 - tap)
            conv = conv + vec_ref[tap : tap + 1, cols] * shift_ref[first : first + length, cols]
        act = (conv * jax.nn.sigmoid(conv)).T.astype(bf16)
        act_ref[at : at + step, :] = act
        return act

    b = act_of(inner, state_width)
    act_of(inner + state_width, state_width)
    step = 2 * head_dim
    for at in range(0, inner, step):
        act = act_of(at, step).astype(f32)
        head = at // head_dim
        coef = jnp.concatenate(
            [jnp.broadcast_to(coef_ref[h : h + 1, :], (head_dim, length)) for h in (head, head + 1)],
            axis=0,
        )
        state_ref[at : at + step, :] = contract((act * coef).astype(bf16), b, ((1,), (1,)))


def edge_kernel(edge_ref, first_ref, vec_ref, w_xbc_ref, coef_ref, state_ref, logs_ref,
                send_ref, act_ref, rows_ref):
    inner, state_width = state_ref.shape
    depth = first_ref.shape[1]
    before = edge_ref[...].astype(f32).T[EDGE - EXTRA :, :]
    x = jnp.concatenate([before, first_ref[...]], axis=0)
    scale = lax.rsqrt(jnp.mean(x * x, axis=1, keepdims=True) + epsilon)
    normed = (x * scale * vec_ref[GAIN_IN : GAIN_IN + 1, :depth]).astype(bf16)
    whole = jnp.dot(normed, w_xbc_ref[...], preferred_element_type=f32)
    rows_ref[...] = whole.astype(bf16).astype(f32)
    conv = vec_ref[BIAS : BIAS + 1, :]
    for tap in range(BIAS):
        at = EXTRA - (BIAS - 1 - tap)
        conv = conv + vec_ref[tap : tap + 1, :] * rows_ref[at : at + EXTRA, :]
    act = (conv * jax.nn.sigmoid(conv)).astype(bf16).astype(f32)
    act_ref[...] = act
    weighted = (act[:, :inner] * coef_ref[...]).astype(bf16).astype(f32)
    none = jnp.zeros_like(weighted)
    weighted = jnp.concatenate([weighted, none], axis=0).astype(bf16)
    b = act[:, inner : inner + state_width]
    b = jnp.concatenate([b, jnp.zeros_like(b)], axis=0).astype(bf16)
    size = inner // GROUP
    for part in range(GROUP):
        rows = slice(part * size, (part + 1) * size)
        late = contract(weighted[:, rows], b, ((0,), (0,)))
        send_ref[part, 0:size, :] = (state_ref[rows, :] + late).astype(bf16)
        send_ref[part, size : size + EXTRA, :] = logs_ref[part * EXTRA : (part + 1) * EXTRA, :]


def pack_logs(total, rows_ref):
    heads = total.shape[0]
    own = rows_ref.shape[0] // EXTRA
    own = heads // own
    rows_ref[...] = jnp.zeros_like(rows_ref)
    rest = total
    for piece in range(3):
        part = rest.astype(bf16).astype(f32)
        rest = rest - part
        for head in range(heads):
            at = head // own * EXTRA + head % own * 3 + piece
            rows_ref[at : at + 1, :] = part[head : head + 1, :]


def read_logs(rows, own):
    rows = rows.astype(f32)
    return [
        rows[3 * h : 3 * h + 1, :] + rows[3 * h + 1 : 3 * h + 2, :] + rows[3 * h + 2 : 3 * h + 3, :]
        for h in range(own)
    ]


def prefix_kernel(own, states_ref, send_ref, rows_ref):
    size = send_ref.shape[0] - EXTRA
    head_dim = size // own
    width = send_ref.shape[1]
    logs = [read_logs(states_ref[m, size : size + EXTRA, :], own) for m in range(GROUP)]
    for h in range(own):
        rows = slice(h * head_dim, (h + 1) * head_dim)
        state = jnp.zeros((head_dim, width), f32)
        for m in range(GROUP):
            state = jnp.exp(logs[m][h]) * state + states_ref[m, rows, :].astype(f32)
        send_ref[rows, :] = state.astype(bf16)
    total = [sum(logs[m][h] for m in range(GROUP)) for h in range(own)]
    pack_logs(jnp.concatenate(total, axis=0), rows_ref)
    send_ref[size : size + EXTRA, :] = rows_ref[...].astype(bf16)


def join_kernel(own, total_ref, earlier_ref, send_ref, same_ref):
    size = send_ref.shape[0] - EXTRA
    head_dim = size // own
    jumps = read_logs(total_ref[size:, :], own)
    for h in range(own):
        rows = slice(h * head_dim, (h + 1) * head_dim)
        state = jnp.exp(jumps[h]) * earlier_ref[rows, :].astype(f32)
        send_ref[rows, :] = (total_ref[rows, :].astype(f32) + state).astype(bf16)
    send_ref[size:, :] = jnp.zeros((EXTRA, send_ref.shape[1]), bf16)
    same_ref[...] = total_ref[...]


def combine_kernel(own, states_ref, *refs):
    *whole, near_ref, middle_ref, far_ref, back_ref = refs
    size = back_ref.shape[1]
    head_dim = size // own
    logs = [read_logs(states_ref[m, size : size + EXTRA, :], own) for m in range(GROUP)]
    near_jumps = read_logs(near_ref[size:, :], own)
    middle_jumps = read_logs(middle_ref[size:, :], own)
    for h in range(own):
        rows = slice(h * head_dim, (h + 1) * head_dim)
        state = middle_ref[rows, :].astype(f32)
        state = state + jnp.exp(middle_jumps[h]) * far_ref[rows, :].astype(f32)
        state = near_ref[rows, :].astype(f32) + jnp.exp(near_jumps[h]) * state
        for ref in whole:
            state = state + ref[rows, :].astype(f32)
        for m in range(GROUP):
            back_ref[m, rows, :] = state.astype(bf16)
            state = jnp.exp(logs[m][h]) * state + states_ref[m, rows, :].astype(f32)


def inside_kernel(normed_ref, w_gate_ref, main_ref, first_ref, dt_ref, cs_ref,
                  gate_ref, y_ref, query_ref, act_ref, scores_ref, mix_ref, weight_ref, sem):
    fetch = pltpu.make_async_copy(w_gate_ref, weight_ref, sem)
    fetch.start()
    heads, length = dt_ref.shape
    inner = gate_ref.shape[0]
    lane = lax.broadcasted_iota(jnp.int32, (EDGE, EDGE), 1)
    rest = jnp.zeros((EDGE - EXTRA, EDGE), f32)
    for at in range(0, act_ref.shape[0], EDGE):
        rows = slice(at, at + EDGE)
        first = jnp.concatenate([first_ref[:, rows], rest], axis=0).T
        kept = main_ref[rows, 0:EDGE].astype(f32)
        act_ref[rows, 0:EDGE] = jnp.where(lane < EXTRA, first, kept).astype(bf16)
        act_ref[rows, EDGE:] = main_ref[rows, EDGE:]
    head_dim = inner // heads
    state_width = (act_ref.shape[0] - inner) // 2
    query_ref[...] = act_ref[inner + state_width :, :]
    scores_ref[...] = contract(
        act_ref[inner : inner + state_width, :], act_ref[inner + state_width :, :], ((0,), (0,))
    )
    cs_col = cs_ref[...].T
    dt_col = dt_ref[...].T
    half = length // 2
    mix_ref[...] = jnp.zeros_like(mix_ref)
    later = lax.broadcasted_iota(jnp.int32, (half, half), 1)
    early = lax.broadcasted_iota(jnp.int32, (half, half), 0)
    keep = later >= early
    for h in range(heads):
        for s in (0, half):
            cs_s = jnp.broadcast_to(cs_col[s : s + half, h : h + 1], (half, half))
            dt_s = jnp.broadcast_to(dt_col[s : s + half, h : h + 1], (half, half))
            for t in range(s, length, half):
                diff = cs_ref[h : h + 1, t : t + half] - cs_s
                if s == t:
                    diff = jnp.where(keep, diff, -jnp.inf)
                mix_ref[s : s + half, t : t + half] = (
                    scores_ref[s : s + half, t : t + half] * jnp.exp(diff) * dt_s
                ).astype(bf16)
        rows = slice(h * head_dim, (h + 1) * head_dim)
        y_ref[rows, :] = jnp.dot(act_ref[rows, :], mix_ref[...], preferred_element_type=f32)
    fetch.wait()
    normed = normed_ref[...]
    for at in range(0, inner, 256):
        gate = contract(weight_ref[:, at : at + 256], normed, ((0,), (0,)))
        gate_ref[at : at + 256, :] = gate.astype(bf16)


def output_kernel(carried_ref, query_ref, cs_ref, y_ref, gate_ref, vec_ref, w_out_ref,
                  out_ref, gated_ref, normed_ref, weight_ref, sem):
    fetch = pltpu.make_async_copy(w_out_ref, weight_ref, sem)
    fetch.start()
    heads, length = cs_ref.shape
    inner = y_ref.shape[0]
    head_dim = inner // heads
    queries = query_ref[...]
    grown = jnp.exp(cs_ref[...])
    total = jnp.zeros((1, length), f32)
    step = 2 * head_dim
    for at in range(0, inner, step):
        picked = jnp.dot(carried_ref[at : at + step, :], queries, preferred_element_type=f32)
        for h in range(at // head_dim, (at + step) // head_dim):
            rows = slice(h * head_dim, (h + 1) * head_dim)
            own = picked[h * head_dim - at : (h + 1) * head_dim - at, :]
            y = y_ref[rows, :] + grown[h : h + 1, :] * own
            gate = gate_ref[rows, :].astype(f32)
            gated = y * (gate * jax.nn.sigmoid(gate))
            gated_ref[rows, :] = gated
            total = total + jnp.sum(gated * gated, axis=0, keepdims=True)
    scale = lax.rsqrt(total / inner + epsilon)
    for at in range(0, inner, EDGE):
        gain = columns_of(vec_ref, at)[:, GAIN_OUT : GAIN_OUT + 1]
        normed_ref[at : at + EDGE, :] = (gated_ref[at : at + EDGE, :] * scale * gain).astype(bf16)
    fetch.wait()
    out_ref[...] = contract(normed_ref[...], weight_ref[...], ((0,), (0,))).astype(bf16)


def call(kernel, outs, scratch, *args, fetched=()):
    vmem = pl.BlockSpec(memory_space=pltpu.VMEM)
    left = pl.BlockSpec(memory_space=pltpu.HBM)
    single = not isinstance(outs, list)
    args = [
        pltpu.with_memory_space_constraint(a, pltpu.HBM) if at in fetched else a
        for at, a in enumerate(args)
    ]
    return pl.pallas_call(
        kernel,
        out_shape=outs,
        in_specs=[left if at in fetched else vmem for at in range(len(args))],
        out_specs=vmem if single else [vmem] * len(outs),
        scratch_shapes=scratch,
        compiler_params=pltpu.CompilerParams(vmem_limit_bytes=12 << 20),
    )(*args)


def local(
    columns,
    gaps,
    norm_in,
    w_gate,
    w_xbc,
    w_step,
    step_bias,
    conv_weight,
    conv_bias,
    rates,
    norm_out,
    w_out,
):
    length = columns.shape[1]
    depth, inner = w_gate.shape
    heads = w_step.shape[1]
    width = w_xbc.shape[1]
    state_width = (width - inner) // 2
    own = heads // GROUP
    size = inner // GROUP
    shape = jax.ShapeDtypeStruct

    rows = [conv_weight, conv_bias[None], norm_in[None], norm_out[None]]
    vec = jnp.concatenate([jnp.pad(r, ((0, 0), (0, width - r.shape[1]))) for r in rows])
    vec = jnp.pad(vec, ((0, 8 - vec.shape[0]), (0, 0)))
    head = jnp.stack([step_bias, rates], axis=1)

    whole = lax.all_to_all(columns, "table", split_axis=0, concat_axis=2, tiled=True)
    staged = [w_xbc, w_step.T, gaps]
    staged = call(
        stage_kernel,
        [shape(a.shape, a.dtype) for a in staged],
        [pltpu.SemaphoreType.DMA((len(staged),))],
        *staged,
        fetched=range(len(staged)),
    )
    whole, vec, head, *staged = lax.optimization_barrier((whole, vec, head, *staged))
    w_xbc, w_step_t, gaps = staged
    x = whole.reshape(length, depth).T
    edge = passed_along(x[:, length - EDGE :], "seq", 1)
    normed, act, dt, cs, state, logs, first, coef_first = call(
        main_kernel,
        [
            shape((depth, length), bf16),
            shape((width, length), bf16),
            shape((heads, length), f32),
            shape((heads, length), f32),
            shape((inner, state_width), f32),
            shape((GROUP * EXTRA, state_width), bf16),
            shape((EXTRA, depth), f32),
            shape((EXTRA, inner), f32),
        ],
        [
            pltpu.VMEM((heads, length), f32),
            pltpu.VMEM((GROUP * EXTRA, state_width), f32),
            pltpu.VMEM((length, depth), bf16),
            pltpu.VMEM((EXTRA + length, width), f32),
        ],
        x, vec, w_xbc, w_step_t, head, gaps,
    )
    send, act_first = call(
        edge_kernel,
        [shape((GROUP, size + EXTRA, state_width), bf16), shape((EXTRA, width), f32)],
        [pltpu.VMEM((2 * EXTRA, width), f32)],
        edge, first, vec, w_xbc, coef_first, state, logs,
    )
    states = within_groups(send)
    total = call(
        functools.partial(prefix_kernel, own),
        shape((size + EXTRA, state_width), bf16),
        [pltpu.VMEM((EXTRA, state_width), f32)],
        states,
    )
    assert lax.axis_size("seq") == 4 * GROUP
    first = passed_along(total, "seq", GROUP, members(0))
    middle = passed_along(total, "seq", 2 * GROUP, members(1))
    far = passed_along(total, "seq", 3 * GROUP, members(0))
    joined, same = call(
        functools.partial(join_kernel, own),
        [shape((size + EXTRA, state_width), bf16)] * 2,
        [],
        total, first,
    )
    after = passed_along(joined, "seq", GROUP, members(1))
    near = passed_along(same, "seq", GROUP, members(2))
    back = call(
        functools.partial(combine_kernel, own),
        shape((GROUP, size, state_width), bf16),
        [],
        states, first, after, near, middle, far,
    )
    back, act = lax.optimization_barrier((back, act))
    carried = within_groups(back).reshape(inner, state_width)
    gate, y, query = call(
        inside_kernel,
        [
            shape((inner, length), bf16),
            shape((inner, length), f32),
            shape((state_width, length), bf16),
        ],
        [
            pltpu.VMEM((width, length), bf16),
            pltpu.VMEM((length, length), f32),
            pltpu.VMEM((length, length), bf16),
            pltpu.VMEM((depth, inner), bf16),
            pltpu.SemaphoreType.DMA,
        ],
        normed, w_gate, act, act_first, dt, cs,
        fetched=(1,),
    )
    out = call(
        output_kernel,
        shape((length, w_out.shape[1]), bf16),
        [
            pltpu.VMEM((inner, length), f32),
            pltpu.VMEM((inner, length), bf16),
            pltpu.VMEM(w_out.shape, bf16),
            pltpu.SemaphoreType.DMA,
        ],
        carried, query, cs, y, gate, vec, w_out,
        fetched=(6,),
    )
    return out[None]


def solution(mesh):
    in_specs = (
        P(None, "seq", "table"),
        P("table", "seq"),
        P(),
        P(),
        P(),
        P(),
        P(),
        P(),
        P(),
        P(),
        P(),
        P(),
    )
    out_specs = P("table", "seq", None)
    return jax.shard_map(local, mesh=mesh, in_specs=in_specs, out_specs=out_specs, check_vma=False)
```

```python
import functools

import jax
import jax.numpy as jnp
from jax import lax
from jax.experimental import pallas as pl
from jax.experimental.pallas import tpu as pltpu
from jax.sharding import PartitionSpec as P

GROUP = 8
EDGE = 128
EXTRA = 8
PARTS = 4
BIAS, GAIN_IN, GAIN_OUT = 4, 5, 6
epsilon = 1e-05
f32 = jnp.float32
bf16 = jnp.bfloat16


def passed_along(block, axis, distance, senders=None):
    devices = range(lax.axis_size(axis))
    route = [(i, i + distance) for i in senders or devices if i + distance in devices]
    return lax.ppermute(block, axis, route)


def members(*groups):
    return [g * GROUP + i for g in groups for i in range(GROUP)]


def within_groups(blocks):
    count = lax.axis_size("seq") // GROUP
    groups = [[g * GROUP + i for i in range(GROUP)] for g in range(count)]
    return lax.all_to_all(
        blocks, "seq", split_axis=0, concat_axis=0, tiled=True, axis_index_groups=groups
    )


def fetch_rows(source, target, sems):
    count = sems.shape[0]
    step = source.shape[0] // count
    copies = [
        pltpu.make_async_copy(
            source.at[at * step : (at + 1) * step], target.at[at * step : (at + 1) * step], sems.at[at]
        )
        for at in range(count)
    ]
    for copy in copies:
        copy.start()
    return copies


def contract(a, b, dims):
    return lax.dot_general(a, b, (dims, ((), ())), preferred_element_type=f32)


def columns_of(vec_ref, at):
    return vec_ref[:, at : at + EDGE].T


def normed_columns(x_ref, vec_ref, out_ref):
    depth, length = x_ref.shape
    total = jnp.zeros((1, length), f32)
    for at in range(0, depth, 64):
        x = x_ref[at : at + 64, :].astype(f32)
        total = total + jnp.sum(x * x, axis=0, keepdims=True)
    scale = lax.rsqrt(total / depth + epsilon)
    for at in range(0, depth, EDGE):
        gain = columns_of(vec_ref, at)[:, GAIN_IN : GAIN_IN + 1]
        x = x_ref[at : at + EDGE, :].astype(f32)
        out_ref[at : at + EDGE, :] = (x * scale * gain).astype(bf16)


def running_sum(values):
    length = values.shape[1]
    lane = lax.broadcasted_iota(jnp.int32, values.shape, 1)
    reach = 1
    while reach < length:
        values = values + jnp.where(lane >= reach, pltpu.roll(values, reach, axis=1), 0.0)
        reach *= 2
    return values


def stage_kernel(*refs):
    count = len(refs) // 2
    sems = refs[-1]
    copies = [
        pltpu.make_async_copy(refs[at], refs[count + at], sems.at[at]) for at in range(count)
    ]
    for copy in copies:
        copy.start()
    for copy in copies:
        copy.wait()


def main_kernel(x_ref, vec_ref, w_xbc_ref, w_step_ref, head_ref, gaps_ref,
                normed_ref, act_ref, dt_ref, cs_ref, state_ref, logs_ref, first_ref, coef_first_ref,
                coef_ref, rows_ref, upright_ref, shift_ref):
    depth, length = x_ref.shape
    heads = dt_ref.shape[0]
    inner, state_width = state_ref.shape
    head_dim = inner // heads
    normed_columns(x_ref, vec_ref, normed_ref)
    normed = normed_ref[...]
    raw = jnp.dot(w_step_ref[...], normed, preferred_element_type=f32)
    raw = raw + head_ref[:, 0:1]
    dt = jnp.maximum(raw, 0.0) + jnp.log1p(jnp.exp(-jnp.abs(raw)))
    dt_ref[...] = dt
    cs = running_sum(-head_ref[:, 1:2] * dt * gaps_ref[...])
    cs_ref[...] = cs
    coef = jnp.exp(cs[:, length - 1 : length] - cs) * dt
    coef_first = coef[:, 0:EDGE].T[0:EXTRA, :]
    for head in range(heads):
        coef_first_ref[:, head * head_dim : (head + 1) * head_dim] = jnp.broadcast_to(
            coef_first[:, head : head + 1], (EXTRA, head_dim)
        )
    lane = lax.broadcasted_iota(jnp.int32, coef.shape, 1)
    coef_ref[...] = jnp.where(lane >= EXTRA, coef, 0.0)
    total = jnp.broadcast_to(cs[:, length - 1 : length], (heads, state_width))
    pack_logs(total, rows_ref)
    logs_ref[...] = rows_ref[...].astype(bf16)

    for at in range(0, depth, EDGE):
        upright_ref[:, at : at + EDGE] = normed_ref[at : at + EDGE, :].astype(f32).T.astype(bf16)
    shift_ref[0:EXTRA, :] = jnp.zeros((EXTRA, shift_ref.shape[1]), f32)
    upright = upright_ref[...]

    def act_of(at, step):
        cols = slice(at, at + step)
        whole = jnp.dot(upright, w_xbc_ref[:, cols], preferred_element_type=f32)
        shift_ref[EXTRA:, cols] = whole.astype(bf16).astype(f32)
        conv = vec_ref[BIAS : BIAS + 1, cols]
        for tap in range(BIAS):
            first = EXTRA - (BIAS - 1 - tap)
            conv = conv + vec_ref[tap : tap + 1, cols] * shift_ref[first : first + length, cols]
        act = (conv * jax.nn.sigmoid(conv)).T.astype(bf16)
        act_ref[at : at + step, :] = act
        return act

    b = act_of(inner, state_width)
    act_of(inner + state_width, state_width)
    step = 2 * head_dim
    for at in range(0, inner, step):
        act = act_of(at, step).astype(f32)
        head = at // head_dim
        coef = jnp.concatenate(
            [jnp.broadcast_to(coef_ref[h : h + 1, :], (head_dim, length)) for h in (head, head + 1)],
            axis=0,
        )
        state_ref[at : at + step, :] = contract((act * coef).astype(bf16), b, ((1,), (1,)))
    first_ref[...] = shift_ref[EXTRA : 2 * EXTRA, :]


def edge_kernel(edge_ref, first_ref, vec_ref, w_xbc_ref, coef_ref, state_ref, logs_ref,
                send_ref, act_ref, rows_ref):
    inner, state_width = state_ref.shape
    depth = edge_ref.shape[0]
    x = edge_ref[...].astype(f32).T[EDGE - EXTRA :, :]
    scale = lax.rsqrt(jnp.mean(x * x, axis=1, keepdims=True) + epsilon)
    normed = (x * scale * vec_ref[GAIN_IN : GAIN_IN + 1, :depth]).astype(bf16)
    before = jnp.dot(normed, w_xbc_ref[...], preferred_element_type=f32)
    rows_ref[0:EXTRA, :] = before.astype(bf16).astype(f32)
    rows_ref[EXTRA:, :] = first_ref[...]
    conv = vec_ref[BIAS : BIAS + 1, :]
    for tap in range(BIAS):
        at = EXTRA - (BIAS - 1 - tap)
        conv = conv + vec_ref[tap : tap + 1, :] * rows_ref[at : at + EXTRA, :]
    act = (conv * jax.nn.sigmoid(conv)).astype(bf16).astype(f32)
    act_ref[...] = act
    weighted = (act[:, :inner] * coef_ref[...]).astype(bf16).astype(f32)
    none = jnp.zeros_like(weighted)
    weighted = jnp.concatenate([weighted, none], axis=0).astype(bf16)
    b = act[:, inner : inner + state_width]
    b = jnp.concatenate([b, jnp.zeros_like(b)], axis=0).astype(bf16)
    size = inner // GROUP
    for part in range(GROUP):
        rows = slice(part * size, (part + 1) * size)
        late = contract(weighted[:, rows], b, ((0,), (0,)))
        send_ref[part, 0:size, :] = (state_ref[rows, :] + late).astype(bf16)
        send_ref[part, size : size + EXTRA, :] = logs_ref[part * EXTRA : (part + 1) * EXTRA, :]


def pack_logs(total, rows_ref):
    heads = total.shape[0]
    own = rows_ref.shape[0] // EXTRA
    own = heads // own
    rows_ref[...] = jnp.zeros_like(rows_ref)
    rest = total
    for piece in range(3):
        part = rest.astype(bf16).astype(f32)
        rest = rest - part
        for head in range(heads):
            at = head // own * EXTRA + head % own * 3 + piece
            rows_ref[at : at + 1, :] = part[head : head + 1, :]


def read_logs(rows, own):
    rows = rows.astype(f32)
    return [
        rows[3 * h : 3 * h + 1, :] + rows[3 * h + 1 : 3 * h + 2, :] + rows[3 * h + 2 : 3 * h + 3, :]
        for h in range(own)
    ]


def prefix_kernel(own, states_ref, send_ref, rows_ref):
    size = send_ref.shape[0] - EXTRA
    head_dim = size // own
    width = send_ref.shape[1]
    logs = [read_logs(states_ref[m, size : size + EXTRA, :], own) for m in range(GROUP)]
    for h in range(own):
        rows = slice(h * head_dim, (h + 1) * head_dim)
        state = jnp.zeros((head_dim, width), f32)
        for m in range(GROUP):
            state = jnp.exp(logs[m][h]) * state + states_ref[m, rows, :].astype(f32)
        send_ref[rows, :] = state.astype(bf16)
    total = [sum(logs[m][h] for m in range(GROUP)) for h in range(own)]
    pack_logs(jnp.concatenate(total, axis=0), rows_ref)
    send_ref[size : size + EXTRA, :] = rows_ref[...].astype(bf16)


def join_kernel(own, total_ref, earlier_ref, send_ref, same_ref):
    size = send_ref.shape[0] - EXTRA
    head_dim = size // own
    jumps = read_logs(total_ref[size:, :], own)
    for h in range(own):
        rows = slice(h * head_dim, (h + 1) * head_dim)
        state = jnp.exp(jumps[h]) * earlier_ref[rows, :].astype(f32)
        send_ref[rows, :] = (total_ref[rows, :].astype(f32) + state).astype(bf16)
    send_ref[size:, :] = jnp.zeros((EXTRA, send_ref.shape[1]), bf16)
    same_ref[...] = total_ref[...]


def combine_kernel(own, states_ref, *refs):
    *whole, near_ref, middle_ref, far_ref, back_ref = refs
    size = back_ref.shape[1]
    head_dim = size // own
    logs = [read_logs(states_ref[m, size : size + EXTRA, :], own) for m in range(GROUP)]
    near_jumps = read_logs(near_ref[size:, :], own)
    middle_jumps = read_logs(middle_ref[size:, :], own)
    for h in range(own):
        rows = slice(h * head_dim, (h + 1) * head_dim)
        state = middle_ref[rows, :].astype(f32)
        state = state + jnp.exp(middle_jumps[h]) * far_ref[rows, :].astype(f32)
        state = near_ref[rows, :].astype(f32) + jnp.exp(near_jumps[h]) * state
        for ref in whole:
            state = state + ref[rows, :].astype(f32)
        for m in range(GROUP):
            back_ref[m, rows, :] = state.astype(bf16)
            state = jnp.exp(logs[m][h]) * state + states_ref[m, rows, :].astype(f32)


def inside_kernel(normed_ref, w_gate_ref, main_ref, first_ref, dt_ref, cs_ref,
                  grown_ref, y_ref, query_ref, act_ref, scores_ref, mix_ref, weight_ref, sem):
    fetches = fetch_rows(w_gate_ref, weight_ref, sem)
    heads, length = dt_ref.shape
    inner = y_ref.shape[0]
    lane = lax.broadcasted_iota(jnp.int32, (EDGE, EDGE), 1)
    rest = jnp.zeros((EDGE - EXTRA, EDGE), f32)
    for at in range(0, act_ref.shape[0], EDGE):
        rows = slice(at, at + EDGE)
        first = jnp.concatenate([first_ref[:, rows], rest], axis=0).T
        kept = main_ref[rows, 0:EDGE].astype(f32)
        act_ref[rows, 0:EDGE] = jnp.where(lane < EXTRA, first, kept).astype(bf16)
        act_ref[rows, EDGE:] = main_ref[rows, EDGE:]
    head_dim = inner // heads
    state_width = (act_ref.shape[0] - inner) // 2
    query_ref[...] = act_ref[inner + state_width :, :]
    scores_ref[...] = contract(
        act_ref[inner : inner + state_width, :], act_ref[inner + state_width :, :], ((0,), (0,))
    )
    cs_col = cs_ref[...].T
    dt_col = dt_ref[...].T
    half = length // 2
    mix_ref[...] = jnp.zeros_like(mix_ref)
    later = lax.broadcasted_iota(jnp.int32, (half, half), 1)
    early = lax.broadcasted_iota(jnp.int32, (half, half), 0)
    keep = later >= early
    for h in range(heads):
        for s in (0, half):
            cs_s = jnp.broadcast_to(cs_col[s : s + half, h : h + 1], (half, half))
            dt_s = jnp.broadcast_to(dt_col[s : s + half, h : h + 1], (half, half))
            for t in range(s, length, half):
                diff = cs_ref[h : h + 1, t : t + half] - cs_s
                if s == t:
                    diff = jnp.where(keep, diff, -jnp.inf)
                mix_ref[s : s + half, t : t + half] = (
                    scores_ref[s : s + half, t : t + half] * jnp.exp(diff) * dt_s
                ).astype(bf16)
        rows = slice(h * head_dim, (h + 1) * head_dim)
        y_ref[rows, :] = jnp.dot(act_ref[rows, :], mix_ref[...], preferred_element_type=f32)
    for fetch in fetches:
        fetch.wait()
    normed = normed_ref[...]
    step = 4 * head_dim
    for at in range(0, inner, step):
        gate = contract(weight_ref[:, at : at + step], normed, ((0,), (0,)))
        gate = gate.astype(bf16).astype(f32)
        gate = gate * jax.nn.sigmoid(gate)
        for h in range(at // head_dim, (at + step) // head_dim):
            rows = slice(h * head_dim, (h + 1) * head_dim)
            own = gate[h * head_dim - at : (h + 1) * head_dim - at, :]
            grown_ref[rows, :] = jnp.exp(cs_ref[h : h + 1, :]) * own
            y_ref[rows, :] = y_ref[rows, :] * own


def output_kernel(carried_ref, query_ref, grown_ref, y_ref, vec_ref, w_out_ref,
                  out_ref, gated_ref, normed_ref, weight_ref, sem):
    fetches = fetch_rows(w_out_ref, weight_ref, sem)
    inner, length = y_ref.shape
    queries = query_ref[...]
    total = jnp.zeros((1, length), f32)
    for at in range(0, inner, EDGE):
        rows = slice(at, at + EDGE)
        picked = jnp.dot(carried_ref[rows, :], queries, preferred_element_type=f32)
        gated = y_ref[rows, :] + grown_ref[rows, :] * picked
        gated_ref[rows, :] = gated
        total = total + jnp.sum(gated * gated, axis=0, keepdims=True)
    scale = lax.rsqrt(total / inner + epsilon)
    for at in range(0, inner, EDGE):
        gain = columns_of(vec_ref, at)[:, GAIN_OUT : GAIN_OUT + 1]
        normed_ref[at : at + EDGE, :] = (gated_ref[at : at + EDGE, :] * scale * gain).astype(bf16)
    for fetch in fetches:
        fetch.wait()
    out_ref[...] = contract(normed_ref[...], weight_ref[...], ((0,), (0,))).astype(bf16)


def call(kernel, outs, scratch, *args, fetched=()):
    vmem = pl.BlockSpec(memory_space=pltpu.VMEM)
    left = pl.BlockSpec(memory_space=pltpu.HBM)
    single = not isinstance(outs, list)
    args = [
        pltpu.with_memory_space_constraint(a, pltpu.HBM) if at in fetched else a
        for at, a in enumerate(args)
    ]
    return pl.pallas_call(
        kernel,
        out_shape=outs,
        in_specs=[left if at in fetched else vmem for at in range(len(args))],
        out_specs=vmem if single else [vmem] * len(outs),
        scratch_shapes=scratch,
        compiler_params=pltpu.CompilerParams(vmem_limit_bytes=12 << 20),
    )(*args)


def local(
    columns,
    gaps,
    norm_in,
    w_gate,
    w_xbc,
    w_step,
    step_bias,
    conv_weight,
    conv_bias,
    rates,
    norm_out,
    w_out,
):
    length = columns.shape[1]
    depth, inner = w_gate.shape
    heads = w_step.shape[1]
    width = w_xbc.shape[1]
    state_width = (width - inner) // 2
    own = heads // GROUP
    size = inner // GROUP
    shape = jax.ShapeDtypeStruct

    rows = [conv_weight, conv_bias[None], norm_in[None], norm_out[None]]
    vec = jnp.concatenate([jnp.pad(r, ((0, 0), (0, width - r.shape[1]))) for r in rows])
    vec = jnp.pad(vec, ((0, 8 - vec.shape[0]), (0, 0)))
    head = jnp.stack([step_bias, rates], axis=1)

    whole = lax.all_to_all(columns, "table", split_axis=0, concat_axis=2, tiled=True)
    staged = [w_xbc, w_step.T, gaps]
    staged = call(
        stage_kernel,
        [shape(a.shape, a.dtype) for a in staged],
        [pltpu.SemaphoreType.DMA((len(staged),))],
        *staged,
        fetched=range(len(staged)),
    )
    whole, vec, head, *staged = lax.optimization_barrier((whole, vec, head, *staged))
    w_xbc, w_step_t, gaps = staged
    x = whole.reshape(length, depth).T
    edge = passed_along(x[:, length - EDGE :], "seq", 1)
    normed, act, dt, cs, state, logs, first, coef_first = call(
        main_kernel,
        [
            shape((depth, length), bf16),
            shape((width, length), bf16),
            shape((heads, length), f32),
            shape((heads, length), f32),
            shape((inner, state_width), f32),
            shape((GROUP * EXTRA, state_width), bf16),
            shape((EXTRA, width), f32),
            shape((EXTRA, inner), f32),
        ],
        [
            pltpu.VMEM((heads, length), f32),
            pltpu.VMEM((GROUP * EXTRA, state_width), f32),
            pltpu.VMEM((length, depth), bf16),
            pltpu.VMEM((EXTRA + length, width), f32),
        ],
        x, vec, w_xbc, w_step_t, head, gaps,
    )
    send, act_first = call(
        edge_kernel,
        [shape((GROUP, size + EXTRA, state_width), bf16), shape((EXTRA, width), f32)],
        [pltpu.VMEM((2 * EXTRA, width), f32)],
        edge, first, vec, w_xbc, coef_first, state, logs,
    )
    states = within_groups(send)
    total = call(
        functools.partial(prefix_kernel, own),
        shape((size + EXTRA, state_width), bf16),
        [pltpu.VMEM((EXTRA, state_width), f32)],
        states,
    )
    assert lax.axis_size("seq") == 4 * GROUP
    first = passed_along(total, "seq", GROUP, members(0))
    middle = passed_along(total, "seq", 2 * GROUP, members(1))
    far = passed_along(total, "seq", 3 * GROUP, members(0))
    joined, same = call(
        functools.partial(join_kernel, own),
        [shape((size + EXTRA, state_width), bf16)] * 2,
        [],
        total, first,
    )
    after = passed_along(joined, "seq", GROUP, members(1))
    near = passed_along(same, "seq", GROUP, members(2))
    back = call(
        functools.partial(combine_kernel, own),
        shape((GROUP, size, state_width), bf16),
        [],
        states, first, after, near, middle, far,
    )
    back, act = lax.optimization_barrier((back, act))
    carried = within_groups(back).reshape(inner, state_width)
    grown, y, query = call(
        inside_kernel,
        [
            shape((inner, length), f32),
            shape((inner, length), f32),
            shape((state_width, length), bf16),
        ],
        [
            pltpu.VMEM((width, length), bf16),
            pltpu.VMEM((length, length), f32),
            pltpu.VMEM((length, length), bf16),
            pltpu.VMEM((depth, inner), bf16),
            pltpu.SemaphoreType.DMA((PARTS,)),
        ],
        normed, w_gate, act, act_first, dt, cs,
        fetched=(1,),
    )
    out = call(
        output_kernel,
        shape((length, w_out.shape[1]), bf16),
        [
            pltpu.VMEM((inner, length), f32),
            pltpu.VMEM((inner, length), bf16),
            pltpu.VMEM(w_out.shape, bf16),
            pltpu.SemaphoreType.DMA((PARTS,)),
        ],
        carried, query, grown, y, vec, w_out,
        fetched=(5,),
    )
    return out[None]


def solution(mesh):
    in_specs = (
        P(None, "seq", "table"),
        P("table", "seq"),
        P(),
        P(),
        P(),
        P(),
        P(),
        P(),
        P(),
        P(),
        P(),
        P(),
    )
    out_specs = P("table", "seq", None)
    return jax.shard_map(local, mesh=mesh, in_specs=in_specs, out_specs=out_specs, check_vma=False)
```

```python
import functools

import jax
import jax.numpy as jnp
from jax import lax
from jax.experimental import pallas as pl
from jax.experimental.pallas import tpu as pltpu
from jax.sharding import PartitionSpec as P

GROUP = 8
EDGE = 128
EXTRA = 8
PARTS = 4
BIAS, GAIN_IN, GAIN_OUT = 4, 5, 6
epsilon = 1e-05
f32 = jnp.float32
bf16 = jnp.bfloat16


def passed_along(block, axis, distance, senders=None):
    devices = range(lax.axis_size(axis))
    route = [(i, i + distance) for i in senders or devices if i + distance in devices]
    return lax.ppermute(block, axis, route)


def members(*groups):
    return [g * GROUP + i for g in groups for i in range(GROUP)]


def within_groups(blocks):
    count = lax.axis_size("seq") // GROUP
    groups = [[g * GROUP + i for i in range(GROUP)] for g in range(count)]
    return lax.all_to_all(
        blocks, "seq", split_axis=0, concat_axis=0, tiled=True, axis_index_groups=groups
    )


def fetch_rows(source, target, sems):
    count = sems.shape[0]
    step = source.shape[0] // count
    copies = [
        pltpu.make_async_copy(
            source.at[at * step : (at + 1) * step], target.at[at * step : (at + 1) * step], sems.at[at]
        )
        for at in range(count)
    ]
    for copy in copies:
        copy.start()
    return copies


def contract(a, b, dims):
    return lax.dot_general(a, b, (dims, ((), ())), preferred_element_type=f32)


def columns_of(vec_ref, at):
    return vec_ref[:, at : at + EDGE].T


def normed_columns(x_ref, vec_ref, out_ref):
    depth, length = x_ref.shape
    total = jnp.zeros((1, length), f32)
    for at in range(0, depth, 64):
        x = x_ref[at : at + 64, :].astype(f32)
        total = total + jnp.sum(x * x, axis=0, keepdims=True)
    scale = lax.rsqrt(total / depth + epsilon)
    for at in range(0, depth, EDGE):
        gain = columns_of(vec_ref, at)[:, GAIN_IN : GAIN_IN + 1]
        x = x_ref[at : at + EDGE, :].astype(f32)
        out_ref[at : at + EDGE, :] = (x * scale * gain).astype(bf16)


def running_sum(values):
    length = values.shape[1]
    lane = lax.broadcasted_iota(jnp.int32, values.shape, 1)
    reach = 1
    while reach < length:
        values = values + jnp.where(lane >= reach, pltpu.roll(values, reach, axis=1), 0.0)
        reach *= 2
    return values


def stage_kernel(*refs):
    count = len(refs) // 2
    sems = refs[-1]
    copies = [
        pltpu.make_async_copy(refs[at], refs[count + at], sems.at[at]) for at in range(count)
    ]
    for copy in copies:
        copy.start()
    for copy in copies:
        copy.wait()


def main_kernel(x_ref, vec_ref, w_xbc_ref, w_step_ref, head_ref, gaps_ref,
                normed_ref, act_ref, dt_ref, cs_ref, state_ref, logs_ref, first_ref, coef_first_ref,
                coef_ref, rows_ref, upright_ref, shift_ref, weighted_ref):
    depth, length = x_ref.shape
    heads = dt_ref.shape[0]
    inner, state_width = state_ref.shape
    head_dim = inner // heads
    normed_columns(x_ref, vec_ref, normed_ref)
    normed = normed_ref[...]
    raw = jnp.dot(w_step_ref[...], normed, preferred_element_type=f32)
    raw = raw + head_ref[:, 0:1]
    dt = jnp.maximum(raw, 0.0) + jnp.log1p(jnp.exp(-jnp.abs(raw)))
    dt_ref[...] = dt
    cs = running_sum(-head_ref[:, 1:2] * dt * gaps_ref[...])
    cs_ref[...] = cs
    coef = jnp.exp(cs[:, length - 1 : length] - cs) * dt
    coef_first = coef[:, 0:EDGE].T[0:EXTRA, :]
    for head in range(heads):
        coef_first_ref[:, head * head_dim : (head + 1) * head_dim] = jnp.broadcast_to(
            coef_first[:, head : head + 1], (EXTRA, head_dim)
        )
    lane = lax.broadcasted_iota(jnp.int32, coef.shape, 1)
    coef_ref[...] = jnp.where(lane >= EXTRA, coef, 0.0)
    total = jnp.broadcast_to(cs[:, length - 1 : length], (heads, state_width))
    pack_logs(total, rows_ref)
    logs_ref[...] = rows_ref[...].astype(bf16)

    for at in range(0, depth, EDGE):
        upright_ref[:, at : at + EDGE] = normed_ref[at : at + EDGE, :].astype(f32).T.astype(bf16)
    shift_ref[0:EXTRA, :] = jnp.zeros((EXTRA, shift_ref.shape[1]), f32)
    upright = upright_ref[...]

    def act_of(at, step):
        cols = slice(at, at + step)
        whole = jnp.dot(upright, w_xbc_ref[:, cols], preferred_element_type=f32)
        shift_ref[EXTRA:, cols] = whole.astype(bf16).astype(f32)
        conv = vec_ref[BIAS : BIAS + 1, cols]
        for tap in range(BIAS):
            first = EXTRA - (BIAS - 1 - tap)
            conv = conv + vec_ref[tap : tap + 1, cols] * shift_ref[first : first + length, cols]
        act = conv * jax.nn.sigmoid(conv)
        turned = act.T.astype(bf16)
        act_ref[at : at + step, :] = turned
        return act.astype(bf16), turned

    b, _ = act_of(inner, state_width)
    act_of(inner + state_width, state_width)
    step = 2 * head_dim
    for at in range(0, inner, step):
        act = act_of(at, step)[1].astype(f32)
        head = at // head_dim
        coef = jnp.concatenate(
            [jnp.broadcast_to(coef_ref[h : h + 1, :], (head_dim, length)) for h in (head, head + 1)],
            axis=0,
        )
        weighted_ref[at : at + step, :] = (act * coef).astype(bf16)
    state_ref[...] = jnp.dot(weighted_ref[...], b, preferred_element_type=f32)
    first_ref[...] = shift_ref[EXTRA : 2 * EXTRA, :]


def edge_kernel(edge_ref, first_ref, vec_ref, w_xbc_ref, coef_ref, state_ref, logs_ref,
                send_ref, act_ref, rows_ref):
    inner, state_width = state_ref.shape
    depth = edge_ref.shape[0]
    x = edge_ref[...].astype(f32).T[EDGE - EXTRA :, :]
    scale = lax.rsqrt(jnp.mean(x * x, axis=1, keepdims=True) + epsilon)
    normed = (x * scale * vec_ref[GAIN_IN : GAIN_IN + 1, :depth]).astype(bf16)
    before = jnp.dot(normed, w_xbc_ref[...], preferred_element_type=f32)
    rows_ref[0:EXTRA, :] = before.astype(bf16).astype(f32)
    rows_ref[EXTRA:, :] = first_ref[...]
    conv = vec_ref[BIAS : BIAS + 1, :]
    for tap in range(BIAS):
        at = EXTRA - (BIAS - 1 - tap)
        conv = conv + vec_ref[tap : tap + 1, :] * rows_ref[at : at + EXTRA, :]
    act = (conv * jax.nn.sigmoid(conv)).astype(bf16).astype(f32)
    act_ref[...] = act
    weighted = (act[:, :inner] * coef_ref[...]).astype(bf16).astype(f32)
    none = jnp.zeros_like(weighted)
    weighted = jnp.concatenate([weighted, none], axis=0).astype(bf16)
    b = act[:, inner : inner + state_width]
    b = jnp.concatenate([b, jnp.zeros_like(b)], axis=0).astype(bf16)
    size = inner // GROUP
    whole = state_ref[...] + contract(weighted, b, ((0,), (0,)))
    for part in range(GROUP):
        send_ref[part, 0:size, :] = whole[part * size : (part + 1) * size, :].astype(bf16)
        send_ref[part, size : size + EXTRA, :] = logs_ref[part * EXTRA : (part + 1) * EXTRA, :]


def pack_logs(total, rows_ref):
    heads = total.shape[0]
    own = rows_ref.shape[0] // EXTRA
    own = heads // own
    rows_ref[...] = jnp.zeros_like(rows_ref)
    rest = total
    for piece in range(3):
        part = rest.astype(bf16).astype(f32)
        rest = rest - part
        for head in range(heads):
            at = head // own * EXTRA + head % own * 3 + piece
            rows_ref[at : at + 1, :] = part[head : head + 1, :]


def read_logs(rows, own):
    rows = rows.astype(f32)
    return [
        rows[3 * h : 3 * h + 1, :] + rows[3 * h + 1 : 3 * h + 2, :] + rows[3 * h + 2 : 3 * h + 3, :]
        for h in range(own)
    ]


def prefix_kernel(own, states_ref, send_ref, rows_ref):
    size = send_ref.shape[0] - EXTRA
    head_dim = size // own
    width = send_ref.shape[1]
    logs = [read_logs(states_ref[m, size : size + EXTRA, :], own) for m in range(GROUP)]
    for h in range(own):
        rows = slice(h * head_dim, (h + 1) * head_dim)
        state = jnp.zeros((head_dim, width), f32)
        for m in range(GROUP):
            state = jnp.exp(logs[m][h]) * state + states_ref[m, rows, :].astype(f32)
        send_ref[rows, :] = state.astype(bf16)
    total = [sum(logs[m][h] for m in range(GROUP)) for h in range(own)]
    pack_logs(jnp.concatenate(total, axis=0), rows_ref)
    send_ref[size : size + EXTRA, :] = rows_ref[...].astype(bf16)


def join_kernel(own, total_ref, earlier_ref, send_ref):
    size = send_ref.shape[0] - EXTRA
    head_dim = size // own
    jumps = read_logs(total_ref[size:, :], own)
    for h in range(own):
        rows = slice(h * head_dim, (h + 1) * head_dim)
        state = jnp.exp(jumps[h]) * earlier_ref[rows, :].astype(f32)
        send_ref[rows, :] = (total_ref[rows, :].astype(f32) + state).astype(bf16)
    send_ref[size:, :] = jnp.zeros((EXTRA, send_ref.shape[1]), bf16)


def combine_kernel(own, states_ref, near_ref, after_ref, far_ref, middle_ref, back_ref):
    size = back_ref.shape[1]
    head_dim = size // own
    logs = [read_logs(states_ref[m, size : size + EXTRA, :], own) for m in range(GROUP)]
    near_jumps = read_logs(near_ref[size:, :], own)
    middle_jumps = read_logs(middle_ref[size:, :], own)
    for h in range(own):
        rows = slice(h * head_dim, (h + 1) * head_dim)
        state = middle_ref[rows, :].astype(f32)
        state = state + jnp.exp(middle_jumps[h]) * far_ref[rows, :].astype(f32)
        state = near_ref[rows, :].astype(f32) + jnp.exp(near_jumps[h]) * state
        state = state + after_ref[rows, :].astype(f32)
        for m in range(GROUP):
            back_ref[m, rows, :] = state.astype(bf16)
            state = jnp.exp(logs[m][h]) * state + states_ref[m, rows, :].astype(f32)


def inside_kernel(normed_ref, w_gate_ref, main_ref, first_ref, dt_ref, cs_ref,
                  grown_ref, y_ref, query_ref, act_ref, scores_ref, mix_ref, weight_ref, sem):
    fetches = fetch_rows(w_gate_ref, weight_ref, sem)
    heads, length = dt_ref.shape
    inner = y_ref.shape[0]
    lane = lax.broadcasted_iota(jnp.int32, (EDGE, EDGE), 1)
    rest = jnp.zeros((EDGE - EXTRA, EDGE), f32)
    for at in range(0, act_ref.shape[0], EDGE):
        rows = slice(at, at + EDGE)
        first = jnp.concatenate([first_ref[:, rows], rest], axis=0).T
        kept = main_ref[rows, 0:EDGE].astype(f32)
        act_ref[rows, 0:EDGE] = jnp.where(lane < EXTRA, first, kept).astype(bf16)
        act_ref[rows, EDGE:] = main_ref[rows, EDGE:]
    head_dim = inner // heads
    state_width = (act_ref.shape[0] - inner) // 2
    query_ref[...] = act_ref[inner + state_width :, :]
    scores_ref[...] = contract(
        act_ref[inner : inner + state_width, :], act_ref[inner + state_width :, :], ((0,), (0,))
    )
    cs_col = cs_ref[...].T
    dt_col = dt_ref[...].T
    half = length // 2
    mix_ref[...] = jnp.zeros_like(mix_ref)
    later = lax.broadcasted_iota(jnp.int32, (half, half), 1)
    early = lax.broadcasted_iota(jnp.int32, (half, half), 0)
    keep = later >= early
    for h in range(heads):
        for s in (0, half):
            cs_s = jnp.broadcast_to(cs_col[s : s + half, h : h + 1], (half, half))
            dt_s = jnp.broadcast_to(dt_col[s : s + half, h : h + 1], (half, half))
            for t in range(s, length, half):
                diff = cs_ref[h : h + 1, t : t + half] - cs_s
                if s == t:
                    diff = jnp.where(keep, diff, -jnp.inf)
                mix_ref[s : s + half, t : t + half] = (
                    scores_ref[s : s + half, t : t + half] * jnp.exp(diff) * dt_s
                ).astype(bf16)
        rows = slice(h * head_dim, (h + 1) * head_dim)
        y_ref[rows, :] = jnp.dot(act_ref[rows, :], mix_ref[...], preferred_element_type=f32)
    for fetch in fetches:
        fetch.wait()
    normed = normed_ref[...]
    step = 4 * head_dim
    for at in range(0, inner, step):
        gate = contract(weight_ref[:, at : at + step], normed, ((0,), (0,)))
        gate = gate.astype(bf16).astype(f32)
        gate = gate * jax.nn.sigmoid(gate)
        for h in range(at // head_dim, (at + step) // head_dim):
            rows = slice(h * head_dim, (h + 1) * head_dim)
            own = gate[h * head_dim - at : (h + 1) * head_dim - at, :]
            grown_ref[rows, :] = jnp.exp(cs_ref[h : h + 1, :]) * own
            y_ref[rows, :] = y_ref[rows, :] * own


def output_kernel(carried_ref, query_ref, grown_ref, y_ref, vec_ref, w_out_ref,
                  out_ref, gated_ref, normed_ref, weight_ref, sem):
    fetches = fetch_rows(w_out_ref, weight_ref, sem)
    inner, length = y_ref.shape
    gated_ref[...] = jnp.dot(carried_ref[...], query_ref[...], preferred_element_type=f32)
    total = jnp.zeros((1, length), f32)
    for at in range(0, inner, EDGE):
        rows = slice(at, at + EDGE)
        gated = y_ref[rows, :] + grown_ref[rows, :] * gated_ref[rows, :]
        gated_ref[rows, :] = gated
        total = total + jnp.sum(gated * gated, axis=0, keepdims=True)
    scale = lax.rsqrt(total / inner + epsilon)
    for at in range(0, inner, EDGE):
        gain = columns_of(vec_ref, at)[:, GAIN_OUT : GAIN_OUT + 1]
        normed_ref[at : at + EDGE, :] = (gated_ref[at : at + EDGE, :] * scale * gain).astype(bf16)
    for fetch in fetches:
        fetch.wait()
    out_ref[...] = contract(normed_ref[...], weight_ref[...], ((0,), (0,))).astype(bf16)


def call(kernel, outs, scratch, *args, fetched=()):
    vmem = pl.BlockSpec(memory_space=pltpu.VMEM)
    left = pl.BlockSpec(memory_space=pltpu.HBM)
    single = not isinstance(outs, list)
    args = [
        pltpu.with_memory_space_constraint(a, pltpu.HBM) if at in fetched else a
        for at, a in enumerate(args)
    ]
    return pl.pallas_call(
        kernel,
        out_shape=outs,
        in_specs=[left if at in fetched else vmem for at in range(len(args))],
        out_specs=vmem if single else [vmem] * len(outs),
        scratch_shapes=scratch,
        compiler_params=pltpu.CompilerParams(vmem_limit_bytes=12 << 20),
    )(*args)


def local(
    columns,
    gaps,
    norm_in,
    w_gate,
    w_xbc,
    w_step,
    step_bias,
    conv_weight,
    conv_bias,
    rates,
    norm_out,
    w_out,
):
    length = columns.shape[1]
    depth, inner = w_gate.shape
    heads = w_step.shape[1]
    width = w_xbc.shape[1]
    state_width = (width - inner) // 2
    own = heads // GROUP
    size = inner // GROUP
    shape = jax.ShapeDtypeStruct

    rows = [conv_weight, conv_bias[None], norm_in[None], norm_out[None]]
    vec = jnp.concatenate([jnp.pad(r, ((0, 0), (0, width - r.shape[1]))) for r in rows])
    vec = jnp.pad(vec, ((0, 8 - vec.shape[0]), (0, 0)))
    head = jnp.stack([step_bias, rates], axis=1)

    whole = lax.all_to_all(columns, "table", split_axis=0, concat_axis=2, tiled=True)
    staged = [w_xbc, w_step.T, gaps]
    staged = call(
        stage_kernel,
        [shape(a.shape, a.dtype) for a in staged],
        [pltpu.SemaphoreType.DMA((len(staged),))],
        *staged,
        fetched=range(len(staged)),
    )
    whole, vec, head, *staged = lax.optimization_barrier((whole, vec, head, *staged))
    w_xbc, w_step_t, gaps = staged
    x = whole.reshape(length, depth).T
    edge = passed_along(x[:, length - EDGE :], "seq", 1)
    normed, act, dt, cs, state, logs, first, coef_first = call(
        main_kernel,
        [
            shape((depth, length), bf16),
            shape((width, length), bf16),
            shape((heads, length), f32),
            shape((heads, length), f32),
            shape((inner, state_width), f32),
            shape((GROUP * EXTRA, state_width), bf16),
            shape((EXTRA, width), f32),
            shape((EXTRA, inner), f32),
        ],
        [
            pltpu.VMEM((heads, length), f32),
            pltpu.VMEM((GROUP * EXTRA, state_width), f32),
            pltpu.VMEM((length, depth), bf16),
            pltpu.VMEM((EXTRA + length, width), f32),
            pltpu.VMEM((inner, length), bf16),
        ],
        x, vec, w_xbc, w_step_t, head, gaps,
    )
    send, act_first = call(
        edge_kernel,
        [shape((GROUP, size + EXTRA, state_width), bf16), shape((EXTRA, width), f32)],
        [pltpu.VMEM((2 * EXTRA, width), f32)],
        edge, first, vec, w_xbc, coef_first, state, logs,
    )
    states = within_groups(send)
    total = call(
        functools.partial(prefix_kernel, own),
        shape((size + EXTRA, state_width), bf16),
        [pltpu.VMEM((EXTRA, state_width), f32)],
        states,
    )
    assert lax.axis_size("seq") == 4 * GROUP
    near = passed_along(total, "seq", GROUP, members(0, 2))
    middle = passed_along(total, "seq", 2 * GROUP, members(1))
    far = passed_along(total, "seq", 3 * GROUP, members(0))
    joined = call(
        functools.partial(join_kernel, own),
        shape((size + EXTRA, state_width), bf16),
        [],
        total, near,
    )
    after = passed_along(joined, "seq", GROUP, members(1))
    back = call(
        functools.partial(combine_kernel, own),
        shape((GROUP, size, state_width), bf16),
        [],
        states, near, after, far, middle,
    )
    back, act = lax.optimization_barrier((back, act))
    carried = within_groups(back).reshape(inner, state_width)
    grown, y, query = call(
        inside_kernel,
        [
            shape((inner, length), f32),
            shape((inner, length), f32),
            shape((state_width, length), bf16),
        ],
        [
            pltpu.VMEM((width, length), bf16),
            pltpu.VMEM((length, length), f32),
            pltpu.VMEM((length, length), bf16),
            pltpu.VMEM((depth, inner), bf16),
            pltpu.SemaphoreType.DMA((PARTS,)),
        ],
        normed, w_gate, act, act_first, dt, cs,
        fetched=(1,),
    )
    out = call(
        output_kernel,
        shape((length, w_out.shape[1]), bf16),
        [
            pltpu.VMEM((inner, length), f32),
            pltpu.VMEM((inner, length), bf16),
            pltpu.VMEM(w_out.shape, bf16),
            pltpu.SemaphoreType.DMA((PARTS,)),
        ],
        carried, query, grown, y, vec, w_out,
        fetched=(5,),
    )
    return out[None]


def solution(mesh):
    in_specs = (
        P(None, "seq", "table"),
        P("table", "seq"),
        P(),
        P(),
        P(),
        P(),
        P(),
        P(),
        P(),
        P(),
        P(),
        P(),
    )
    out_specs = P("table", "seq", None)
    return jax.shard_map(local, mesh=mesh, in_specs=in_specs, out_specs=out_specs, check_vma=False)
```

```python
import functools

import jax
import jax.numpy as jnp
from jax import lax
from jax.experimental import pallas as pl
from jax.experimental.pallas import tpu as pltpu
from jax.sharding import PartitionSpec as P

GROUP = 8
EDGE = 128
EXTRA = 8
PARTS = 4
BIAS, GAIN_IN, GAIN_OUT = 4, 5, 6
epsilon = 1e-05
f32 = jnp.float32
bf16 = jnp.bfloat16


def passed_along(block, axis, distance, senders=None):
    devices = range(lax.axis_size(axis))
    route = [(i, i + distance) for i in senders or devices if i + distance in devices]
    return lax.ppermute(block, axis, route)


def members(*groups):
    return [g * GROUP + i for g in groups for i in range(GROUP)]


def within_groups(blocks):
    count = lax.axis_size("seq") // GROUP
    groups = [[g * GROUP + i for i in range(GROUP)] for g in range(count)]
    return lax.all_to_all(
        blocks, "seq", split_axis=0, concat_axis=0, tiled=True, axis_index_groups=groups
    )


def fetch_rows(source, target, sems):
    count = sems.shape[0]
    step = source.shape[0] // count
    copies = [
        pltpu.make_async_copy(
            source.at[at * step : (at + 1) * step], target.at[at * step : (at + 1) * step], sems.at[at]
        )
        for at in range(count)
    ]
    for copy in copies:
        copy.start()
    return copies


def contract(a, b, dims):
    return lax.dot_general(a, b, (dims, ((), ())), preferred_element_type=f32)


def columns_of(vec_ref, at):
    return vec_ref[:, at : at + EDGE].T


def normed_columns(x_ref, vec_ref, out_ref):
    depth, length = x_ref.shape
    total = jnp.zeros((1, length), f32)
    for at in range(0, depth, 64):
        x = x_ref[at : at + 64, :].astype(f32)
        total = total + jnp.sum(x * x, axis=0, keepdims=True)
    scale = lax.rsqrt(total / depth + epsilon)
    for at in range(0, depth, EDGE):
        gain = columns_of(vec_ref, at)[:, GAIN_IN : GAIN_IN + 1]
        x = x_ref[at : at + EDGE, :].astype(f32)
        out_ref[at : at + EDGE, :] = (x * scale * gain).astype(bf16)


def running_sum(values):
    length = values.shape[1]
    lane = lax.broadcasted_iota(jnp.int32, values.shape, 1)
    reach = 1
    while reach < length:
        values = values + jnp.where(lane >= reach, pltpu.roll(values, reach, axis=1), 0.0)
        reach *= 2
    return values


def stage_kernel(*refs):
    count = len(refs) // 2
    sems = refs[-1]
    copies = [
        pltpu.make_async_copy(refs[at], refs[count + at], sems.at[at]) for at in range(count)
    ]
    for copy in copies:
        copy.start()
    for copy in copies:
        copy.wait()


def main_kernel(x_ref, vec_ref, w_xbc_ref, w_step_ref, head_ref, gaps_ref,
                normed_ref, act_ref, dt_ref, cs_ref, state_ref, logs_ref, first_ref, coef_first_ref,
                coef_ref, rows_ref, upright_ref, shift_ref, weighted_ref):
    depth, length = x_ref.shape
    heads = dt_ref.shape[0]
    inner, state_width = state_ref.shape
    head_dim = inner // heads
    normed_columns(x_ref, vec_ref, normed_ref)
    normed = normed_ref[...]
    raw = jnp.dot(w_step_ref[...], normed, preferred_element_type=f32)
    raw = raw + head_ref[:, 0:1]
    dt = jnp.maximum(raw, 0.0) + jnp.log1p(jnp.exp(-jnp.abs(raw)))
    dt_ref[...] = dt
    cs = running_sum(-head_ref[:, 1:2] * dt * gaps_ref[...])
    cs_ref[...] = cs
    coef = jnp.exp(cs[:, length - 1 : length] - cs) * dt
    coef_first = coef[:, 0:EDGE].T[0:EXTRA, :]
    for head in range(heads):
        coef_first_ref[:, head * head_dim : (head + 1) * head_dim] = jnp.broadcast_to(
            coef_first[:, head : head + 1], (EXTRA, head_dim)
        )
    lane = lax.broadcasted_iota(jnp.int32, coef.shape, 1)
    coef_ref[...] = jnp.where(lane >= EXTRA, coef, 0.0)
    total = jnp.broadcast_to(cs[:, length - 1 : length], (heads, state_width))
    pack_logs(total, rows_ref)
    logs_ref[...] = rows_ref[...].astype(bf16)

    for at in range(0, depth, EDGE):
        upright_ref[:, at : at + EDGE] = normed_ref[at : at + EDGE, :].astype(f32).T.astype(bf16)
    shift_ref[0:EXTRA, :] = jnp.zeros((EXTRA, shift_ref.shape[1]), f32)
    upright = upright_ref[...]

    def act_of(at, step):
        cols = slice(at, at + step)
        whole = jnp.dot(upright, w_xbc_ref[:, cols], preferred_element_type=f32)
        shift_ref[EXTRA:, cols] = whole.astype(bf16).astype(f32)
        conv = vec_ref[BIAS : BIAS + 1, cols]
        for tap in range(BIAS):
            first = EXTRA - (BIAS - 1 - tap)
            conv = conv + vec_ref[tap : tap + 1, cols] * shift_ref[first : first + length, cols]
        act = conv * jax.nn.sigmoid(conv)
        turned = act.T.astype(bf16)
        act_ref[at : at + step, :] = turned
        return act.astype(bf16), turned

    b, _ = act_of(inner, state_width)
    act_of(inner + state_width, state_width)
    step = 2 * head_dim
    for at in range(0, inner, step):
        act = act_of(at, step)[1].astype(f32)
        head = at // head_dim
        coef = jnp.concatenate(
            [jnp.broadcast_to(coef_ref[h : h + 1, :], (head_dim, length)) for h in (head, head + 1)],
            axis=0,
        )
        weighted_ref[at : at + step, :] = (act * coef).astype(bf16)
    state_ref[...] = jnp.dot(weighted_ref[...], b, preferred_element_type=f32)
    first_ref[...] = shift_ref[EXTRA : 2 * EXTRA, :]


def edge_kernel(edge_ref, first_ref, vec_ref, w_xbc_ref, coef_ref, state_ref, logs_ref,
                send_ref, act_ref, rows_ref):
    inner, state_width = state_ref.shape
    depth = edge_ref.shape[0]
    x = edge_ref[...].astype(f32).T[EDGE - EXTRA :, :]
    scale = lax.rsqrt(jnp.mean(x * x, axis=1, keepdims=True) + epsilon)
    normed = (x * scale * vec_ref[GAIN_IN : GAIN_IN + 1, :depth]).astype(bf16)
    before = jnp.dot(normed, w_xbc_ref[...], preferred_element_type=f32)
    rows_ref[0:EXTRA, :] = before.astype(bf16).astype(f32)
    rows_ref[EXTRA:, :] = first_ref[...]
    conv = vec_ref[BIAS : BIAS + 1, :]
    for tap in range(BIAS):
        at = EXTRA - (BIAS - 1 - tap)
        conv = conv + vec_ref[tap : tap + 1, :] * rows_ref[at : at + EXTRA, :]
    act = (conv * jax.nn.sigmoid(conv)).astype(bf16).astype(f32)
    act_ref[...] = act
    weighted = (act[:, :inner] * coef_ref[...]).astype(bf16).astype(f32)
    none = jnp.zeros_like(weighted)
    weighted = jnp.concatenate([weighted, none], axis=0).astype(bf16)
    b = act[:, inner : inner + state_width]
    b = jnp.concatenate([b, jnp.zeros_like(b)], axis=0).astype(bf16)
    size = inner // GROUP
    whole = state_ref[...] + contract(weighted, b, ((0,), (0,)))
    for part in range(GROUP):
        send_ref[part, 0:size, :] = whole[part * size : (part + 1) * size, :].astype(bf16)
        send_ref[part, size : size + EXTRA, :] = logs_ref[part * EXTRA : (part + 1) * EXTRA, :]


def pack_logs(total, rows_ref):
    heads = total.shape[0]
    own = rows_ref.shape[0] // EXTRA
    own = heads // own
    rows_ref[...] = jnp.zeros_like(rows_ref)
    rest = total
    for piece in range(3):
        part = rest.astype(bf16).astype(f32)
        rest = rest - part
        for head in range(heads):
            at = head // own * EXTRA + head % own * 3 + piece
            rows_ref[at : at + 1, :] = part[head : head + 1, :]


def read_logs(rows, own):
    rows = rows.astype(f32)
    return [
        rows[3 * h : 3 * h + 1, :] + rows[3 * h + 1 : 3 * h + 2, :] + rows[3 * h + 2 : 3 * h + 3, :]
        for h in range(own)
    ]


def prefix_kernel(own, states_ref, send_ref, rows_ref):
    size = send_ref.shape[0] - EXTRA
    head_dim = size // own
    width = send_ref.shape[1]
    logs = [read_logs(states_ref[m, size : size + EXTRA, :], own) for m in range(GROUP)]
    for h in range(own):
        rows = slice(h * head_dim, (h + 1) * head_dim)
        state = jnp.zeros((head_dim, width), f32)
        for m in range(GROUP):
            state = jnp.exp(logs[m][h]) * state + states_ref[m, rows, :].astype(f32)
        send_ref[rows, :] = state.astype(bf16)
    total = [sum(logs[m][h] for m in range(GROUP)) for h in range(own)]
    pack_logs(jnp.concatenate(total, axis=0), rows_ref)
    send_ref[size : size + EXTRA, :] = rows_ref[...].astype(bf16)


def join_kernel(own, total_ref, earlier_ref, send_ref):
    size = send_ref.shape[0] - EXTRA
    head_dim = size // own
    jumps = read_logs(total_ref[size:, :], own)
    for h in range(own):
        rows = slice(h * head_dim, (h + 1) * head_dim)
        state = jnp.exp(jumps[h]) * earlier_ref[rows, :].astype(f32)
        send_ref[rows, :] = (total_ref[rows, :].astype(f32) + state).astype(bf16)
    send_ref[size:, :] = jnp.zeros((EXTRA, send_ref.shape[1]), bf16)


def combine_kernel(own, states_ref, near_ref, after_ref, middle_ref, far_ref, back_ref):
    size = back_ref.shape[1]
    head_dim = size // own
    logs = [read_logs(states_ref[m, size : size + EXTRA, :], own) for m in range(GROUP)]
    near_jumps = read_logs(near_ref[size:, :], own)
    middle_jumps = read_logs(middle_ref[size:, :], own)
    for h in range(own):
        rows = slice(h * head_dim, (h + 1) * head_dim)
        state = middle_ref[rows, :].astype(f32)
        state = state + jnp.exp(middle_jumps[h]) * far_ref[rows, :].astype(f32)
        state = near_ref[rows, :].astype(f32) + jnp.exp(near_jumps[h]) * state
        state = state + after_ref[rows, :].astype(f32)
        for m in range(GROUP):
            back_ref[m, rows, :] = state.astype(bf16)
            state = jnp.exp(logs[m][h]) * state + states_ref[m, rows, :].astype(f32)


def inside_kernel(normed_ref, w_gate_ref, main_ref, first_ref, dt_ref, cs_ref,
                  gate_ref, y_ref, query_ref, act_ref, scores_ref, mix_ref, weight_ref, sem):
    fetches = fetch_rows(w_gate_ref, weight_ref, sem)
    heads, length = dt_ref.shape
    inner = y_ref.shape[0]
    lane = lax.broadcasted_iota(jnp.int32, (EDGE, EDGE), 1)
    rest = jnp.zeros((EDGE - EXTRA, EDGE), f32)
    for at in range(0, act_ref.shape[0], EDGE):
        rows = slice(at, at + EDGE)
        first = jnp.concatenate([first_ref[:, rows], rest], axis=0).T
        kept = main_ref[rows, 0:EDGE].astype(f32)
        act_ref[rows, 0:EDGE] = jnp.where(lane < EXTRA, first, kept).astype(bf16)
        act_ref[rows, EDGE:] = main_ref[rows, EDGE:]
    head_dim = inner // heads
    state_width = (act_ref.shape[0] - inner) // 2
    query_ref[...] = act_ref[inner + state_width :, :]
    scores_ref[...] = contract(
        act_ref[inner : inner + state_width, :], act_ref[inner + state_width :, :], ((0,), (0,))
    )
    cs_col = cs_ref[...].T
    dt_col = dt_ref[...].T
    half = length // 2
    mix_ref[...] = jnp.zeros_like(mix_ref)
    later = lax.broadcasted_iota(jnp.int32, (half, half), 1)
    early = lax.broadcasted_iota(jnp.int32, (half, half), 0)
    keep = later >= early
    for h in range(heads):
        for s in (0, half):
            cs_s = jnp.broadcast_to(cs_col[s : s + half, h : h + 1], (half, half))
            dt_s = jnp.broadcast_to(dt_col[s : s + half, h : h + 1], (half, half))
            for t in range(s, length, half):
                diff = cs_ref[h : h + 1, t : t + half] - cs_s
                if s == t:
                    diff = jnp.where(keep, diff, -jnp.inf)
                mix_ref[s : s + half, t : t + half] = (
                    scores_ref[s : s + half, t : t + half] * jnp.exp(diff) * dt_s
                ).astype(bf16)
        rows = slice(h * head_dim, (h + 1) * head_dim)
        y_ref[rows, :] = jnp.dot(act_ref[rows, :], mix_ref[...], preferred_element_type=f32)
    for fetch in fetches:
        fetch.wait()
    normed = normed_ref[...]
    step = 4 * head_dim
    for at in range(0, inner, step):
        gate = contract(weight_ref[:, at : at + step], normed, ((0,), (0,)))
        gate_ref[at : at + step, :] = gate.astype(bf16)


def output_kernel(carried_ref, query_ref, cs_ref, gate_ref, y_ref, vec_ref, w_out_ref,
                  out_ref, gated_ref, normed_ref):
    inner, length = y_ref.shape
    gated_ref[...] = jnp.dot(carried_ref[...], query_ref[...], preferred_element_type=f32)
    heads = cs_ref.shape[0]
    head_dim = inner // heads
    grown = jnp.exp(cs_ref[...])
    total = jnp.zeros((1, length), f32)
    for h in range(heads):
        rows = slice(h * head_dim, (h + 1) * head_dim)
        gate = gate_ref[rows, :].astype(f32)
        gated = y_ref[rows, :] + grown[h : h + 1, :] * gated_ref[rows, :]
        gated = gated * (gate * jax.nn.sigmoid(gate))
        gated_ref[rows, :] = gated
        total = total + jnp.sum(gated * gated, axis=0, keepdims=True)
    scale = lax.rsqrt(total / inner + epsilon)
    for at in range(0, inner, EDGE):
        gain = columns_of(vec_ref, at)[:, GAIN_OUT : GAIN_OUT + 1]
        normed_ref[at : at + EDGE, :] = (gated_ref[at : at + EDGE, :] * scale * gain).astype(bf16)
    out_ref[...] = contract(normed_ref[...], w_out_ref[...], ((0,), (0,))).astype(bf16)


def call(kernel, outs, scratch, *args, fetched=()):
    vmem = pl.BlockSpec(memory_space=pltpu.VMEM)
    left = pl.BlockSpec(memory_space=pltpu.HBM)
    single = not isinstance(outs, list)
    args = [
        pltpu.with_memory_space_constraint(a, pltpu.HBM) if at in fetched else a
        for at, a in enumerate(args)
    ]
    return pl.pallas_call(
        kernel,
        out_shape=outs,
        in_specs=[left if at in fetched else vmem for at in range(len(args))],
        out_specs=vmem if single else [vmem] * len(outs),
        scratch_shapes=scratch,
        compiler_params=pltpu.CompilerParams(vmem_limit_bytes=12 << 20),
    )(*args)


def local(
    columns,
    gaps,
    norm_in,
    w_gate,
    w_xbc,
    w_step,
    step_bias,
    conv_weight,
    conv_bias,
    rates,
    norm_out,
    w_out,
):
    length = columns.shape[1]
    depth, inner = w_gate.shape
    heads = w_step.shape[1]
    width = w_xbc.shape[1]
    state_width = (width - inner) // 2
    own = heads // GROUP
    size = inner // GROUP
    shape = jax.ShapeDtypeStruct

    rows = [conv_weight, conv_bias[None], norm_in[None], norm_out[None]]
    vec = jnp.concatenate([jnp.pad(r, ((0, 0), (0, width - r.shape[1]))) for r in rows])
    vec = jnp.pad(vec, ((0, 8 - vec.shape[0]), (0, 0)))
    head = jnp.stack([step_bias, rates], axis=1)

    whole = lax.all_to_all(columns, "table", split_axis=0, concat_axis=2, tiled=True)
    staged = [w_xbc, w_step.T, gaps]
    staged = call(
        stage_kernel,
        [shape(a.shape, a.dtype) for a in staged],
        [pltpu.SemaphoreType.DMA((len(staged),))],
        *staged,
        fetched=range(len(staged)),
    )
    whole, vec, head, *staged = lax.optimization_barrier((whole, vec, head, *staged))
    w_xbc, w_step_t, gaps = staged
    x = whole.reshape(length, depth).T
    edge = passed_along(x[:, length - EDGE :], "seq", 1)
    normed, act, dt, cs, state, logs, first, coef_first = call(
        main_kernel,
        [
            shape((depth, length), bf16),
            shape((width, length), bf16),
            shape((heads, length), f32),
            shape((heads, length), f32),
            shape((inner, state_width), f32),
            shape((GROUP * EXTRA, state_width), bf16),
            shape((EXTRA, width), f32),
            shape((EXTRA, inner), f32),
        ],
        [
            pltpu.VMEM((heads, length), f32),
            pltpu.VMEM((GROUP * EXTRA, state_width), f32),
            pltpu.VMEM((length, depth), bf16),
            pltpu.VMEM((EXTRA + length, width), f32),
            pltpu.VMEM((inner, length), bf16),
        ],
        x, vec, w_xbc, w_step_t, head, gaps,
    )
    send, act_first = call(
        edge_kernel,
        [shape((GROUP, size + EXTRA, state_width), bf16), shape((EXTRA, width), f32)],
        [pltpu.VMEM((2 * EXTRA, width), f32)],
        edge, first, vec, w_xbc, coef_first, state, logs,
    )
    states = within_groups(send)
    total = call(
        functools.partial(prefix_kernel, own),
        shape((size + EXTRA, state_width), bf16),
        [pltpu.VMEM((EXTRA, state_width), f32)],
        states,
    )
    assert lax.axis_size("seq") == 4 * GROUP
    near = passed_along(total, "seq", GROUP, members(0, 2))
    middle = passed_along(total, "seq", 2 * GROUP, members(1))
    far = passed_along(total, "seq", 3 * GROUP, members(0))
    joined = call(
        functools.partial(join_kernel, own),
        shape((size + EXTRA, state_width), bf16),
        [],
        total, near,
    )
    after = passed_along(joined, "seq", GROUP, members(1))
    back = call(
        functools.partial(combine_kernel, own),
        shape((GROUP, size, state_width), bf16),
        [],
        states, near, after, middle, far,
    )
    back, act = lax.optimization_barrier((back, act))
    carried = within_groups(back).reshape(inner, state_width)
    gate, y, query = call(
        inside_kernel,
        [
            shape((inner, length), bf16),
            shape((inner, length), f32),
            shape((state_width, length), bf16),
        ],
        [
            pltpu.VMEM((width, length), bf16),
            pltpu.VMEM((length, length), f32),
            pltpu.VMEM((length, length), bf16),
            pltpu.VMEM((depth, inner), bf16),
            pltpu.SemaphoreType.DMA((PARTS,)),
        ],
        normed, w_gate, act, act_first, dt, cs,
        fetched=(1,),
    )
    gate, y, query, w_out = lax.optimization_barrier((gate, y, query, w_out))
    (w_out,) = call(
        stage_kernel,
        [shape(w_out.shape, w_out.dtype)],
        [pltpu.SemaphoreType.DMA((1,))],
        w_out,
        fetched=(0,),
    )
    out = call(
        output_kernel,
        shape((length, w_out.shape[1]), bf16),
        [
            pltpu.VMEM((inner, length), f32),
            pltpu.VMEM((inner, length), bf16),
        ],
        carried, query, cs, gate, y, vec, w_out,
    )
    return out[None]


def solution(mesh):
    in_specs = (
        P(None, "seq", "table"),
        P("table", "seq"),
        P(),
        P(),
        P(),
        P(),
        P(),
        P(),
        P(),
        P(),
        P(),
        P(),
    )
    out_specs = P("table", "seq", None)
    return jax.shard_map(local, mesh=mesh, in_specs=in_specs, out_specs=out_specs, check_vma=False)
```

```python
import functools

import jax
import jax.numpy as jnp
from jax import lax
from jax.experimental import pallas as pl
from jax.experimental.pallas import tpu as pltpu
from jax.sharding import PartitionSpec as P

GROUP = 8
EDGE = 128
EXTRA = 8
PARTS = 4
BIAS, GAIN_IN, GAIN_OUT = 4, 5, 6
epsilon = 1e-05
f32 = jnp.float32
bf16 = jnp.bfloat16


def passed_along(block, axis, distance, senders=None):
    devices = range(lax.axis_size(axis))
    route = [(i, i + distance) for i in senders or devices if i + distance in devices]
    return lax.ppermute(block, axis, route)


def members(*groups):
    return [g * GROUP + i for g in groups for i in range(GROUP)]


def within_groups(blocks):
    count = lax.axis_size("seq") // GROUP
    groups = [[g * GROUP + i for i in range(GROUP)] for g in range(count)]
    return lax.all_to_all(
        blocks, "seq", split_axis=0, concat_axis=0, tiled=True, axis_index_groups=groups
    )


def fetch_rows(source, target, sems):
    count = sems.shape[0]
    step = source.shape[0] // count
    copies = [
        pltpu.make_async_copy(
            source.at[at * step : (at + 1) * step], target.at[at * step : (at + 1) * step], sems.at[at]
        )
        for at in range(count)
    ]
    for copy in copies:
        copy.start()
    return copies


def contract(a, b, dims):
    return lax.dot_general(a, b, (dims, ((), ())), preferred_element_type=f32)


def columns_of(vec_ref, at):
    return vec_ref[:, at : at + EDGE].T


def normed_columns(x_ref, vec_ref, out_ref):
    depth, length = x_ref.shape
    total = jnp.zeros((1, length), f32)
    for at in range(0, depth, 64):
        x = x_ref[at : at + 64, :].astype(f32)
        total = total + jnp.sum(x * x, axis=0, keepdims=True)
    scale = lax.rsqrt(total / depth + epsilon)
    for at in range(0, depth, EDGE):
        gain = columns_of(vec_ref, at)[:, GAIN_IN : GAIN_IN + 1]
        x = x_ref[at : at + EDGE, :].astype(f32)
        out_ref[at : at + EDGE, :] = (x * scale * gain).astype(bf16)


def running_sum(values):
    length = values.shape[1]
    lane = lax.broadcasted_iota(jnp.int32, values.shape, 1)
    reach = 1
    while reach < length:
        values = values + jnp.where(lane >= reach, pltpu.roll(values, reach, axis=1), 0.0)
        reach *= 2
    return values


def stage_kernel(*refs):
    count = len(refs) // 2
    sems = refs[-1]
    copies = [
        pltpu.make_async_copy(refs[at], refs[count + at], sems.at[at]) for at in range(count)
    ]
    for copy in copies:
        copy.start()
    for copy in copies:
        copy.wait()


def main_kernel(turn_ref, *refs, before):
    outs = 8
    operands, rest = refs[:6], refs[6 + (outs if before else 0) :]

    @pl.when((turn_ref[0] == 0) == before)
    def _():
        project_and_sum(*operands, *rest)


def project_and_sum(x_ref, vec_ref, w_xbc_ref, w_step_ref, head_ref, gaps_ref,
                normed_ref, act_ref, dt_ref, cs_ref, state_ref, logs_ref, first_ref, coef_first_ref,
                coef_ref, rows_ref, upright_ref, shift_ref, weighted_ref):
    depth, length = x_ref.shape
    heads = dt_ref.shape[0]
    inner, state_width = state_ref.shape
    head_dim = inner // heads
    normed_columns(x_ref, vec_ref, normed_ref)
    normed = normed_ref[...]
    raw = jnp.dot(w_step_ref[...], normed, preferred_element_type=f32)
    raw = raw + head_ref[:, 0:1]
    dt = jnp.maximum(raw, 0.0) + jnp.log1p(jnp.exp(-jnp.abs(raw)))
    dt_ref[...] = dt
    cs = running_sum(-head_ref[:, 1:2] * dt * gaps_ref[...])
    cs_ref[...] = cs
    coef = jnp.exp(cs[:, length - 1 : length] - cs) * dt
    coef_first = coef[:, 0:EDGE].T[0:EXTRA, :]
    for head in range(heads):
        coef_first_ref[:, head * head_dim : (head + 1) * head_dim] = jnp.broadcast_to(
            coef_first[:, head : head + 1], (EXTRA, head_dim)
        )
    lane = lax.broadcasted_iota(jnp.int32, coef.shape, 1)
    coef_ref[...] = jnp.where(lane >= EXTRA, coef, 0.0)
    total = jnp.broadcast_to(cs[:, length - 1 : length], (heads, state_width))
    pack_logs(total, rows_ref)
    logs_ref[...] = rows_ref[...].astype(bf16)

    for at in range(0, depth, EDGE):
        upright_ref[:, at : at + EDGE] = normed_ref[at : at + EDGE, :].astype(f32).T.astype(bf16)
    shift_ref[0:EXTRA, :] = jnp.zeros((EXTRA, shift_ref.shape[1]), f32)
    upright = upright_ref[...]

    def act_of(at, step):
        cols = slice(at, at + step)
        whole = jnp.dot(upright, w_xbc_ref[:, cols], preferred_element_type=f32)
        shift_ref[EXTRA:, cols] = whole.astype(bf16).astype(f32)
        conv = vec_ref[BIAS : BIAS + 1, cols]
        for tap in range(BIAS):
            first = EXTRA - (BIAS - 1 - tap)
            conv = conv + vec_ref[tap : tap + 1, cols] * shift_ref[first : first + length, cols]
        act = conv * jax.nn.sigmoid(conv)
        turned = act.T.astype(bf16)
        act_ref[at : at + step, :] = turned
        return act.astype(bf16), turned

    b, _ = act_of(inner, state_width)
    act_of(inner + state_width, state_width)
    step = 2 * head_dim
    for at in range(0, inner, step):
        act = act_of(at, step)[1].astype(f32)
        head = at // head_dim
        coef = jnp.concatenate(
            [jnp.broadcast_to(coef_ref[h : h + 1, :], (head_dim, length)) for h in (head, head + 1)],
            axis=0,
        )
        weighted_ref[at : at + step, :] = (act * coef).astype(bf16)
    state_ref[...] = jnp.dot(weighted_ref[...], b, preferred_element_type=f32)
    first_ref[...] = shift_ref[EXTRA : 2 * EXTRA, :]


def edge_kernel(edge_a_ref, edge_b_ref, first_ref, vec_ref, w_xbc_ref, coef_ref, state_ref, logs_ref,
                send_ref, act_ref, rows_ref):
    inner, state_width = state_ref.shape
    depth = edge_a_ref.shape[0]
    x = (edge_a_ref[...].astype(f32) + edge_b_ref[...].astype(f32)).T[EDGE - EXTRA :, :]
    scale = lax.rsqrt(jnp.mean(x * x, axis=1, keepdims=True) + epsilon)
    normed = (x * scale * vec_ref[GAIN_IN : GAIN_IN + 1, :depth]).astype(bf16)
    before = jnp.dot(normed, w_xbc_ref[...], preferred_element_type=f32)
    rows_ref[0:EXTRA, :] = before.astype(bf16).astype(f32)
    rows_ref[EXTRA:, :] = first_ref[...]
    conv = vec_ref[BIAS : BIAS + 1, :]
    for tap in range(BIAS):
        at = EXTRA - (BIAS - 1 - tap)
        conv = conv + vec_ref[tap : tap + 1, :] * rows_ref[at : at + EXTRA, :]
    act = (conv * jax.nn.sigmoid(conv)).astype(bf16).astype(f32)
    act_ref[...] = act
    weighted = (act[:, :inner] * coef_ref[...]).astype(bf16).astype(f32)
    none = jnp.zeros_like(weighted)
    weighted = jnp.concatenate([weighted, none], axis=0).astype(bf16)
    b = act[:, inner : inner + state_width]
    b = jnp.concatenate([b, jnp.zeros_like(b)], axis=0).astype(bf16)
    size = inner // GROUP
    whole = state_ref[...] + contract(weighted, b, ((0,), (0,)))
    for part in range(GROUP):
        send_ref[part, 0:size, :] = whole[part * size : (part + 1) * size, :].astype(bf16)
        send_ref[part, size : size + EXTRA, :] = logs_ref[part * EXTRA : (part + 1) * EXTRA, :]


def pack_logs(total, rows_ref):
    heads = total.shape[0]
    own = rows_ref.shape[0] // EXTRA
    own = heads // own
    rows_ref[...] = jnp.zeros_like(rows_ref)
    rest = total
    for piece in range(3):
        part = rest.astype(bf16).astype(f32)
        rest = rest - part
        for head in range(heads):
            at = head // own * EXTRA + head % own * 3 + piece
            rows_ref[at : at + 1, :] = part[head : head + 1, :]


def read_logs(rows, own):
    rows = rows.astype(f32)
    return [
        rows[3 * h : 3 * h + 1, :] + rows[3 * h + 1 : 3 * h + 2, :] + rows[3 * h + 2 : 3 * h + 3, :]
        for h in range(own)
    ]


def prefix_kernel(own, states_ref, send_ref, rows_ref):
    size = send_ref.shape[0] - EXTRA
    head_dim = size // own
    width = send_ref.shape[1]
    logs = [read_logs(states_ref[m, size : size + EXTRA, :], own) for m in range(GROUP)]
    for h in range(own):
        rows = slice(h * head_dim, (h + 1) * head_dim)
        state = jnp.zeros((head_dim, width), f32)
        for m in range(GROUP):
            state = jnp.exp(logs[m][h]) * state + states_ref[m, rows, :].astype(f32)
        send_ref[rows, :] = state.astype(bf16)
    total = [sum(logs[m][h] for m in range(GROUP)) for h in range(own)]
    pack_logs(jnp.concatenate(total, axis=0), rows_ref)
    send_ref[size : size + EXTRA, :] = rows_ref[...].astype(bf16)


def join_kernel(own, total_ref, earlier_ref, send_ref):
    size = send_ref.shape[0] - EXTRA
    head_dim = size // own
    jumps = read_logs(total_ref[size:, :], own)
    for h in range(own):
        rows = slice(h * head_dim, (h + 1) * head_dim)
        state = jnp.exp(jumps[h]) * earlier_ref[rows, :].astype(f32)
        send_ref[rows, :] = (total_ref[rows, :].astype(f32) + state).astype(bf16)
    send_ref[size:, :] = jnp.zeros((EXTRA, send_ref.shape[1]), bf16)


def combine_kernel(own, states_ref, near_ref, after_ref, middle_ref, far_ref, back_ref):
    size = back_ref.shape[1]
    head_dim = size // own
    logs = [read_logs(states_ref[m, size : size + EXTRA, :], own) for m in range(GROUP)]
    near_jumps = read_logs(near_ref[size:, :], own)
    middle_jumps = read_logs(middle_ref[size:, :], own)
    for h in range(own):
        rows = slice(h * head_dim, (h + 1) * head_dim)
        state = middle_ref[rows, :].astype(f32)
        state = state + jnp.exp(middle_jumps[h]) * far_ref[rows, :].astype(f32)
        state = near_ref[rows, :].astype(f32) + jnp.exp(near_jumps[h]) * state
        state = state + after_ref[rows, :].astype(f32)
        for m in range(GROUP):
            back_ref[m, rows, :] = state.astype(bf16)
            state = jnp.exp(logs[m][h]) * state + states_ref[m, rows, :].astype(f32)


def inside_kernel(normed_ref, w_gate_ref, main_ref, first_ref, dt_ref, cs_ref,
                  gate_ref, y_ref, query_ref, act_ref, scores_ref, mix_ref, weight_ref, sem):
    fetches = fetch_rows(w_gate_ref, weight_ref, sem)
    heads, length = dt_ref.shape
    inner = y_ref.shape[0]
    lane = lax.broadcasted_iota(jnp.int32, (EDGE, EDGE), 1)
    rest = jnp.zeros((EDGE - EXTRA, EDGE), f32)
    for at in range(0, act_ref.shape[0], EDGE):
        rows = slice(at, at + EDGE)
        first = jnp.concatenate([first_ref[:, rows], rest], axis=0).T
        kept = main_ref[rows, 0:EDGE].astype(f32)
        act_ref[rows, 0:EDGE] = jnp.where(lane < EXTRA, first, kept).astype(bf16)
        act_ref[rows, EDGE:] = main_ref[rows, EDGE:]
    head_dim = inner // heads
    state_width = (act_ref.shape[0] - inner) // 2
    query_ref[...] = act_ref[inner + state_width :, :]
    scores_ref[...] = contract(
        act_ref[inner : inner + state_width, :], act_ref[inner + state_width :, :], ((0,), (0,))
    )
    cs_col = cs_ref[...].T
    dt_col = dt_ref[...].T
    half = length // 2
    mix_ref[...] = jnp.zeros_like(mix_ref)
    later = lax.broadcasted_iota(jnp.int32, (half, half), 1)
    early = lax.broadcasted_iota(jnp.int32, (half, half), 0)
    keep = later >= early
    for h in range(heads):
        for s in (0, half):
            cs_s = jnp.broadcast_to(cs_col[s : s + half, h : h + 1], (half, half))
            dt_s = jnp.broadcast_to(dt_col[s : s + half, h : h + 1], (half, half))
            for t in range(s, length, half):
                diff = cs_ref[h : h + 1, t : t + half] - cs_s
                if s == t:
                    diff = jnp.where(keep, diff, -jnp.inf)
                mix_ref[s : s + half, t : t + half] = (
                    scores_ref[s : s + half, t : t + half] * jnp.exp(diff) * dt_s
                ).astype(bf16)
        rows = slice(h * head_dim, (h + 1) * head_dim)
        y_ref[rows, :] = jnp.dot(act_ref[rows, :], mix_ref[...], preferred_element_type=f32)
    for fetch in fetches:
        fetch.wait()
    normed = normed_ref[...]
    step = 4 * head_dim
    for at in range(0, inner, step):
        gate = contract(weight_ref[:, at : at + step], normed, ((0,), (0,)))
        gate_ref[at : at + step, :] = gate.astype(bf16)


def output_kernel(carried_ref, query_ref, cs_ref, gate_ref, y_ref, vec_ref, w_out_ref,
                  out_ref, gated_ref, normed_ref):
    inner, length = y_ref.shape
    gated_ref[...] = jnp.dot(carried_ref[...], query_ref[...], preferred_element_type=f32)
    heads = cs_ref.shape[0]
    head_dim = inner // heads
    grown = jnp.exp(cs_ref[...])
    total = jnp.zeros((1, length), f32)
    for h in range(heads):
        rows = slice(h * head_dim, (h + 1) * head_dim)
        gate = gate_ref[rows, :].astype(f32)
        gated = y_ref[rows, :] + grown[h : h + 1, :] * gated_ref[rows, :]
        gated = gated * (gate * jax.nn.sigmoid(gate))
        gated_ref[rows, :] = gated
        total = total + jnp.sum(gated * gated, axis=0, keepdims=True)
    scale = lax.rsqrt(total / inner + epsilon)
    for at in range(0, inner, EDGE):
        gain = columns_of(vec_ref, at)[:, GAIN_OUT : GAIN_OUT + 1]
        normed_ref[at : at + EDGE, :] = (gated_ref[at : at + EDGE, :] * scale * gain).astype(bf16)
    out_ref[...] = contract(normed_ref[...], w_out_ref[...], ((0,), (0,))).astype(bf16)


def call(kernel, outs, scratch, *args, fetched=(), scalars=0, aliases={}):
    vmem = pl.BlockSpec(memory_space=pltpu.VMEM)
    left = pl.BlockSpec(memory_space=pltpu.HBM)
    single = not isinstance(outs, list)
    args = [
        pltpu.with_memory_space_constraint(a, pltpu.HBM) if at in fetched else a
        for at, a in enumerate(args)
    ]
    return pl.pallas_call(
        kernel,
        out_shape=outs,
        in_specs=[
            pl.BlockSpec(memory_space=pltpu.SMEM)
            if at < scalars
            else left
            if at in fetched
            else vmem
            for at in range(len(args))
        ],
        input_output_aliases=aliases,
        out_specs=vmem if single else [vmem] * len(outs),
        scratch_shapes=scratch,
        compiler_params=pltpu.CompilerParams(vmem_limit_bytes=12 << 20),
    )(*args)


def local(
    columns,
    gaps,
    norm_in,
    w_gate,
    w_xbc,
    w_step,
    step_bias,
    conv_weight,
    conv_bias,
    rates,
    norm_out,
    w_out,
):
    length = columns.shape[1]
    depth, inner = w_gate.shape
    heads = w_step.shape[1]
    width = w_xbc.shape[1]
    state_width = (width - inner) // 2
    own = heads // GROUP
    size = inner // GROUP
    shape = jax.ShapeDtypeStruct

    rows = [conv_weight, conv_bias[None], norm_in[None], norm_out[None]]
    vec = jnp.concatenate([jnp.pad(r, ((0, 0), (0, width - r.shape[1]))) for r in rows])
    vec = jnp.pad(vec, ((0, 8 - vec.shape[0]), (0, 0)))
    head = jnp.stack([step_bias, rates], axis=1)

    whole = lax.all_to_all(columns, "table", split_axis=0, concat_axis=2, tiled=True)
    staged = [w_xbc, w_step.T, gaps]
    staged = call(
        stage_kernel,
        [shape(a.shape, a.dtype) for a in staged],
        [pltpu.SemaphoreType.DMA((len(staged),))],
        *staged,
        fetched=range(len(staged)),
    )
    whole, vec, head, *staged = lax.optimization_barrier((whole, vec, head, *staged))
    w_xbc, w_step_t, gaps = staged
    x = whole.reshape(length, depth).T
    edge = x[:, length - EDGE :]
    places = lax.axis_size("seq")
    turn = (lax.axis_index("seq") % 2).astype(jnp.int32)[None]
    shapes = [
        shape((depth, length), bf16),
        shape((width, length), bf16),
        shape((heads, length), f32),
        shape((heads, length), f32),
        shape((inner, state_width), f32),
        shape((GROUP * EXTRA, state_width), bf16),
        shape((EXTRA, width), f32),
        shape((EXTRA, inner), f32),
    ]
    scratch = [
        pltpu.VMEM((heads, length), f32),
        pltpu.VMEM((GROUP * EXTRA, state_width), f32),
        pltpu.VMEM((length, depth), bf16),
        pltpu.VMEM((EXTRA + length, width), f32),
        pltpu.VMEM((inner, length), bf16),
    ]
    operands = [turn, x, vec, w_xbc, w_step_t, head, gaps]
    results = call(
        functools.partial(main_kernel, before=False), shapes, scratch, *operands, scalars=1
    )
    edge, *results = lax.optimization_barrier((edge, *results))
    edge_a = passed_along(edge, "seq", 1, range(1, places, 2))
    edge_b = passed_along(edge, "seq", 1, range(0, places, 2))
    results = call(
        functools.partial(main_kernel, before=True),
        shapes,
        scratch,
        *operands,
        *results,
        scalars=1,
        aliases={len(operands) + at: at for at in range(len(shapes))},
    )
    normed, act, dt, cs, state, logs, first, coef_first = results
    send, act_first = call(
        edge_kernel,
        [shape((GROUP, size + EXTRA, state_width), bf16), shape((EXTRA, width), f32)],
        [pltpu.VMEM((2 * EXTRA, width), f32)],
        edge_b, edge_a, first, vec, w_xbc, coef_first, state, logs,
    )
    states = within_groups(send)
    total = call(
        functools.partial(prefix_kernel, own),
        shape((size + EXTRA, state_width), bf16),
        [pltpu.VMEM((EXTRA, state_width), f32)],
        states,
    )
    assert lax.axis_size("seq") == 4 * GROUP
    near = passed_along(total, "seq", GROUP, members(0, 2))
    middle = passed_along(total, "seq", 2 * GROUP, members(1))
    far = passed_along(total, "seq", 3 * GROUP, members(0))
    joined = call(
        functools.partial(join_kernel, own),
        shape((size + EXTRA, state_width), bf16),
        [],
        total, near,
    )
    after = passed_along(joined, "seq", GROUP, members(1))
    back = call(
        functools.partial(combine_kernel, own),
        shape((GROUP, size, state_width), bf16),
        [],
        states, near, after, middle, far,
    )
    back, act = lax.optimization_barrier((back, act))
    carried = within_groups(back).reshape(inner, state_width)
    gate, y, query = call(
        inside_kernel,
        [
            shape((inner, length), bf16),
            shape((inner, length), f32),
            shape((state_width, length), bf16),
        ],
        [
            pltpu.VMEM((width, length), bf16),
            pltpu.VMEM((length, length), f32),
            pltpu.VMEM((length, length), bf16),
            pltpu.VMEM((depth, inner), bf16),
            pltpu.SemaphoreType.DMA((PARTS,)),
        ],
        normed, w_gate, act, act_first, dt, cs,
        fetched=(1,),
    )
    gate, y, query, w_out = lax.optimization_barrier((gate, y, query, w_out))
    (w_out,) = call(
        stage_kernel,
        [shape(w_out.shape, w_out.dtype)],
        [pltpu.SemaphoreType.DMA((1,))],
        w_out,
        fetched=(0,),
    )
    out = call(
        output_kernel,
        shape((length, w_out.shape[1]), bf16),
        [
            pltpu.VMEM((inner, length), f32),
            pltpu.VMEM((inner, length), bf16),
        ],
        carried, query, cs, gate, y, vec, w_out,
    )
    return out[None]


def solution(mesh):
    in_specs = (
        P(None, "seq", "table"),
        P("table", "seq"),
        P(),
        P(),
        P(),
        P(),
        P(),
        P(),
        P(),
        P(),
        P(),
        P(),
    )
    out_specs = P("table", "seq", None)
    return jax.shard_map(local, mesh=mesh, in_specs=in_specs, out_specs=out_specs, check_vma=False)
```

```python
import functools

import jax
import jax.numpy as jnp
from jax import lax
from jax.experimental import pallas as pl
from jax.experimental.pallas import tpu as pltpu
from jax.sharding import PartitionSpec as P

GROUP = 8
EDGE = 128
EXTRA = 8
PARTS = 4
BIAS, GAIN_IN, GAIN_OUT = 4, 5, 6
epsilon = 1e-05
f32 = jnp.float32
bf16 = jnp.bfloat16


def passed_along(block, axis, distance, senders=None):
    devices = range(lax.axis_size(axis))
    route = [(i, i + distance) for i in senders or devices if i + distance in devices]
    return lax.ppermute(block, axis, route)


def members(*groups):
    return [g * GROUP + i for g in groups for i in range(GROUP)]


def within_groups(blocks):
    count = lax.axis_size("seq") // GROUP
    groups = [[g * GROUP + i for i in range(GROUP)] for g in range(count)]
    return lax.all_to_all(
        blocks, "seq", split_axis=0, concat_axis=0, tiled=True, axis_index_groups=groups
    )


def fetch_rows(source, target, sems):
    count = sems.shape[0]
    step = source.shape[0] // count
    copies = [
        pltpu.make_async_copy(
            source.at[at * step : (at + 1) * step], target.at[at * step : (at + 1) * step], sems.at[at]
        )
        for at in range(count)
    ]
    for copy in copies:
        copy.start()
    return copies


def contract(a, b, dims):
    return lax.dot_general(a, b, (dims, ((), ())), preferred_element_type=f32)


def columns_of(vec_ref, at):
    return vec_ref[:, at : at + EDGE].T


def normed_columns(x_ref, vec_ref, out_ref):
    depth, length = x_ref.shape
    total = jnp.zeros((1, length), f32)
    for at in range(0, depth, 64):
        x = x_ref[at : at + 64, :].astype(f32)
        total = total + jnp.sum(x * x, axis=0, keepdims=True)
    scale = lax.rsqrt(total / depth + epsilon)
    for at in range(0, depth, EDGE):
        gain = columns_of(vec_ref, at)[:, GAIN_IN : GAIN_IN + 1]
        x = x_ref[at : at + EDGE, :].astype(f32)
        out_ref[at : at + EDGE, :] = (x * scale * gain).astype(bf16)


def running_sum(values):
    length = values.shape[1]
    lane = lax.broadcasted_iota(jnp.int32, values.shape, 1)
    reach = 1
    while reach < length:
        values = values + jnp.where(lane >= reach, pltpu.roll(values, reach, axis=1), 0.0)
        reach *= 2
    return values


def stage_kernel(*refs):
    count = len(refs) // 2
    sems = refs[-1]
    copies = [
        pltpu.make_async_copy(refs[at], refs[count + at], sems.at[at]) for at in range(count)
    ]
    for copy in copies:
        copy.start()
    for copy in copies:
        copy.wait()


def main_kernel(x_ref, vec_ref, w_xbc_ref, w_step_ref, head_ref, gaps_ref,
                normed_ref, act_ref, dt_ref, cs_ref, state_ref, logs_ref, first_ref, coef_first_ref,
                coef_ref, rows_ref, upright_ref, shift_ref, weighted_ref):
    depth, length = x_ref.shape
    heads = dt_ref.shape[0]
    inner, state_width = state_ref.shape
    head_dim = inner // heads
    normed_columns(x_ref, vec_ref, normed_ref)
    normed = normed_ref[...]
    raw = jnp.dot(w_step_ref[...], normed, preferred_element_type=f32)
    raw = raw + head_ref[:, 0:1]
    dt = jnp.maximum(raw, 0.0) + jnp.log1p(jnp.exp(-jnp.abs(raw)))
    dt_ref[...] = dt
    cs = running_sum(-head_ref[:, 1:2] * dt * gaps_ref[...])
    cs_ref[...] = cs
    coef = jnp.exp(cs[:, length - 1 : length] - cs) * dt
    coef_first = coef[:, 0:EDGE].T[0:EXTRA, :]
    for head in range(heads):
        coef_first_ref[:, head * head_dim : (head + 1) * head_dim] = jnp.broadcast_to(
            coef_first[:, head : head + 1], (EXTRA, head_dim)
        )
    lane = lax.broadcasted_iota(jnp.int32, coef.shape, 1)
    coef_ref[...] = jnp.where(lane >= EXTRA, coef, 0.0)
    total = jnp.broadcast_to(cs[:, length - 1 : length], (heads, state_width))
    pack_logs(total, rows_ref)
    logs_ref[...] = rows_ref[...].astype(bf16)

    for at in range(0, depth, EDGE):
        upright_ref[:, at : at + EDGE] = normed_ref[at : at + EDGE, :].astype(f32).T.astype(bf16)
    shift_ref[0:EXTRA, :] = jnp.zeros((EXTRA, shift_ref.shape[1]), f32)
    upright = upright_ref[...]

    def act_of(at, step):
        cols = slice(at, at + step)
        whole = jnp.dot(upright, w_xbc_ref[:, cols], preferred_element_type=f32)
        shift_ref[EXTRA:, cols] = whole.astype(bf16).astype(f32)
        conv = vec_ref[BIAS : BIAS + 1, cols]
        for tap in range(BIAS):
            first = EXTRA - (BIAS - 1 - tap)
            conv = conv + vec_ref[tap : tap + 1, cols] * shift_ref[first : first + length, cols]
        act = conv * jax.nn.sigmoid(conv)
        turned = act.T.astype(bf16)
        act_ref[at : at + step, :] = turned
        return act.astype(bf16), turned

    b, _ = act_of(inner, state_width)
    act_of(inner + state_width, state_width)
    step = 2 * head_dim
    for at in range(0, inner, step):
        act = act_of(at, step)[1].astype(f32)
        head = at // head_dim
        coef = jnp.concatenate(
            [jnp.broadcast_to(coef_ref[h : h + 1, :], (head_dim, length)) for h in (head, head + 1)],
            axis=0,
        )
        weighted_ref[at : at + step, :] = (act * coef).astype(bf16)
    state_ref[...] = jnp.dot(weighted_ref[...], b, preferred_element_type=f32)
    first_ref[...] = shift_ref[EXTRA : 2 * EXTRA, :]


def edge_kernel(edge_ref, first_ref, vec_ref, w_xbc_ref, coef_ref, state_ref, logs_ref,
                send_ref, act_ref, rows_ref):
    inner, state_width = state_ref.shape
    depth = edge_ref.shape[0]
    x = edge_ref[...].astype(f32).T[EDGE - EXTRA :, :]
    scale = lax.rsqrt(jnp.mean(x * x, axis=1, keepdims=True) + epsilon)
    normed = (x * scale * vec_ref[GAIN_IN : GAIN_IN + 1, :depth]).astype(bf16)
    before = jnp.dot(normed, w_xbc_ref[...], preferred_element_type=f32)
    rows_ref[0:EXTRA, :] = before.astype(bf16).astype(f32)
    rows_ref[EXTRA:, :] = first_ref[...]
    conv = vec_ref[BIAS : BIAS + 1, :]
    for tap in range(BIAS):
        at = EXTRA - (BIAS - 1 - tap)
        conv = conv + vec_ref[tap : tap + 1, :] * rows_ref[at : at + EXTRA, :]
    act = (conv * jax.nn.sigmoid(conv)).astype(bf16).astype(f32)
    act_ref[...] = act
    weighted = (act[:, :inner] * coef_ref[...]).astype(bf16).astype(f32)
    none = jnp.zeros_like(weighted)
    weighted = jnp.concatenate([weighted, none], axis=0).astype(bf16)
    b = act[:, inner : inner + state_width]
    b = jnp.concatenate([b, jnp.zeros_like(b)], axis=0).astype(bf16)
    size = inner // GROUP
    whole = state_ref[...] + contract(weighted, b, ((0,), (0,)))
    for part in range(GROUP):
        send_ref[part, 0:size, :] = whole[part * size : (part + 1) * size, :].astype(bf16)
        send_ref[part, size : size + EXTRA, :] = logs_ref[part * EXTRA : (part + 1) * EXTRA, :]


def pack_logs(total, rows_ref):
    heads = total.shape[0]
    own = rows_ref.shape[0] // EXTRA
    own = heads // own
    rows_ref[...] = jnp.zeros_like(rows_ref)
    rest = total
    for piece in range(3):
        part = rest.astype(bf16).astype(f32)
        rest = rest - part
        for head in range(heads):
            at = head // own * EXTRA + head % own * 3 + piece
            rows_ref[at : at + 1, :] = part[head : head + 1, :]


def read_logs(rows, own):
    rows = rows.astype(f32)
    return [
        rows[3 * h : 3 * h + 1, :] + rows[3 * h + 1 : 3 * h + 2, :] + rows[3 * h + 2 : 3 * h + 3, :]
        for h in range(own)
    ]


def prefix_kernel(own, states_ref, send_ref, rows_ref):
    size = send_ref.shape[0] - EXTRA
    head_dim = size // own
    width = send_ref.shape[1]
    logs = [read_logs(states_ref[m, size : size + EXTRA, :], own) for m in range(GROUP)]
    for h in range(own):
        rows = slice(h * head_dim, (h + 1) * head_dim)
        state = jnp.zeros((head_dim, width), f32)
        for m in range(GROUP):
            state = jnp.exp(logs[m][h]) * state + states_ref[m, rows, :].astype(f32)
        send_ref[rows, :] = state.astype(bf16)
    total = [sum(logs[m][h] for m in range(GROUP)) for h in range(own)]
    pack_logs(jnp.concatenate(total, axis=0), rows_ref)
    send_ref[size : size + EXTRA, :] = rows_ref[...].astype(bf16)


def join_kernel(own, total_ref, earlier_ref, send_ref, again_ref, same_ref):
    same_ref[...] = total_ref[...]
    size = send_ref.shape[0] - EXTRA
    head_dim = size // own
    jumps = read_logs(total_ref[size:, :], own)
    for h in range(own):
        rows = slice(h * head_dim, (h + 1) * head_dim)
        state = jnp.exp(jumps[h]) * earlier_ref[rows, :].astype(f32)
        send_ref[rows, :] = (total_ref[rows, :].astype(f32) + state).astype(bf16)
    send_ref[size:, :] = jnp.zeros((EXTRA, send_ref.shape[1]), bf16)
    again_ref[...] = send_ref[...]


def combine_kernel(own, states_ref, first_ref, after_b_ref, after_a_ref, near_ref, back_ref):
    size = back_ref.shape[1]
    head_dim = size // own
    logs = [read_logs(states_ref[m, size : size + EXTRA, :], own) for m in range(GROUP)]
    jumps = read_logs(near_ref[size:, :], own)
    for h in range(own):
        rows = slice(h * head_dim, (h + 1) * head_dim)
        after = after_a_ref[rows, :].astype(f32) + after_b_ref[rows, :].astype(f32)
        state = first_ref[rows, :].astype(f32) + near_ref[rows, :].astype(f32)
        state = state + jnp.exp(jumps[h]) * after
        for m in range(GROUP):
            back_ref[m, rows, :] = state.astype(bf16)
            state = jnp.exp(logs[m][h]) * state + states_ref[m, rows, :].astype(f32)


def inside_kernel(normed_ref, w_gate_ref, main_ref, first_ref, dt_ref, cs_ref,
                  grown_ref, y_ref, query_ref, act_ref, scores_ref, mix_ref, weight_ref, sem):
    fetches = fetch_rows(w_gate_ref, weight_ref, sem)
    heads, length = dt_ref.shape
    inner = y_ref.shape[0]
    lane = lax.broadcasted_iota(jnp.int32, (EDGE, EDGE), 1)
    rest = jnp.zeros((EDGE - EXTRA, EDGE), f32)
    for at in range(0, act_ref.shape[0], EDGE):
        rows = slice(at, at + EDGE)
        first = jnp.concatenate([first_ref[:, rows], rest], axis=0).T
        kept = main_ref[rows, 0:EDGE].astype(f32)
        act_ref[rows, 0:EDGE] = jnp.where(lane < EXTRA, first, kept).astype(bf16)
        act_ref[rows, EDGE:] = main_ref[rows, EDGE:]
    head_dim = inner // heads
    state_width = (act_ref.shape[0] - inner) // 2
    query_ref[...] = act_ref[inner + state_width :, :]
    scores_ref[...] = contract(
        act_ref[inner : inner + state_width, :], act_ref[inner + state_width :, :], ((0,), (0,))
    )
    cs_col = cs_ref[...].T
    dt_col = dt_ref[...].T
    half = length // 2
    mix_ref[...] = jnp.zeros_like(mix_ref)
    later = lax.broadcasted_iota(jnp.int32, (half, half), 1)
    early = lax.broadcasted_iota(jnp.int32, (half, half), 0)
    keep = later >= early
    for h in range(heads):
        for s in (0, half):
            cs_s = jnp.broadcast_to(cs_col[s : s + half, h : h + 1], (half, half))
            dt_s = jnp.broadcast_to(dt_col[s : s + half, h : h + 1], (half, half))
            for t in range(s, length, half):
                diff = cs_ref[h : h + 1, t : t + half] - cs_s
                if s == t:
                    diff = jnp.where(keep, diff, -jnp.inf)
                mix_ref[s : s + half, t : t + half] = (
                    scores_ref[s : s + half, t : t + half] * jnp.exp(diff) * dt_s
                ).astype(bf16)
        rows = slice(h * head_dim, (h + 1) * head_dim)
        y_ref[rows, :] = jnp.dot(act_ref[rows, :], mix_ref[...], preferred_element_type=f32)
    for fetch in fetches:
        fetch.wait()
    normed = normed_ref[...]
    step = 4 * head_dim
    for at in range(0, inner, step):
        gate = contract(weight_ref[:, at : at + step], normed, ((0,), (0,)))
        gate = gate.astype(bf16).astype(f32)
        gate = gate * jax.nn.sigmoid(gate)
        for h in range(at // head_dim, (at + step) // head_dim):
            rows = slice(h * head_dim, (h + 1) * head_dim)
            own = gate[h * head_dim - at : (h + 1) * head_dim - at, :]
            grown_ref[rows, :] = (jnp.exp(cs_ref[h : h + 1, :]) * own).astype(bf16)
            y_ref[rows, :] = y_ref[rows, :] * own


def output_kernel(carried_ref, query_ref, grown_ref, y_ref, vec_ref, w_out_ref,
                  out_ref, gated_ref, normed_ref):
    inner, length = y_ref.shape
    gated_ref[...] = jnp.dot(carried_ref[...], query_ref[...], preferred_element_type=f32)
    total = jnp.zeros((1, length), f32)
    for at in range(0, inner, EDGE):
        rows = slice(at, at + EDGE)
        gated = y_ref[rows, :] + grown_ref[rows, :].astype(f32) * gated_ref[rows, :]
        gated_ref[rows, :] = gated
        total = total + jnp.sum(gated * gated, axis=0, keepdims=True)
    scale = lax.rsqrt(total / inner + epsilon)
    for at in range(0, inner, EDGE):
        gain = columns_of(vec_ref, at)[:, GAIN_OUT : GAIN_OUT + 1]
        normed_ref[at : at + EDGE, :] = (gated_ref[at : at + EDGE, :] * scale * gain).astype(bf16)
    out_ref[...] = contract(normed_ref[...], w_out_ref[...], ((0,), (0,))).astype(bf16)


def call(kernel, outs, scratch, *args, fetched=()):
    vmem = pl.BlockSpec(memory_space=pltpu.VMEM)
    left = pl.BlockSpec(memory_space=pltpu.HBM)
    single = not isinstance(outs, list)
    args = [
        pltpu.with_memory_space_constraint(a, pltpu.HBM) if at in fetched else a
        for at, a in enumerate(args)
    ]
    return pl.pallas_call(
        kernel,
        out_shape=outs,
        in_specs=[left if at in fetched else vmem for at in range(len(args))],
        out_specs=vmem if single else [vmem] * len(outs),
        scratch_shapes=scratch,
        compiler_params=pltpu.CompilerParams(vmem_limit_bytes=12 << 20),
    )(*args)


def local(
    columns,
    gaps,
    norm_in,
    w_gate,
    w_xbc,
    w_step,
    step_bias,
    conv_weight,
    conv_bias,
    rates,
    norm_out,
    w_out,
):
    length = columns.shape[1]
    depth, inner = w_gate.shape
    heads = w_step.shape[1]
    width = w_xbc.shape[1]
    state_width = (width - inner) // 2
    own = heads // GROUP
    size = inner // GROUP
    shape = jax.ShapeDtypeStruct

    rows = [conv_weight, conv_bias[None], norm_in[None], norm_out[None]]
    vec = jnp.concatenate([jnp.pad(r, ((0, 0), (0, width - r.shape[1]))) for r in rows])
    vec = jnp.pad(vec, ((0, 8 - vec.shape[0]), (0, 0)))
    head = jnp.stack([step_bias, rates], axis=1)

    whole = lax.all_to_all(columns, "table", split_axis=0, concat_axis=2, tiled=True)
    staged = [w_xbc, w_step.T, gaps]
    staged = call(
        stage_kernel,
        [shape(a.shape, a.dtype) for a in staged],
        [pltpu.SemaphoreType.DMA((len(staged),))],
        *staged,
        fetched=range(len(staged)),
    )
    whole, vec, head, *staged = lax.optimization_barrier((whole, vec, head, *staged))
    w_xbc, w_step_t, gaps = staged
    x = whole.reshape(length, depth).T
    edge = passed_along(x[:, length - EDGE :], "seq", 1)
    normed, act, dt, cs, state, logs, first, coef_first = call(
        main_kernel,
        [
            shape((depth, length), bf16),
            shape((width, length), bf16),
            shape((heads, length), f32),
            shape((heads, length), f32),
            shape((inner, state_width), f32),
            shape((GROUP * EXTRA, state_width), bf16),
            shape((EXTRA, width), f32),
            shape((EXTRA, inner), f32),
        ],
        [
            pltpu.VMEM((heads, length), f32),
            pltpu.VMEM((GROUP * EXTRA, state_width), f32),
            pltpu.VMEM((length, depth), bf16),
            pltpu.VMEM((EXTRA + length, width), f32),
            pltpu.VMEM((inner, length), bf16),
        ],
        x, vec, w_xbc, w_step_t, head, gaps,
    )
    send, act_first = call(
        edge_kernel,
        [shape((GROUP, size + EXTRA, state_width), bf16), shape((EXTRA, width), f32)],
        [pltpu.VMEM((2 * EXTRA, width), f32)],
        edge, first, vec, w_xbc, coef_first, state, logs,
    )
    states = within_groups(send)
    total = call(
        functools.partial(prefix_kernel, own),
        shape((size + EXTRA, state_width), bf16),
        [pltpu.VMEM((EXTRA, state_width), f32)],
        states,
    )
    assert lax.axis_size("seq") == 4 * GROUP
    first = passed_along(total, "seq", GROUP, members(0))
    joined, again, same = call(
        functools.partial(join_kernel, own),
        [shape((size + EXTRA, state_width), bf16)] * 3,
        [],
        total, first,
    )
    after_b = passed_along(joined, "seq", 2 * GROUP, members(1))
    after_a = passed_along(again, "seq", GROUP, members(1))
    near = passed_along(same, "seq", GROUP, members(2))
    back = call(
        functools.partial(combine_kernel, own),
        shape((GROUP, size, state_width), bf16),
        [],
        states, first, after_b, after_a, near,
    )
    back, act = lax.optimization_barrier((back, act))
    carried = within_groups(back).reshape(inner, state_width)
    grown, y, query = call(
        inside_kernel,
        [
            shape((inner, length), bf16),
            shape((inner, length), f32),
            shape((state_width, length), bf16),
        ],
        [
            pltpu.VMEM((width, length), bf16),
            pltpu.VMEM((length, length), f32),
            pltpu.VMEM((length, length), bf16),
            pltpu.VMEM((depth, inner), bf16),
            pltpu.SemaphoreType.DMA((PARTS,)),
        ],
        normed, w_gate, act, act_first, dt, cs,
        fetched=(1,),
    )
    grown, y, query, w_out = lax.optimization_barrier((grown, y, query, w_out))
    (w_out,) = call(
        stage_kernel,
        [shape(w_out.shape, w_out.dtype)],
        [pltpu.SemaphoreType.DMA((1,))],
        w_out,
        fetched=(0,),
    )
    out = call(
        output_kernel,
        shape((length, w_out.shape[1]), bf16),
        [
            pltpu.VMEM((inner, length), f32),
            pltpu.VMEM((inner, length), bf16),
        ],
        carried, query, grown, y, vec, w_out,
    )
    return out[None]


def solution(mesh):
    in_specs = (
        P(None, "seq", "table"),
        P("table", "seq"),
        P(),
        P(),
        P(),
        P(),
        P(),
        P(),
        P(),
        P(),
        P(),
        P(),
    )
    out_specs = P("table", "seq", None)
    return jax.shard_map(local, mesh=mesh, in_specs=in_specs, out_specs=out_specs, check_vma=False)
```

```python
import functools

import jax
import jax.numpy as jnp
from jax import lax
from jax.experimental import pallas as pl
from jax.experimental.pallas import tpu as pltpu
from jax.sharding import PartitionSpec as P

GROUP = 8
EDGE = 128
EXTRA = 8
PARTS = 4
BIAS, GAIN_IN, GAIN_OUT = 4, 5, 6
epsilon = 1e-05
f32 = jnp.float32
bf16 = jnp.bfloat16


def passed_along(block, axis, distance, senders=None):
    devices = range(lax.axis_size(axis))
    route = [(i, i + distance) for i in senders or devices if i + distance in devices]
    return lax.ppermute(block, axis, route)


def members(*groups):
    return [g * GROUP + i for g in groups for i in range(GROUP)]


def within_groups(blocks):
    count = lax.axis_size("seq") // GROUP
    groups = [[g * GROUP + i for i in range(GROUP)] for g in range(count)]
    return lax.all_to_all(
        blocks, "seq", split_axis=0, concat_axis=0, tiled=True, axis_index_groups=groups
    )


def fetch_rows(source, target, sems):
    count = sems.shape[0]
    step = source.shape[0] // count
    copies = [
        pltpu.make_async_copy(
            source.at[at * step : (at + 1) * step], target.at[at * step : (at + 1) * step], sems.at[at]
        )
        for at in range(count)
    ]
    for copy in copies:
        copy.start()
    return copies


def contract(a, b, dims):
    return lax.dot_general(a, b, (dims, ((), ())), preferred_element_type=f32)


def columns_of(vec_ref, at):
    return vec_ref[:, at : at + EDGE].T


def normed_columns(x_ref, vec_ref, out_ref):
    depth, length = x_ref.shape
    total = jnp.zeros((1, length), f32)
    for at in range(0, depth, 64):
        x = x_ref[at : at + 64, :].astype(f32)
        total = total + jnp.sum(x * x, axis=0, keepdims=True)
    scale = lax.rsqrt(total / depth + epsilon)
    for at in range(0, depth, EDGE):
        gain = columns_of(vec_ref, at)[:, GAIN_IN : GAIN_IN + 1]
        x = x_ref[at : at + EDGE, :].astype(f32)
        out_ref[at : at + EDGE, :] = (x * scale * gain).astype(bf16)


def running_sum(values):
    length = values.shape[1]
    lane = lax.broadcasted_iota(jnp.int32, values.shape, 1)
    reach = 1
    while reach < length:
        values = values + jnp.where(lane >= reach, pltpu.roll(values, reach, axis=1), 0.0)
        reach *= 2
    return values


def stage_kernel(*refs):
    count = len(refs) // 2
    sems = refs[-1]
    copies = [
        pltpu.make_async_copy(refs[at], refs[count + at], sems.at[at]) for at in range(count)
    ]
    for copy in copies:
        copy.start()
    for copy in copies:
        copy.wait()


def main_kernel(x_ref, vec_ref, w_xbc_ref, w_step_ref, head_ref, gaps_ref,
                normed_ref, act_ref, dt_ref, cs_ref, state_ref, logs_ref, first_ref, coef_first_ref,
                coef_ref, rows_ref, upright_ref, shift_ref, weighted_ref):
    depth, length = x_ref.shape
    heads = dt_ref.shape[0]
    inner, state_width = state_ref.shape
    head_dim = inner // heads
    normed_columns(x_ref, vec_ref, normed_ref)
    normed = normed_ref[...]
    raw = jnp.dot(w_step_ref[...], normed, preferred_element_type=f32)
    raw = raw + head_ref[:, 0:1]
    dt = jnp.maximum(raw, 0.0) + jnp.log1p(jnp.exp(-jnp.abs(raw)))
    dt_ref[...] = dt
    cs = running_sum(-head_ref[:, 1:2] * dt * gaps_ref[...])
    cs_ref[...] = cs
    coef = jnp.exp(cs[:, length - 1 : length] - cs) * dt
    coef_first = coef[:, 0:EDGE].T[0:EXTRA, :]
    for head in range(heads):
        coef_first_ref[:, head * head_dim : (head + 1) * head_dim] = jnp.broadcast_to(
            coef_first[:, head : head + 1], (EXTRA, head_dim)
        )
    lane = lax.broadcasted_iota(jnp.int32, coef.shape, 1)
    coef_ref[...] = jnp.where(lane >= EXTRA, coef, 0.0)
    total = jnp.broadcast_to(cs[:, length - 1 : length], (heads, state_width))
    pack_logs(total, rows_ref)
    logs_ref[...] = rows_ref[...].astype(bf16)

    for at in range(0, depth, EDGE):
        upright_ref[:, at : at + EDGE] = normed_ref[at : at + EDGE, :].astype(f32).T.astype(bf16)
    shift_ref[0:EXTRA, :] = jnp.zeros((EXTRA, shift_ref.shape[1]), f32)
    upright = upright_ref[...]

    def act_of(at, step):
        cols = slice(at, at + step)
        whole = jnp.dot(upright, w_xbc_ref[:, cols], preferred_element_type=f32)
        shift_ref[EXTRA:, cols] = whole.astype(bf16).astype(f32)
        conv = vec_ref[BIAS : BIAS + 1, cols]
        for tap in range(BIAS):
            first = EXTRA - (BIAS - 1 - tap)
            conv = conv + vec_ref[tap : tap + 1, cols] * shift_ref[first : first + length, cols]
        act = conv * jax.nn.sigmoid(conv)
        turned = act.T.astype(bf16)
        act_ref[at : at + step, :] = turned
        return act.astype(bf16), turned

    b, _ = act_of(inner, state_width)
    act_of(inner + state_width, state_width)
    step = 2 * head_dim
    for at in range(0, inner, step):
        act = act_of(at, step)[1].astype(f32)
        head = at // head_dim
        coef = jnp.concatenate(
            [jnp.broadcast_to(coef_ref[h : h + 1, :], (head_dim, length)) for h in (head, head + 1)],
            axis=0,
        )
        weighted_ref[at : at + step, :] = (act * coef).astype(bf16)
    state_ref[...] = jnp.dot(weighted_ref[...], b, preferred_element_type=f32)
    first_ref[...] = shift_ref[EXTRA : 2 * EXTRA, :]


def last_kernel(x_ref, last_ref):
    length = x_ref.shape[1]
    last = x_ref[:, length - EDGE :].astype(f32).T
    last_ref[...] = last[EDGE - EXTRA :, :].astype(bf16)


def edge_kernel(edge_ref, first_ref, vec_ref, w_xbc_ref, coef_ref, state_ref, logs_ref,
                send_ref, act_ref, rows_ref):
    inner, state_width = state_ref.shape
    depth = edge_ref.shape[1]
    x = edge_ref[...].astype(f32)
    scale = lax.rsqrt(jnp.mean(x * x, axis=1, keepdims=True) + epsilon)
    normed = (x * scale * vec_ref[GAIN_IN : GAIN_IN + 1, :depth]).astype(bf16)
    before = jnp.dot(normed, w_xbc_ref[...], preferred_element_type=f32)
    rows_ref[0:EXTRA, :] = before.astype(bf16).astype(f32)
    rows_ref[EXTRA:, :] = first_ref[...]
    conv = vec_ref[BIAS : BIAS + 1, :]
    for tap in range(BIAS):
        at = EXTRA - (BIAS - 1 - tap)
        conv = conv + vec_ref[tap : tap + 1, :] * rows_ref[at : at + EXTRA, :]
    act = (conv * jax.nn.sigmoid(conv)).astype(bf16).astype(f32)
    act_ref[...] = act
    weighted = (act[:, :inner] * coef_ref[...]).astype(bf16).astype(f32)
    none = jnp.zeros_like(weighted)
    weighted = jnp.concatenate([weighted, none], axis=0).astype(bf16)
    b = act[:, inner : inner + state_width]
    b = jnp.concatenate([b, jnp.zeros_like(b)], axis=0).astype(bf16)
    size = inner // GROUP
    whole = state_ref[...] + contract(weighted, b, ((0,), (0,)))
    for part in range(GROUP):
        send_ref[part, 0:size, :] = whole[part * size : (part + 1) * size, :].astype(bf16)
        send_ref[part, size : size + EXTRA, :] = logs_ref[part * EXTRA : (part + 1) * EXTRA, :]


def pack_logs(total, rows_ref):
    heads = total.shape[0]
    own = rows_ref.shape[0] // EXTRA
    own = heads // own
    rows_ref[...] = jnp.zeros_like(rows_ref)
    rest = total
    for piece in range(3):
        part = rest.astype(bf16).astype(f32)
        rest = rest - part
        for head in range(heads):
            at = head // own * EXTRA + head % own * 3 + piece
            rows_ref[at : at + 1, :] = part[head : head + 1, :]


def read_logs(rows, own):
    rows = rows.astype(f32)
    return [
        rows[3 * h : 3 * h + 1, :] + rows[3 * h + 1 : 3 * h + 2, :] + rows[3 * h + 2 : 3 * h + 3, :]
        for h in range(own)
    ]


def prefix_kernel(own, states_ref, send_ref, rows_ref):
    size = send_ref.shape[0] - EXTRA
    head_dim = size // own
    width = send_ref.shape[1]
    logs = [read_logs(states_ref[m, size : size + EXTRA, :], own) for m in range(GROUP)]
    for h in range(own):
        rows = slice(h * head_dim, (h + 1) * head_dim)
        state = jnp.zeros((head_dim, width), f32)
        for m in range(GROUP):
            state = jnp.exp(logs[m][h]) * state + states_ref[m, rows, :].astype(f32)
        send_ref[rows, :] = state.astype(bf16)
    total = [sum(logs[m][h] for m in range(GROUP)) for h in range(own)]
    pack_logs(jnp.concatenate(total, axis=0), rows_ref)
    send_ref[size : size + EXTRA, :] = rows_ref[...].astype(bf16)


def join_kernel(own, total_ref, earlier_ref, send_ref, again_ref, same_ref):
    same_ref[...] = total_ref[...]
    size = send_ref.shape[0] - EXTRA
    head_dim = size // own
    jumps = read_logs(total_ref[size:, :], own)
    for h in range(own):
        rows = slice(h * head_dim, (h + 1) * head_dim)
        state = jnp.exp(jumps[h]) * earlier_ref[rows, :].astype(f32)
        send_ref[rows, :] = (total_ref[rows, :].astype(f32) + state).astype(bf16)
    send_ref[size:, :] = jnp.zeros((EXTRA, send_ref.shape[1]), bf16)
    again_ref[...] = send_ref[...]


def combine_kernel(own, states_ref, first_ref, after_b_ref, after_a_ref, near_ref, back_ref):
    size = back_ref.shape[1]
    head_dim = size // own
    logs = [read_logs(states_ref[m, size : size + EXTRA, :], own) for m in range(GROUP)]
    jumps = read_logs(near_ref[size:, :], own)
    for h in range(own):
        rows = slice(h * head_dim, (h + 1) * head_dim)
        after = after_a_ref[rows, :].astype(f32) + after_b_ref[rows, :].astype(f32)
        state = first_ref[rows, :].astype(f32) + near_ref[rows, :].astype(f32)
        state = state + jnp.exp(jumps[h]) * after
        for m in range(GROUP):
            back_ref[m, rows, :] = state.astype(bf16)
            state = jnp.exp(logs[m][h]) * state + states_ref[m, rows, :].astype(f32)


def inside_kernel(normed_ref, w_gate_ref, main_ref, first_ref, dt_ref, cs_ref,
                  grown_ref, y_ref, query_ref, act_ref, scores_ref, mix_ref, weight_ref, sem):
    fetches = fetch_rows(w_gate_ref, weight_ref, sem)
    heads, length = dt_ref.shape
    inner = y_ref.shape[0]
    lane = lax.broadcasted_iota(jnp.int32, (EDGE, EDGE), 1)
    rest = jnp.zeros((EDGE - EXTRA, EDGE), f32)
    for at in range(0, act_ref.shape[0], EDGE):
        rows = slice(at, at + EDGE)
        first = jnp.concatenate([first_ref[:, rows], rest], axis=0).T
        kept = main_ref[rows, 0:EDGE].astype(f32)
        act_ref[rows, 0:EDGE] = jnp.where(lane < EXTRA, first, kept).astype(bf16)
        act_ref[rows, EDGE:] = main_ref[rows, EDGE:]
    head_dim = inner // heads
    state_width = (act_ref.shape[0] - inner) // 2
    query_ref[...] = act_ref[inner + state_width :, :]
    scores_ref[...] = contract(
        act_ref[inner : inner + state_width, :], act_ref[inner + state_width :, :], ((0,), (0,))
    )
    cs_col = cs_ref[...].T
    dt_col = dt_ref[...].T
    half = length // 2
    mix_ref[...] = jnp.zeros_like(mix_ref)
    later = lax.broadcasted_iota(jnp.int32, (half, half), 1)
    early = lax.broadcasted_iota(jnp.int32, (half, half), 0)
    keep = later >= early
    for h in range(heads):
        for s in (0, half):
            cs_s = jnp.broadcast_to(cs_col[s : s + half, h : h + 1], (half, half))
            dt_s = jnp.broadcast_to(dt_col[s : s + half, h : h + 1], (half, half))
            for t in range(s, length, half):
                diff = cs_ref[h : h + 1, t : t + half] - cs_s
                if s == t:
                    diff = jnp.where(keep, diff, -jnp.inf)
                mix_ref[s : s + half, t : t + half] = (
                    scores_ref[s : s + half, t : t + half] * jnp.exp(diff) * dt_s
                ).astype(bf16)
        rows = slice(h * head_dim, (h + 1) * head_dim)
        y_ref[rows, :] = jnp.dot(act_ref[rows, :], mix_ref[...], preferred_element_type=f32)
    for fetch in fetches:
        fetch.wait()
    normed = normed_ref[...]
    step = 4 * head_dim
    for at in range(0, inner, step):
        gate = contract(weight_ref[:, at : at + step], normed, ((0,), (0,)))
        gate = gate.astype(bf16).astype(f32)
        gate = gate * jax.nn.sigmoid(gate)
        for h in range(at // head_dim, (at + step) // head_dim):
            rows = slice(h * head_dim, (h + 1) * head_dim)
            own = gate[h * head_dim - at : (h + 1) * head_dim - at, :]
            grown_ref[rows, :] = (jnp.exp(cs_ref[h : h + 1, :]) * own).astype(bf16)
            y_ref[rows, :] = y_ref[rows, :] * own


def output_kernel(carried_ref, query_ref, grown_ref, y_ref, vec_ref, w_out_ref,
                  out_ref, gated_ref, normed_ref):
    inner, length = y_ref.shape
    gated_ref[...] = jnp.dot(carried_ref[...], query_ref[...], preferred_element_type=f32)
    total = jnp.zeros((1, length), f32)
    for at in range(0, inner, EDGE):
        rows = slice(at, at + EDGE)
        gated = y_ref[rows, :] + grown_ref[rows, :].astype(f32) * gated_ref[rows, :]
        gated_ref[rows, :] = gated
        total = total + jnp.sum(gated * gated, axis=0, keepdims=True)
    scale = lax.rsqrt(total / inner + epsilon)
    for at in range(0, inner, EDGE):
        gain = columns_of(vec_ref, at)[:, GAIN_OUT : GAIN_OUT + 1]
        normed_ref[at : at + EDGE, :] = (gated_ref[at : at + EDGE, :] * scale * gain).astype(bf16)
    out_ref[...] = contract(normed_ref[...], w_out_ref[...], ((0,), (0,))).astype(bf16)


def call(kernel, outs, scratch, *args, fetched=()):
    vmem = pl.BlockSpec(memory_space=pltpu.VMEM)
    left = pl.BlockSpec(memory_space=pltpu.HBM)
    single = not isinstance(outs, list)
    args = [
        pltpu.with_memory_space_constraint(a, pltpu.HBM) if at in fetched else a
        for at, a in enumerate(args)
    ]
    return pl.pallas_call(
        kernel,
        out_shape=outs,
        in_specs=[left if at in fetched else vmem for at in range(len(args))],
        out_specs=vmem if single else [vmem] * len(outs),
        scratch_shapes=scratch,
        compiler_params=pltpu.CompilerParams(vmem_limit_bytes=12 << 20),
    )(*args)


def local(
    columns,
    gaps,
    norm_in,
    w_gate,
    w_xbc,
    w_step,
    step_bias,
    conv_weight,
    conv_bias,
    rates,
    norm_out,
    w_out,
):
    length = columns.shape[1]
    depth, inner = w_gate.shape
    heads = w_step.shape[1]
    width = w_xbc.shape[1]
    state_width = (width - inner) // 2
    own = heads // GROUP
    size = inner // GROUP
    shape = jax.ShapeDtypeStruct

    rows = [conv_weight, conv_bias[None], norm_in[None], norm_out[None]]
    vec = jnp.concatenate([jnp.pad(r, ((0, 0), (0, width - r.shape[1]))) for r in rows])
    vec = jnp.pad(vec, ((0, 8 - vec.shape[0]), (0, 0)))
    head = jnp.stack([step_bias, rates], axis=1)

    whole = lax.all_to_all(columns, "table", split_axis=0, concat_axis=2, tiled=True)
    staged = [w_xbc, w_step.T, gaps]
    staged = call(
        stage_kernel,
        [shape(a.shape, a.dtype) for a in staged],
        [pltpu.SemaphoreType.DMA((len(staged),))],
        *staged,
        fetched=range(len(staged)),
    )
    whole, vec, head, *staged = lax.optimization_barrier((whole, vec, head, *staged))
    w_xbc, w_step_t, gaps = staged
    x = whole.reshape(length, depth).T
    edge = passed_along(call(last_kernel, shape((EXTRA, depth), bf16), [], x), "seq", 1)
    normed, act, dt, cs, state, logs, first, coef_first = call(
        main_kernel,
        [
            shape((depth, length), bf16),
            shape((width, length), bf16),
            shape((heads, length), f32),
            shape((heads, length), f32),
            shape((inner, state_width), f32),
            shape((GROUP * EXTRA, state_width), bf16),
            shape((EXTRA, width), f32),
            shape((EXTRA, inner), f32),
        ],
        [
            pltpu.VMEM((heads, length), f32),
            pltpu.VMEM((GROUP * EXTRA, state_width), f32),
            pltpu.VMEM((length, depth), bf16),
            pltpu.VMEM((EXTRA + length, width), f32),
            pltpu.VMEM((inner, length), bf16),
        ],
        x, vec, w_xbc, w_step_t, head, gaps,
    )
    send, act_first = call(
        edge_kernel,
        [shape((GROUP, size + EXTRA, state_width), bf16), shape((EXTRA, width), f32)],
        [pltpu.VMEM((2 * EXTRA, width), f32)],
        edge, first, vec, w_xbc, coef_first, state, logs,
    )
    states = within_groups(send)
    total = call(
        functools.partial(prefix_kernel, own),
        shape((size + EXTRA, state_width), bf16),
        [pltpu.VMEM((EXTRA, state_width), f32)],
        states,
    )
    assert lax.axis_size("seq") == 4 * GROUP
    first = passed_along(total, "seq", GROUP, members(0))
    joined, again, same = call(
        functools.partial(join_kernel, own),
        [shape((size + EXTRA, state_width), bf16)] * 3,
        [],
        total, first,
    )
    after_b = passed_along(joined, "seq", 2 * GROUP, members(1))
    after_a = passed_along(again, "seq", GROUP, members(1))
    near = passed_along(same, "seq", GROUP, members(2))
    back = call(
        functools.partial(combine_kernel, own),
        shape((GROUP, size, state_width), bf16),
        [],
        states, first, after_b, after_a, near,
    )
    back, act = lax.optimization_barrier((back, act))
    carried = within_groups(back).reshape(inner, state_width)
    grown, y, query = call(
        inside_kernel,
        [
            shape((inner, length), bf16),
            shape((inner, length), f32),
            shape((state_width, length), bf16),
        ],
        [
            pltpu.VMEM((width, length), bf16),
            pltpu.VMEM((length, length), f32),
            pltpu.VMEM((length, length), bf16),
            pltpu.VMEM((depth, inner), bf16),
            pltpu.SemaphoreType.DMA((PARTS,)),
        ],
        normed, w_gate, act, act_first, dt, cs,
        fetched=(1,),
    )
    grown, y, query, w_out = lax.optimization_barrier((grown, y, query, w_out))
    (w_out,) = call(
        stage_kernel,
        [shape(w_out.shape, w_out.dtype)],
        [pltpu.SemaphoreType.DMA((1,))],
        w_out,
        fetched=(0,),
    )
    out = call(
        output_kernel,
        shape((length, w_out.shape[1]), bf16),
        [
            pltpu.VMEM((inner, length), f32),
            pltpu.VMEM((inner, length), bf16),
        ],
        carried, query, grown, y, vec, w_out,
    )
    return out[None]


def solution(mesh):
    in_specs = (
        P(None, "seq", "table"),
        P("table", "seq"),
        P(),
        P(),
        P(),
        P(),
        P(),
        P(),
        P(),
        P(),
        P(),
        P(),
    )
    out_specs = P("table", "seq", None)
    return jax.shard_map(local, mesh=mesh, in_specs=in_specs, out_specs=out_specs, check_vma=False)
```

```python
import functools

import jax
import jax.numpy as jnp
from jax import lax
from jax.experimental import pallas as pl
from jax.experimental.pallas import tpu as pltpu
from jax.sharding import PartitionSpec as P

GROUP = 8
EDGE = 128
EXTRA = 8
PARTS = 4
BIAS, GAIN_IN, GAIN_OUT = 4, 5, 6
epsilon = 1e-05
f32 = jnp.float32
bf16 = jnp.bfloat16


def passed_along(block, axis, distance, senders=None):
    devices = range(lax.axis_size(axis))
    route = [(i, i + distance) for i in senders or devices if i + distance in devices]
    return lax.ppermute(block, axis, route)


def members(*groups):
    return [g * GROUP + i for g in groups for i in range(GROUP)]


def within_groups(blocks):
    count = lax.axis_size("seq") // GROUP
    groups = [[g * GROUP + i for i in range(GROUP)] for g in range(count)]
    return lax.all_to_all(
        blocks, "seq", split_axis=0, concat_axis=0, tiled=True, axis_index_groups=groups
    )


def fetch_rows(source, target, sems):
    count = sems.shape[0]
    step = source.shape[0] // count
    copies = [
        pltpu.make_async_copy(
            source.at[at * step : (at + 1) * step], target.at[at * step : (at + 1) * step], sems.at[at]
        )
        for at in range(count)
    ]
    for copy in copies:
        copy.start()
    return copies


def contract(a, b, dims):
    return lax.dot_general(a, b, (dims, ((), ())), preferred_element_type=f32)


def columns_of(vec_ref, at):
    return vec_ref[:, at : at + EDGE].T


def normed_columns(x_ref, vec_ref, out_ref):
    depth, length = x_ref.shape
    total = jnp.zeros((1, length), f32)
    for at in range(0, depth, 64):
        x = x_ref[at : at + 64, :].astype(f32)
        total = total + jnp.sum(x * x, axis=0, keepdims=True)
    scale = lax.rsqrt(total / depth + epsilon)
    for at in range(0, depth, EDGE):
        gain = columns_of(vec_ref, at)[:, GAIN_IN : GAIN_IN + 1]
        x = x_ref[at : at + EDGE, :].astype(f32)
        out_ref[at : at + EDGE, :] = (x * scale * gain).astype(bf16)


def running_sum(values):
    length = values.shape[1]
    lane = lax.broadcasted_iota(jnp.int32, values.shape, 1)
    reach = 1
    while reach < length:
        values = values + jnp.where(lane >= reach, pltpu.roll(values, reach, axis=1), 0.0)
        reach *= 2
    return values


def stage_kernel(*refs):
    count = len(refs) // 2
    sems = refs[-1]
    copies = [
        pltpu.make_async_copy(refs[at], refs[count + at], sems.at[at]) for at in range(count)
    ]
    for copy in copies:
        copy.start()
    for copy in copies:
        copy.wait()


def main_kernel(x_ref, vec_ref, w_xbc_ref, w_step_ref, head_ref, gaps_ref,
                normed_ref, act_ref, dt_ref, cs_ref, state_ref, logs_ref, first_ref, coef_first_ref,
                coef_ref, rows_ref, upright_ref, shift_ref, weighted_ref):
    depth, length = x_ref.shape
    heads = dt_ref.shape[0]
    inner, state_width = state_ref.shape
    head_dim = inner // heads
    normed_columns(x_ref, vec_ref, normed_ref)
    normed = normed_ref[...]
    raw = jnp.dot(w_step_ref[...], normed, preferred_element_type=f32)
    raw = raw + head_ref[:, 0:1]
    dt = jnp.maximum(raw, 0.0) + jnp.log1p(jnp.exp(-jnp.abs(raw)))
    dt_ref[...] = dt
    cs = running_sum(-head_ref[:, 1:2] * dt * gaps_ref[...])
    cs_ref[...] = cs
    coef = jnp.exp(cs[:, length - 1 : length] - cs) * dt
    coef_first = coef[:, 0:EDGE].T[0:EXTRA, :]
    for head in range(heads):
        coef_first_ref[:, head * head_dim : (head + 1) * head_dim] = jnp.broadcast_to(
            coef_first[:, head : head + 1], (EXTRA, head_dim)
        )
    lane = lax.broadcasted_iota(jnp.int32, coef.shape, 1)
    coef_ref[...] = jnp.where(lane >= EXTRA, coef, 0.0)
    total = jnp.broadcast_to(cs[:, length - 1 : length], (heads, state_width))
    pack_logs(total, rows_ref)
    logs_ref[...] = rows_ref[...].astype(bf16)

    for at in range(0, depth, EDGE):
        upright_ref[:, at : at + EDGE] = normed_ref[at : at + EDGE, :].astype(f32).T.astype(bf16)
    shift_ref[0:EXTRA, :] = jnp.zeros((EXTRA, shift_ref.shape[1]), f32)
    upright = upright_ref[...]

    def act_of(at, step):
        cols = slice(at, at + step)
        whole = jnp.dot(upright, w_xbc_ref[:, cols], preferred_element_type=f32)
        shift_ref[EXTRA:, cols] = whole.astype(bf16).astype(f32)
        conv = vec_ref[BIAS : BIAS + 1, cols]
        for tap in range(BIAS):
            first = EXTRA - (BIAS - 1 - tap)
            conv = conv + vec_ref[tap : tap + 1, cols] * shift_ref[first : first + length, cols]
        act = conv * jax.nn.sigmoid(conv)
        turned = act.T.astype(bf16)
        act_ref[at : at + step, :] = turned
        return act.astype(bf16), turned

    b, _ = act_of(inner, state_width)
    act_of(inner + state_width, state_width)
    step = 4 * head_dim
    for at in range(0, inner, step):
        act = act_of(at, step)[1].astype(f32)
        head = at // head_dim
        coef = jnp.concatenate(
            [jnp.broadcast_to(coef_ref[h : h + 1, :], (head_dim, length)) for h in range(head, head + 4)],
            axis=0,
        )
        weighted_ref[at : at + step, :] = (act * coef).astype(bf16)
    state_ref[...] = jnp.dot(weighted_ref[...], b, preferred_element_type=f32)
    first_ref[...] = shift_ref[EXTRA : 2 * EXTRA, :]


def last_kernel(x_ref, last_ref):
    length = x_ref.shape[1]
    last = x_ref[:, length - EDGE :].astype(f32).T
    last_ref[...] = last[EDGE - EXTRA :, :].astype(bf16)


def edge_kernel(edge_ref, first_ref, vec_ref, w_xbc_ref, coef_ref, state_ref, logs_ref,
                send_ref, act_ref, rows_ref):
    inner, state_width = state_ref.shape
    depth = edge_ref.shape[1]
    x = edge_ref[...].astype(f32)
    scale = lax.rsqrt(jnp.mean(x * x, axis=1, keepdims=True) + epsilon)
    normed = (x * scale * vec_ref[GAIN_IN : GAIN_IN + 1, :depth]).astype(bf16)
    before = jnp.dot(normed, w_xbc_ref[...], preferred_element_type=f32)
    rows_ref[0:EXTRA, :] = before.astype(bf16).astype(f32)
    rows_ref[EXTRA:, :] = first_ref[...]
    conv = vec_ref[BIAS : BIAS + 1, :]
    for tap in range(BIAS):
        at = EXTRA - (BIAS - 1 - tap)
        conv = conv + vec_ref[tap : tap + 1, :] * rows_ref[at : at + EXTRA, :]
    act = (conv * jax.nn.sigmoid(conv)).astype(bf16).astype(f32)
    act_ref[...] = act
    weighted = (act[:, :inner] * coef_ref[...]).astype(bf16).astype(f32)
    none = jnp.zeros_like(weighted)
    weighted = jnp.concatenate([weighted, none], axis=0).astype(bf16)
    b = act[:, inner : inner + state_width]
    b = jnp.concatenate([b, jnp.zeros_like(b)], axis=0).astype(bf16)
    size = inner // GROUP
    whole = state_ref[...] + contract(weighted, b, ((0,), (0,)))
    for part in range(GROUP):
        send_ref[part, 0:size, :] = whole[part * size : (part + 1) * size, :].astype(bf16)
        send_ref[part, size : size + EXTRA, :] = logs_ref[part * EXTRA : (part + 1) * EXTRA, :]


def pack_logs(total, rows_ref):
    heads = total.shape[0]
    own = rows_ref.shape[0] // EXTRA
    own = heads // own
    rows_ref[...] = jnp.zeros_like(rows_ref)
    rest = total
    for piece in range(3):
        part = rest.astype(bf16).astype(f32)
        rest = rest - part
        for head in range(heads):
            at = head // own * EXTRA + head % own * 3 + piece
            rows_ref[at : at + 1, :] = part[head : head + 1, :]


def read_logs(rows, own):
    rows = rows.astype(f32)
    return [
        rows[3 * h : 3 * h + 1, :] + rows[3 * h + 1 : 3 * h + 2, :] + rows[3 * h + 2 : 3 * h + 3, :]
        for h in range(own)
    ]


def prefix_kernel(own, states_ref, send_ref, rows_ref):
    size = send_ref.shape[0] - EXTRA
    head_dim = size // own
    width = send_ref.shape[1]
    logs = [read_logs(states_ref[m, size : size + EXTRA, :], own) for m in range(GROUP)]
    for h in range(own):
        rows = slice(h * head_dim, (h + 1) * head_dim)
        state = jnp.zeros((head_dim, width), f32)
        for m in range(GROUP):
            state = jnp.exp(logs[m][h]) * state + states_ref[m, rows, :].astype(f32)
        send_ref[rows, :] = state.astype(bf16)
    total = [sum(logs[m][h] for m in range(GROUP)) for h in range(own)]
    pack_logs(jnp.concatenate(total, axis=0), rows_ref)
    send_ref[size : size + EXTRA, :] = rows_ref[...].astype(bf16)


def join_kernel(own, total_ref, earlier_ref, send_ref, again_ref, same_ref):
    same_ref[...] = total_ref[...]
    size = send_ref.shape[0] - EXTRA
    head_dim = size // own
    jumps = read_logs(total_ref[size:, :], own)
    for h in range(own):
        rows = slice(h * head_dim, (h + 1) * head_dim)
        state = jnp.exp(jumps[h]) * earlier_ref[rows, :].astype(f32)
        send_ref[rows, :] = (total_ref[rows, :].astype(f32) + state).astype(bf16)
    send_ref[size:, :] = jnp.zeros((EXTRA, send_ref.shape[1]), bf16)
    again_ref[...] = send_ref[...]


def combine_kernel(own, states_ref, first_ref, after_b_ref, after_a_ref, near_ref, back_ref):
    size = back_ref.shape[1]
    head_dim = size // own
    logs = [read_logs(states_ref[m, size : size + EXTRA, :], own) for m in range(GROUP)]
    jumps = read_logs(near_ref[size:, :], own)
    for h in range(own):
        rows = slice(h * head_dim, (h + 1) * head_dim)
        after = after_a_ref[rows, :].astype(f32) + after_b_ref[rows, :].astype(f32)
        state = first_ref[rows, :].astype(f32) + near_ref[rows, :].astype(f32)
        state = state + jnp.exp(jumps[h]) * after
        for m in range(GROUP):
            back_ref[m, rows, :] = state.astype(bf16)
            state = jnp.exp(logs[m][h]) * state + states_ref[m, rows, :].astype(f32)


def inside_kernel(normed_ref, w_gate_ref, main_ref, first_ref, dt_ref, cs_ref,
                  grown_ref, y_ref, query_ref, act_ref, scores_ref, mix_ref, weight_ref, sem):
    fetches = fetch_rows(w_gate_ref, weight_ref, sem)
    heads, length = dt_ref.shape
    inner = y_ref.shape[0]
    lane = lax.broadcasted_iota(jnp.int32, (EDGE, EDGE), 1)
    rest = jnp.zeros((EDGE - EXTRA, EDGE), f32)
    for at in range(0, act_ref.shape[0], EDGE):
        rows = slice(at, at + EDGE)
        first = jnp.concatenate([first_ref[:, rows], rest], axis=0).T
        kept = main_ref[rows, 0:EDGE].astype(f32)
        act_ref[rows, 0:EDGE] = jnp.where(lane < EXTRA, first, kept).astype(bf16)
        act_ref[rows, EDGE:] = main_ref[rows, EDGE:]
    head_dim = inner // heads
    state_width = (act_ref.shape[0] - inner) // 2
    query_ref[...] = act_ref[inner + state_width :, :]
    scores_ref[...] = contract(
        act_ref[inner : inner + state_width, :], act_ref[inner + state_width :, :], ((0,), (0,))
    )
    cs_col = cs_ref[...].T
    dt_col = dt_ref[...].T
    half = length // 2
    mix_ref[...] = jnp.zeros_like(mix_ref)
    later = lax.broadcasted_iota(jnp.int32, (half, half), 1)
    early = lax.broadcasted_iota(jnp.int32, (half, half), 0)
    keep = later >= early
    for h in range(heads):
        for s in (0, half):
            cs_s = jnp.broadcast_to(cs_col[s : s + half, h : h + 1], (half, half))
            dt_s = jnp.broadcast_to(dt_col[s : s + half, h : h + 1], (half, half))
            for t in range(s, length, half):
                diff = cs_ref[h : h + 1, t : t + half] - cs_s
                if s == t:
                    diff = jnp.where(keep, diff, -jnp.inf)
                mix_ref[s : s + half, t : t + half] = (
                    scores_ref[s : s + half, t : t + half] * jnp.exp(diff) * dt_s
                ).astype(bf16)
        rows = slice(h * head_dim, (h + 1) * head_dim)
        y_ref[rows, :] = jnp.dot(act_ref[rows, :], mix_ref[...], preferred_element_type=f32)
    for fetch in fetches:
        fetch.wait()
    normed = normed_ref[...]
    step = 4 * head_dim
    for at in range(0, inner, step):
        gate = contract(weight_ref[:, at : at + step], normed, ((0,), (0,)))
        gate = gate.astype(bf16).astype(f32)
        gate = gate * jax.nn.sigmoid(gate)
        for h in range(at // head_dim, (at + step) // head_dim):
            rows = slice(h * head_dim, (h + 1) * head_dim)
            own = gate[h * head_dim - at : (h + 1) * head_dim - at, :]
            grown_ref[rows, :] = (jnp.exp(cs_ref[h : h + 1, :]) * own).astype(bf16)
            y_ref[rows, :] = y_ref[rows, :] * own


def output_kernel(carried_ref, query_ref, grown_ref, y_ref, vec_ref, w_out_ref,
                  out_ref, gated_ref, normed_ref):
    inner, length = y_ref.shape
    gated_ref[...] = jnp.dot(carried_ref[...], query_ref[...], preferred_element_type=f32)
    total = jnp.zeros((1, length), f32)
    for at in range(0, inner, EDGE):
        rows = slice(at, at + EDGE)
        gated = y_ref[rows, :] + grown_ref[rows, :].astype(f32) * gated_ref[rows, :]
        gated_ref[rows, :] = gated
        total = total + jnp.sum(gated * gated, axis=0, keepdims=True)
    scale = lax.rsqrt(total / inner + epsilon)
    for at in range(0, inner, EDGE):
        gain = columns_of(vec_ref, at)[:, GAIN_OUT : GAIN_OUT + 1]
        normed_ref[at : at + EDGE, :] = (gated_ref[at : at + EDGE, :] * scale * gain).astype(bf16)
    out_ref[...] = contract(normed_ref[...], w_out_ref[...], ((0,), (0,))).astype(bf16)


def call(kernel, outs, scratch, *args, fetched=()):
    vmem = pl.BlockSpec(memory_space=pltpu.VMEM)
    left = pl.BlockSpec(memory_space=pltpu.HBM)
    single = not isinstance(outs, list)
    args = [
        pltpu.with_memory_space_constraint(a, pltpu.HBM) if at in fetched else a
        for at, a in enumerate(args)
    ]
    return pl.pallas_call(
        kernel,
        out_shape=outs,
        in_specs=[left if at in fetched else vmem for at in range(len(args))],
        out_specs=vmem if single else [vmem] * len(outs),
        scratch_shapes=scratch,
        compiler_params=pltpu.CompilerParams(vmem_limit_bytes=12 << 20),
    )(*args)


def local(
    columns,
    gaps,
    norm_in,
    w_gate,
    w_xbc,
    w_step,
    step_bias,
    conv_weight,
    conv_bias,
    rates,
    norm_out,
    w_out,
):
    length = columns.shape[1]
    depth, inner = w_gate.shape
    heads = w_step.shape[1]
    width = w_xbc.shape[1]
    state_width = (width - inner) // 2
    own = heads // GROUP
    size = inner // GROUP
    shape = jax.ShapeDtypeStruct

    rows = [conv_weight, conv_bias[None], norm_in[None], norm_out[None]]
    vec = jnp.concatenate([jnp.pad(r, ((0, 0), (0, width - r.shape[1]))) for r in rows])
    vec = jnp.pad(vec, ((0, 8 - vec.shape[0]), (0, 0)))
    head = jnp.stack([step_bias, rates], axis=1)

    whole = lax.all_to_all(columns, "table", split_axis=0, concat_axis=2, tiled=True)
    staged = [w_xbc, w_step.T, gaps]
    staged = call(
        stage_kernel,
        [shape(a.shape, a.dtype) for a in staged],
        [pltpu.SemaphoreType.DMA((len(staged),))],
        *staged,
        fetched=range(len(staged)),
    )
    whole, vec, head, *staged = lax.optimization_barrier((whole, vec, head, *staged))
    w_xbc, w_step_t, gaps = staged
    x = whole.reshape(length, depth).T
    edge = passed_along(call(last_kernel, shape((EXTRA, depth), bf16), [], x), "seq", 1)
    normed, act, dt, cs, state, logs, first, coef_first = call(
        main_kernel,
        [
            shape((depth, length), bf16),
            shape((width, length), bf16),
            shape((heads, length), f32),
            shape((heads, length), f32),
            shape((inner, state_width), f32),
            shape((GROUP * EXTRA, state_width), bf16),
            shape((EXTRA, width), f32),
            shape((EXTRA, inner), f32),
        ],
        [
            pltpu.VMEM((heads, length), f32),
            pltpu.VMEM((GROUP * EXTRA, state_width), f32),
            pltpu.VMEM((length, depth), bf16),
            pltpu.VMEM((EXTRA + length, width), f32),
            pltpu.VMEM((inner, length), bf16),
        ],
        x, vec, w_xbc, w_step_t, head, gaps,
    )
    send, act_first = call(
        edge_kernel,
        [shape((GROUP, size + EXTRA, state_width), bf16), shape((EXTRA, width), f32)],
        [pltpu.VMEM((2 * EXTRA, width), f32)],
        edge, first, vec, w_xbc, coef_first, state, logs,
    )
    states = within_groups(send)
    total = call(
        functools.partial(prefix_kernel, own),
        shape((size + EXTRA, state_width), bf16),
        [pltpu.VMEM((EXTRA, state_width), f32)],
        states,
    )
    assert lax.axis_size("seq") == 4 * GROUP
    first = passed_along(total, "seq", GROUP, members(0))
    joined, again, same = call(
        functools.partial(join_kernel, own),
        [shape((size + EXTRA, state_width), bf16)] * 3,
        [],
        total, first,
    )
    after_b = passed_along(joined, "seq", 2 * GROUP, members(1))
    after_a = passed_along(again, "seq", GROUP, members(1))
    near = passed_along(same, "seq", GROUP, members(2))
    back = call(
        functools.partial(combine_kernel, own),
        shape((GROUP, size, state_width), bf16),
        [],
        states, first, after_b, after_a, near,
    )
    back, act = lax.optimization_barrier((back, act))
    carried = within_groups(back).reshape(inner, state_width)
    grown, y, query = call(
        inside_kernel,
        [
            shape((inner, length), bf16),
            shape((inner, length), f32),
            shape((state_width, length), bf16),
        ],
        [
            pltpu.VMEM((width, length), bf16),
            pltpu.VMEM((length, length), f32),
            pltpu.VMEM((length, length), bf16),
            pltpu.VMEM((depth, inner), bf16),
            pltpu.SemaphoreType.DMA((PARTS,)),
        ],
        normed, w_gate, act, act_first, dt, cs,
        fetched=(1,),
    )
    grown, y, query, w_out = lax.optimization_barrier((grown, y, query, w_out))
    (w_out,) = call(
        stage_kernel,
        [shape(w_out.shape, w_out.dtype)],
        [pltpu.SemaphoreType.DMA((1,))],
        w_out,
        fetched=(0,),
    )
    out = call(
        output_kernel,
        shape((length, w_out.shape[1]), bf16),
        [
            pltpu.VMEM((inner, length), f32),
            pltpu.VMEM((inner, length), bf16),
        ],
        carried, query, grown, y, vec, w_out,
    )
    return out[None]


def solution(mesh):
    in_specs = (
        P(None, "seq", "table"),
        P("table", "seq"),
        P(),
        P(),
        P(),
        P(),
        P(),
        P(),
        P(),
        P(),
        P(),
        P(),
    )
    out_specs = P("table", "seq", None)
    return jax.shard_map(local, mesh=mesh, in_specs=in_specs, out_specs=out_specs, check_vma=False)
```
